512 devices in a mesh: ev: 8 (over y_hi, x), sp: 64 (over z, y_lo, core).
Axes of the slice: x: 4, y: 4 (y_hi: 2, y_lo: 2; y = y_hi * 2 + y_lo), z: 16, core: 2. Of those that a mesh axis runs over, the one named last changes fastest.
Arguments:
- partial_kernels: float32 [8, 32, 512, 128], P('ev', None, 'sp'), may hold values from -6 to 6
- block_ids: int32 [8, 512], P('ev', 'sp'), may hold values from 0 to 255, as said below
- radial_smoother: float32 [128, 128], replicated, may hold values from -0.5 to 2
- shell_level: int32 [128], P('sp'), may hold values from 1 to 4
- lateral_scale: float32 [512, 1024], replicated, may hold values from 0.5 to 1
Outputs:
- smoothed_kernel: float32 [128, 512, 1024], P('sp', None, 'ev')
The draws below stay inside these ranges and needn't reach their ends.
Inputs may be any that keep to these rules, and one draw needn't show every extreme that they name: `block_ids`: each index of ev and sp holds 8 distinct ids; an id's owner is id // 32; one holder gives at most 2 ids to one owner, and in every stripe some owner receives 2 ids from every group.
All inputs are finite; a program needn't handle non-finite values.
Results may differ from the reference program's by a relative error of at most 0.000073.
Values sent between devices are 32-bit elements; how exact they have to be, the bound alone decides.
No kernel may reach another device: no remote copies, remote signals or barrier semaphores. Data moves between devices by JAX's collectives and lax.ppermute only.
A program may use at most 64 MiB of HBM per device.

```python
import jax
import jax.numpy as jnp
from jax import lax

NR = 128
RB = 32
BY = 128
BPT = 8
PASSES = 4
LIST = 8
NSEG = 4
LX = 512
LY = 1024
N_EV = 8
N_SP = 64


def draw_block_ids(key, part):
    subkeys = jax.random.split(key, 6)
    per_owner = BPT * NSEG
    favored = jax.random.randint(subkeys[0], (1, N_SP, 1), 0, N_EV)
    scores = jax.random.randint(subkeys[1], (N_EV, N_SP, N_EV - 1), 0, 1 << 20) * N_EV + jnp.arange(N_EV - 1)
    others = jnp.argsort(scores, axis=-1).astype(jnp.int32) + 1
    owner_order = (favored + jnp.concatenate([jnp.zeros((N_EV, N_SP, 1), jnp.int32), others], axis=-1)) % N_EV
    leading = owner_order[..., 0::2]
    trailing = owner_order[..., 1::2]
    doubled = jax.random.randint(subkeys[2], (N_EV, N_SP, N_EV // 2), 0, 2)
    doubled = doubled.at[..., 0].set(1)
    partner = jnp.where(doubled == 1, leading, trailing)
    spot_first = jax.random.randint(subkeys[3], (N_EV, N_SP, N_EV // 2), 0, per_owner)
    spot_second = (spot_first + 1 + jax.random.randint(subkeys[4], (N_EV, N_SP, N_EV // 2), 0, per_owner - 1)) % per_owner
    entry_owner = jnp.stack([leading, partner], axis=-1).reshape(N_EV, N_SP, N_EV)
    entry_spot = jnp.stack([spot_first, spot_second], axis=-1).reshape(N_EV, N_SP, N_EV)
    block_list = entry_owner * per_owner + entry_spot
    shuffle_scores = jax.random.randint(subkeys[5], (N_EV, N_SP, N_EV), 0, 1 << 20) * N_EV + jnp.arange(N_EV)
    shuffled_order = jnp.argsort(shuffle_scores, axis=-1)
    block_list = jnp.take_along_axis(block_list, shuffled_order, axis=-1)
    return block_list.reshape(N_EV, N_SP * N_EV).astype(jnp.int32)


def draw_radial_smoother(key, part):
    key_diag, key_off = jax.random.split(key)
    row_index = jnp.arange(NR)[:, None]
    col_index = jnp.arange(NR)[None, :]
    distance = jnp.abs(row_index - col_index).astype(jnp.float32)
    offdiag = jax.random.uniform(key_off, (NR, NR), jnp.float32, minval=-1.0, maxval=1.0)
    diag_part = jax.random.uniform(key_diag, (NR,), jnp.float32, minval=0.8, maxval=1.4)
    matrix = 0.15 * jnp.exp(-distance / 6.0) * offdiag + jnp.where(distance == 0.0, diag_part[:, None], 0.0)
    return matrix.astype(jnp.float32)


def place_ends(array, own_key, low, largest):
    spot = [jax.random.randint(jax.random.fold_in(own_key, axis), (), 0, length) for axis, length in enumerate(array.shape)]
    main_axis = array.shape.index(max(array.shape))
    beside = spot[:main_axis] + [(spot[main_axis] + 1) % array.shape[main_axis]] + spot[main_axis + 1:]
    return array.at[tuple(spot)].set(low).at[tuple(beside)].set(largest)


def levels(stream_key, shape, cuts, smallest, largest):
    def one(axis_at, parts):
        draws = jax.random.uniform(jax.random.fold_in(jax.random.fold_in(stream_key, 6), axis_at), (parts,), jnp.float32, smallest / len(cuts), largest / len(cuts))
        return jnp.repeat(jnp.exp(draws), shape[axis_at] // parts).reshape((-1,) + (1,) * (len(shape) - axis_at - 1))

    gain = one(*cuts[0])
    for cut in cuts[1:]:
        gain = gain * one(*cut)
    return gain


def centred(own_key, extent, width, limit, cuts=(), kind=jnp.bfloat16):
    entries = jax.random.normal(own_key, extent, jnp.float32) * width
    if len(cuts) > 0:
        entries = levels(own_key, extent, cuts, -0.22, 0.18) * entries
    return jnp.clip(entries, min=-limit, max=limit).astype(kind)


def setup_inputs(seed: int = 0) -> dict:
    key_list = jax.random.split(jax.random.key(seed), 6)
    return {
        "partial_kernels": centred(key_list[0], (N_EV, RB, N_SP * LIST, BY), 1.0, 6.0, ((0, 8), (2, 64)), jnp.float32),
        "block_ids": draw_block_ids(jax.random.fold_in(key_list[5], 71), 0),
        "radial_smoother": draw_radial_smoother(jax.random.fold_in(key_list[5], 71), 0),
        "shell_level": place_ends(jax.random.randint(key_list[3], (NR,), 1, 5), jax.random.fold_in(key_list[3], 1), 1, 4).astype(jnp.int32),
        "lateral_scale": jnp.clip(jax.random.uniform(key_list[4], (LX, LY), jnp.float32, 0.5, 1.0), 0.5, 1.0),
    }


diffusion_rate = 0.0615


def reference(partial_kernels, block_ids, radial_smoother, shell_level, lateral_scale):
    per_owner = BPT * NSEG
    stripe = (jnp.arange(N_SP * LIST, dtype=jnp.int32) // LIST)[None, :]
    owners = block_ids // per_owner
    within = block_ids % per_owner
    row_in = within // NSEG
    seg_of = within % NSEG
    x_place = (stripe * BPT + row_in).reshape(-1).astype(jnp.int32)
    y_place = owners.reshape(-1).astype(jnp.int32)
    seg_place = seg_of.reshape(-1).astype(jnp.int32)
    blocks = jnp.transpose(partial_kernels, (0, 2, 1, 3)).reshape(N_EV * N_SP * LIST, RB, BY)
    grid_sum = jnp.zeros((NSEG, LX, N_EV, RB, BY), jnp.float32)
    grid_sum = grid_sum.at[seg_place, x_place, y_place].add(blocks)
    kernel = jnp.transpose(grid_sum, (0, 3, 1, 2, 4)).reshape(NR, LX * LY)
    smoothed = jnp.dot(radial_smoother, kernel, precision=lax.Precision.HIGHEST).reshape(NR, LX, LY)
    coefficient = diffusion_rate * shell_level.astype(jnp.float32)[:, None, None] * lateral_scale[None]
    kernel_field = smoothed
    for repeat in range(PASSES):
        padded = jnp.pad(kernel_field, ((0, 0), (1, 1), (1, 1)))
        beside = padded[:, 2:, 1:-1] + padded[:, :-2, 1:-1] + padded[:, 1:-1, 2:] + padded[:, 1:-1, :-2]
        kernel_field = kernel_field + coefficient * (beside - 4.0 * kernel_field)
    return kernel_field
```

```python
import functools

import jax
import jax.numpy as jnp
from jax import lax
from jax.experimental import pallas as pl
from jax.experimental.pallas import tpu as pltpu
from jax.sharding import PartitionSpec as P

NR = 128
RB = 32
BY = 128
BPT = 8
CAP = 2
PASSES = 4
NSEG = 4
PER_OWNER = BPT * NSEG
LANES = 128
TILE = 8
MESSAGE = CAP * RB + TILE
LABELS = 64
PIECE = 2 * BPT + 1

diffusion_rate = 0.0615

VMEM = pl.BlockSpec(memory_space=pltpu.VMEM)
SMEM = pl.BlockSpec(memory_space=pltpu.SMEM)
ANY = pl.BlockSpec(memory_space=pl.ANY)


def lane_index(shape=(TILE, LANES)):
    return lax.broadcasted_iota(jnp.int32, shape, len(shape) - 1)


def pack_kernel(owners, ids_ref, blocks_ref, out_ref):
    listed = ids_ref.shape[1]
    lane = lane_index()
    zero = jnp.zeros((TILE, LANES), jnp.float32)
    for row in range(0, owners * MESSAGE, TILE):
        out_ref[row : row + TILE, :] = zero
    ids = [ids_ref[0, j] for j in range(listed)]
    owner_of = [lax.shift_right_logical(i, 5) for i in ids]
    for j in range(listed):
        owner = owner_of[j]
        within = lax.bitwise_and(ids[j], PER_OWNER - 1).astype(jnp.float32)
        rank = jnp.int32(0)
        for i in range(j):
            rank = rank + jnp.where(owner_of[i] == owner, 1, 0)
        base = owner * MESSAGE
        first = zero
        last = zero
        for a in range(RB // TILE):
            cells = blocks_ref[pl.ds(a * TILE * listed + j, TILE, stride=listed), :]
            start = pl.multiple_of(base + rank * RB + a * TILE, TILE)
            out_ref[pl.ds(start, TILE), :] = cells
            head = jnp.where(lane < 4, cells, 0.0)
            tail = jnp.where(lane >= LANES - 4, cells, 0.0)
            first = first + (pltpu.roll(head, 16 * a, 1) if a else head)
            last = last + pltpu.roll(tail, 16 * a + 4, 1)
        edge = pl.multiple_of(base + CAP * RB, TILE)
        here = pl.ds(edge, TILE)
        out_ref[here, :] = out_ref[here, :] + jnp.where(lane == LABELS + rank, within, 0.0)
        later = rank == 1
        to_left = jnp.where(later, pltpu.roll(first, 12, 1), pltpu.roll(first, 8, 1))
        to_left = to_left + jnp.where(lane == LABELS + 4 + rank, within, 0.0)
        to_right = jnp.where(later, pltpu.roll(last, 4, 1), last)
        to_right = to_right + jnp.where(lane == LABELS + 2 + rank, within, 0.0)

        @pl.when(owner > 0)
        def _():
            there = pl.ds(pl.multiple_of(edge - MESSAGE, TILE), TILE)
            out_ref[there, :] = out_ref[there, :] + to_left

        @pl.when(owner < owners - 1)
        def _():
            there = pl.ds(pl.multiple_of(edge + MESSAGE, TILE), TILE)
            out_ref[there, :] = out_ref[there, :] + to_right


def smooth_kernel(groups, arrived_hbm, smoother_ref, out_ref, arrived_ref, labels_ref, columns_ref, sems):
    labels_copy = pltpu.make_async_copy(
        arrived_hbm.at[:, pl.ds(CAP * RB, 1), :], labels_ref, sems.at[0]
    )
    cells_copy = pltpu.make_async_copy(arrived_hbm, arrived_ref, sems.at[1])
    labels_copy.start()
    cells_copy.start()
    lane = lane_index()
    columns_ref[...] = jnp.zeros_like(columns_ref)
    labels_copy.wait()
    cells_copy.wait()
    for g in range(groups):
        for rank in range(CAP):
            label = labels_ref[g, 0, LABELS + rank].astype(jnp.int32)
            row = lax.shift_right_logical(label, 2)
            segment = lax.bitwise_and(label, NSEG - 1)
            where = (
                pl.ds(pl.multiple_of(segment * RB, RB), RB),
                pl.ds(pl.multiple_of(row * LANES, LANES), LANES),
            )
            columns_ref[where] = columns_ref[where] + arrived_ref[g, rank * RB : (rank + 1) * RB, :]
        edges = arrived_ref[g, CAP * RB :, :]
        for h in range(2 * CAP):
            label = labels_ref[g, 0, LABELS + 2 + h].astype(jnp.int32)
            row = lax.shift_right_logical(label, 2)
            segment = lax.bitwise_and(label, NSEG - 1)
            target = (BPT - 1 - row) * 8 + (4 if h >= CAP else 0) + LANES
            for a in range(RB // TILE):
                source = 16 * a + 4 * h
                four = jnp.where((lane >= source) & (lane < source + 4), edges, 0.0)
                moved = pltpu.roll(four, lax.bitwise_and(target - source, LANES - 1), 1)
                where = (
                    pl.ds(pl.multiple_of(segment * RB + a * TILE, TILE), TILE),
                    pl.ds(BPT * LANES, LANES),
                )
                columns_ref[where] = columns_ref[where] + moved
    edge_columns = columns_ref[:, BPT * LANES :]
    columns_ref[:, BPT * LANES :] = edge_columns + pltpu.roll(edge_columns, LANES // 2, 1)
    half = NR // 2
    smoother = jnp.concatenate(
        [smoother_ref[pl.ds(0, half, stride=2), :], smoother_ref[pl.ds(1, half, stride=2), :]], axis=0
    )
    for row in range(BPT):
        done = jnp.dot(
            smoother,
            columns_ref[:, row * LANES : (row + 1) * LANES],
            precision=lax.Precision.HIGHEST,
            preferred_element_type=jnp.float32,
        )
        out_ref[pl.ds(row, half, stride=PIECE), :] = done[:half]
        out_ref[pl.ds(BPT + row, half, stride=PIECE), :] = done[half:]
    done = jnp.dot(
        smoother,
        columns_ref[:, BPT * LANES :],
        precision=lax.Precision.HIGHEST,
        preferred_element_type=jnp.float32,
    )
    low = lane_index((half, LANES)) < LANES // 2
    out_ref[pl.ds(2 * BPT, half, stride=PIECE), :] = jnp.where(low, done[:half], done[half:])


def diffuse_kernel(
    owners, cells_ref, level_ref, scale_hbm, out_ref, scale_ref, main_a, main_b, side_a, side_b, sems
):
    shells, rows, width = out_ref.shape
    here = lax.axis_index("ev")
    places = (jnp.maximum(here - 1, 0), here, jnp.minimum(here + 1, owners - 1))
    copies = [
        pltpu.make_async_copy(
            scale_hbm.at[:, pl.ds(pl.multiple_of(place * width, width), width)],
            scale_ref.at[n],
            sems.at[n],
        )
        for n, place in enumerate(places)
    ]
    for copy in copies:
        copy.start()
    lane = lane_index()
    nothing = jnp.zeros((TILE, LANES), jnp.float32)
    for buffer in (main_a, main_b, side_a, side_b):
        for shell in range(shells):
            buffer[shell, 0:TILE, :] = nothing
            buffer[shell, TILE + rows : 2 * TILE + rows, :] = nothing
    is_side = (lane < 4) | (lane >= LANES - 4)
    for stripe in range(rows // BPT):
        at = stripe * PIECE
        wide = jnp.broadcast_to(cells_ref[at + 2 * BPT : at + PIECE, :], (TILE, LANES))
        for shell in range(shells):
            spot = TILE + stripe * BPT
            main_a[shell, spot : spot + BPT, :] = cells_ref[at + shell * BPT : at + (shell + 1) * BPT, :]
            turned = pltpu.roll(wide, 68 - 64 * shell, 1, stride=8, stride_axis=0)
            side_a[shell, spot : spot + BPT, :] = jnp.where(is_side, turned, 0.0)
    for copy in copies:
        copy.wait()
    factors = [diffusion_rate * level_ref[shell].astype(jnp.float32) for shell in range(shells)]
    step = 16
    lane = lane_index((step, LANES))
    is_first = lane == 0
    is_last = lane == LANES - 1
    keep_right = (lane < 4) & (here < owners - 1)
    keep_left = (lane >= LANES - 4) & (here > 0)

    def around(buffer, shell, start):
        above = buffer[shell, start - 1 : start - 1 + step, :]
        middle = buffer[shell, start : start + step, :]
        below = buffer[shell, start + 1 : start + 1 + step, :]
        return above + below, middle, pltpu.roll(middle, 1, 1), pltpu.roll(middle, LANES - 1, 1)

    buffers = ((main_a, side_a), (main_b, side_b))
    for repeat in range(PASSES):
        (main, side), (main_next, side_next) = buffers[repeat % 2], buffers[(repeat + 1) % 2]
        final = repeat == PASSES - 1
        for block in range(rows // step):
            start = TILE + block * step
            at = slice(block * step, (block + 1) * step)
            scale = scale_ref[1, at, :]
            if not final:
                scale_side = jnp.where(
                    keep_right, scale_ref[2, at, :], jnp.where(keep_left, scale_ref[0, at, :], 0.0)
                )
            for shell in range(shells):
                vertical, middle, left, right = around(main, shell, start)
                side_vertical, side_middle, side_left, side_right = around(side, shell, start)
                beside = vertical + jnp.where(is_first, side_left, left) + jnp.where(is_last, side_right, right)
                new = middle + (factors[shell] * scale) * (beside - 4.0 * middle)
                if final:
                    out_ref[shell, at, :] = new
                    continue
                main_next[shell, start : start + step, :] = new
                beside = (
                    side_vertical
                    + jnp.where(is_first, left, side_left)
                    + jnp.where(is_last, right, side_right)
                )
                new = side_middle + (factors[shell] * scale_side) * (beside - 4.0 * side_middle)
                side_next[shell, start : start + step, :] = new


def per_device(partial_kernels, block_ids, radial_smoother, shell_level, lateral_scale):
    owners = lax.axis_size("ev")
    holders = lax.axis_size("sp")
    listed = block_ids.shape[1]
    rows = lateral_scale.shape[0]
    packed = pl.pallas_call(
        functools.partial(pack_kernel, owners),
        out_shape=jax.ShapeDtypeStruct((owners * MESSAGE, LANES), jnp.float32),
        in_specs=[SMEM, VMEM],
        out_specs=VMEM,
    )(block_ids, partial_kernels.reshape(RB * listed, BY))
    arrived = lax.all_to_all(
        packed.reshape(owners, MESSAGE, LANES), "ev", split_axis=0, concat_axis=0, tiled=True
    )
    pieces = pl.pallas_call(
        functools.partial(smooth_kernel, owners),
        out_shape=jax.ShapeDtypeStruct((holders * PIECE, LANES), jnp.float32),
        in_specs=[ANY, VMEM],
        out_specs=VMEM,
        scratch_shapes=[
            pltpu.VMEM((owners, MESSAGE, LANES), jnp.float32),
            pltpu.SMEM((owners, 1, LANES), jnp.float32),
            pltpu.VMEM((NR, (BPT + 1) * LANES), jnp.float32),
            pltpu.SemaphoreType.DMA((2,)),
        ],
    )(arrived, radial_smoother)
    shells = lax.all_to_all(
        pieces.reshape(holders, 1, PIECE * LANES), "sp", split_axis=0, concat_axis=0, tiled=True
    ).reshape(holders * PIECE, LANES)
    mine = shell_level.shape[0]
    field = pltpu.VMEM((mine, rows + 2 * TILE, LANES), jnp.float32)
    return pl.pallas_call(
        functools.partial(diffuse_kernel, owners),
        out_shape=jax.ShapeDtypeStruct((mine, rows, LANES), jnp.float32),
        in_specs=[VMEM, SMEM, ANY],
        out_specs=VMEM,
        scratch_shapes=[
            pltpu.VMEM((3, rows, LANES), jnp.float32),
            field,
            field,
            field,
            field,
            pltpu.SemaphoreType.DMA((3,)),
        ],
    )(shells, shell_level, lateral_scale)


def solution(mesh):
    placed = (P("ev", None, "sp", None), P("ev", "sp"), P(), P("sp"), P())
    return jax.shard_map(
        per_device, mesh=mesh, in_specs=placed, out_specs=P("sp", None, "ev"), check_vma=False
    )
```

```python
import functools

import jax
import jax.numpy as jnp
from jax import lax
from jax.experimental import pallas as pl
from jax.experimental.pallas import tpu as pltpu
from jax.sharding import PartitionSpec as P

NR = 128
RB = 32
BY = 128
BPT = 8
CAP = 2
PASSES = 4
NSEG = 4
PER_OWNER = BPT * NSEG
LANES = 128
TILE = 8
MESSAGE = CAP * RB + TILE
LABELS = 64
STRIP = 16
SIDES = 4
PIECE = 2 * BPT + 1

diffusion_rate = 0.0615

SMALL = pltpu.CompilerParams(vmem_limit_bytes=12 * 1024 * 1024)
VMEM = pl.BlockSpec(memory_space=pltpu.VMEM)
HBM = pl.BlockSpec(memory_space=pltpu.HBM)


def lane_index(shape=(TILE, LANES)):
    return lax.broadcasted_iota(jnp.int32, shape, len(shape) - 1)


def pack_kernel(owners, ids_hbm, blocks_hbm, out_ref, ids_ref, blocks_ref, sems):
    ids_copy = pltpu.make_async_copy(ids_hbm, ids_ref, sems.at[0])
    blocks_copy = pltpu.make_async_copy(blocks_hbm, blocks_ref, sems.at[1])
    ids_copy.start()
    blocks_copy.start()
    listed = ids_ref.shape[1]
    lane = lane_index()
    zero = jnp.zeros((TILE, LANES), jnp.float32)
    for row in range(0, owners * MESSAGE, TILE):
        out_ref[row : row + TILE, :] = zero
    ids_copy.wait()
    ids = [ids_ref[0, j] for j in range(listed)]
    owner_of = [lax.shift_right_logical(i, 5) for i in ids]
    ranks = []
    for j in range(listed):
        rank = jnp.int32(0)
        for i in range(j):
            rank = rank + jnp.where(owner_of[i] == owner_of[j], 1, 0)
        ranks.append(rank)
    blocks_copy.wait()

    def add(owner, cells):
        there = pl.ds(pl.multiple_of(owner * MESSAGE + CAP * RB, TILE), TILE)
        out_ref[there, :] = out_ref[there, :] + cells

    for j in range(listed):
        owner, rank = owner_of[j], ranks[j]
        within = lax.bitwise_and(ids[j], PER_OWNER - 1).astype(jnp.float32)
        first = zero
        last = zero
        for a in range(RB // TILE):
            cells = blocks_ref[pl.ds(a * TILE * listed + j, TILE, stride=listed), :]
            start = pl.multiple_of(owner * MESSAGE + rank * RB + a * TILE, TILE)
            out_ref[pl.ds(start, TILE), :] = cells
            head = jnp.where(lane < 4, cells, 0.0)
            tail = jnp.where(lane >= LANES - 4, cells, 0.0)
            first = first + (pltpu.roll(head, 16 * a, 1) if a else head)
            last = last + pltpu.roll(tail, 16 * a + 4, 1)
        add(owner, jnp.where(lane == LABELS + rank, within, 0.0))
        later = rank == 1
        to_left = jnp.where(later, pltpu.roll(first, 12, 1), pltpu.roll(first, 8, 1))
        to_left = to_left + jnp.where(lane == LABELS + 4 + rank, within, 0.0)
        to_right = jnp.where(later, pltpu.roll(last, 4, 1), last)
        to_right = to_right + jnp.where(lane == LABELS + 2 + rank, within, 0.0)
        add(jnp.maximum(owner - 1, 0), jnp.where(owner > 0, to_left, 0.0))
        add(jnp.minimum(owner + 1, owners - 1), jnp.where(owner < owners - 1, to_right, 0.0))


def halves(cells):
    high = cells.astype(jnp.bfloat16)
    low = (cells - high.astype(jnp.float32)).astype(jnp.bfloat16)
    return high, low


def smooth_kernel(
    groups, arrived_ref, smoother_hbm, out_ref, spots_ref, labels_ref, columns_ref, smoother_ref, sems
):
    smoother_copy = pltpu.make_async_copy(smoother_hbm, smoother_ref, sems.at[1])
    smoother_copy.start()
    labels = arrived_ref[:, CAP * RB, :].astype(jnp.int32)
    rows = lax.shift_right_logical(labels, 2)
    label_lane = lane_index((groups, LANES)) - (LABELS + CAP)
    shift = jnp.where(label_lane >= CAP, 4, 0)
    spots_ref[0] = lax.bitwise_and(labels, NSEG - 1) * RB
    spots_ref[1] = rows * LANES
    spots_ref[2] = (BPT - 1 - rows) * 8 + shift
    labels_copy = pltpu.make_async_copy(spots_ref, labels_ref, sems.at[0])
    labels_copy.start()
    lane = lane_index()
    lane_four = lax.bitwise_and(lane, ~3)
    columns_ref[...] = jnp.zeros_like(columns_ref)
    labels_copy.wait()
    for g in range(groups):
        for rank in range(CAP):
            where = (
                pl.ds(pl.multiple_of(labels_ref[0, g, LABELS + rank], RB), RB),
                pl.ds(pl.multiple_of(labels_ref[1, g, LABELS + rank], LANES), LANES),
            )
            columns_ref[where] = columns_ref[where] + arrived_ref[g, rank * RB : (rank + 1) * RB, :]
    for g in range(groups):
        edges = arrived_ref[g, CAP * RB :, :]
        for h in range(2 * CAP):
            target = labels_ref[2, g, LABELS + CAP + h]
            keep = lane_four == target
            turned = pltpu.roll(edges, lax.bitwise_and(target + (LANES - 4 * h), LANES - 1), 1)
            parts = [turned] + [
                pltpu.roll(turned, LANES - 16 * a, 1) for a in range(1, RB // TILE)
            ]
            four = jnp.concatenate([jnp.where(keep, part, 0.0) for part in parts], axis=0)
            where = (
                pl.ds(pl.multiple_of(labels_ref[0, g, LABELS + CAP + h], RB), RB),
                pl.ds(BPT * LANES, LANES),
            )
            columns_ref[where] = columns_ref[where] + four
    edge_columns = columns_ref[:, BPT * LANES :]
    columns_ref[:, BPT * LANES :] = edge_columns + pltpu.roll(edge_columns, LANES // 2, 1)
    smoother_copy.wait()
    half = NR // 2
    smoother = jnp.concatenate(
        [smoother_ref[pl.ds(0, half, stride=2), :], smoother_ref[pl.ds(1, half, stride=2), :]], axis=0
    )
    high, low = halves(smoother)
    twice = jnp.concatenate([high, high], axis=1)

    def smoothed(start, width):
        first, second = halves(columns_ref[:, start : start + width])
        both = jnp.concatenate([first, second], axis=0)
        return jnp.dot(twice, both, preferred_element_type=jnp.float32) + jnp.dot(
            low, first, preferred_element_type=jnp.float32
        )

    for row in range(0, BPT, 2):
        done = smoothed(row * LANES, 2 * LANES)
        for i in range(2):
            cells = done[:, i * LANES : (i + 1) * LANES]
            out_ref[pl.ds(row + i, half, stride=PIECE), :] = cells[:half]
            out_ref[pl.ds(BPT + row + i, half, stride=PIECE), :] = cells[half:]
    done = smoothed(BPT * LANES, LANES)
    lower = lane_index((half, LANES)) < LANES // 2
    out_ref[pl.ds(2 * BPT, half, stride=PIECE), :] = jnp.where(lower, done[:half], done[half:])


def diffuse_kernel(
    owners, cells_ref, level_hbm, scale_ref, out_hbm,
    level_ref, main_a, main_b, side_a, side_b, side_scale, centre_ref, beside_ref, out_ref,
    near_ref, side_near_ref, edge_ref, sems,
):
    shells, rows, width = out_ref.shape
    level_copy = pltpu.make_async_copy(level_hbm, level_ref, sems.at[SIDES])
    level_copy.start()
    here = lax.axis_index("ev")
    own = pl.multiple_of(here * width, width)
    before = pl.multiple_of(jnp.maximum(here - 1, 0) * width, width)
    after = pl.multiple_of(jnp.minimum(here + 1, owners - 1) * width, width)
    nothing = jnp.zeros((TILE, LANES), jnp.float32)
    stripes = rows // BPT
    tiles = stripes // SIDES
    side_rows = tiles * TILE
    chunk = 8 * TILE
    for buffer in (main_a, main_b):
        for shell in range(shells):
            buffer[shell, 0:TILE, :] = nothing
            buffer[shell, TILE + rows : 2 * TILE + rows, :] = nothing

    row_of = lax.broadcasted_iota(jnp.int32, (LANES, LANES), 0)
    lane_of = lax.broadcasted_iota(jnp.int32, (LANES, LANES), 1)

    def ones(chosen):
        return jnp.where(chosen, 1.0, 0.0).astype(jnp.bfloat16)

    near = ones(jnp.abs(row_of - lane_of) == 1)
    near_ref[0:LANES, :] = near
    near_ref[LANES:, :] = near
    from_in, to_in = lax.bitwise_and(row_of, STRIP - 1), lax.bitwise_and(lane_of, STRIP - 1)
    same_strip = lax.shift_right_logical(row_of, 4) == lax.shift_right_logical(lane_of, 4)
    same_run = lax.shift_right_logical(row_of, 2) == lax.shift_right_logical(lane_of, 2)
    joined = (jnp.abs(from_in - to_in) == 7) & (jnp.maximum(from_in, to_in) == 11)
    joined = joined | ((jnp.abs(from_in - to_in) == 9) & (jnp.maximum(from_in, to_in) == 12))
    side_near = ones(((jnp.abs(row_of - lane_of) == 1) & same_run) | (joined & same_strip))
    exchanged = jnp.where(to_in == 11, lane_of + 1, jnp.where(to_in == 12, lane_of - 1, lane_of))
    exchange = ones(row_of == exchanged)
    for part in range(2):
        at = slice(part * LANES, (part + 1) * LANES)
        side_near_ref[at, 0:LANES] = side_near
        side_near_ref[at, LANES:] = exchange

    lane = lane_index()
    spot_in = lax.bitwise_and(lane, STRIP - 1)
    in_strip = [(lane >= STRIP * n) & (lane < STRIP * (n + 1)) for n in range(2 * SIDES)]
    inner = spot_in < 8
    outer = spot_in >= 8
    for v in range(tiles):
        side = nothing
        for n in range(SIDES):
            stripe = n * tiles + v
            at = stripe * PIECE
            spot = TILE + stripe * BPT
            wide = jnp.broadcast_to(cells_ref[at + 2 * BPT : at + PIECE, :], (TILE, LANES))
            turned = pltpu.roll(wide, STRIP * (n + 1), 1, stride=8, stride_axis=0)
            side = jnp.where((in_strip[n] | in_strip[SIDES + n]) & outer, turned, side)
            for shell in range(shells):
                cells = cells_ref[at + shell * BPT : at + (shell + 1) * BPT, :]
                main_a[shell, spot : spot + BPT, :] = cells
                slot = (1 - shell) * SIDES + n
                side = jnp.where(
                    in_strip[slot] & inner, pltpu.roll(cells, STRIP * slot + 4, 1), side
                )
        side_a[TILE + v * TILE : 2 * TILE + v * TILE, :] = side
    keep_after = (lane < 4) & (here < owners - 1)
    keep_before = (lane >= LANES - 4) & (here > 0)
    for v in range(tiles):
        scale = nothing
        for n in range(SIDES):
            stripe = n * tiles + v
            at = slice(stripe * BPT, (stripe + 1) * BPT)
            beyond = jnp.where(
                keep_after,
                scale_ref[at, pl.ds(after, width)],
                jnp.where(keep_before, scale_ref[at, pl.ds(before, width)], 0.0),
            )
            mine = pltpu.roll(scale_ref[at, pl.ds(own, width)], STRIP * n + 4, 1)
            scale = jnp.where(in_strip[n] & inner, mine, scale)
            scale = jnp.where(in_strip[n] & outer, pltpu.roll(beyond, STRIP * n + 12, 1), scale)
        side_scale[v * TILE : (v + 1) * TILE, :] = scale + pltpu.roll(scale, LANES // 2, 1)

    lane_row = lane_index((1, LANES))
    stripe_in = lax.bitwise_and(lane_row, SIDES * STRIP - 1)
    last_row = TILE + side_rows - 1

    def join(side):
        down = pltpu.roll(side[last_row : last_row + 1, :], STRIP, 1)
        side[TILE - 1 : TILE, :] = jnp.where(stripe_in < STRIP, 0.0, down)
        up = pltpu.roll(side[TILE : TILE + 1, :], LANES - STRIP, 1)
        side[last_row + 1 : last_row + 2, :] = jnp.where(stripe_in >= (SIDES - 1) * STRIP, 0.0, up)

    join(side_a)
    level_copy.wait()
    factors = [diffusion_rate * level_ref[shell].astype(jnp.float32) for shell in range(shells)]
    chunk_lane = lane_index((chunk, LANES))
    is_edge = (chunk_lane == 0) | (chunk_lane == LANES - 1)
    side_factor = jnp.where(chunk_lane < LANES // 2, factors[1], factors[0])
    copies = []
    buffers = ((main_a, side_a), (main_b, side_b))
    for repeat in range(PASSES):
        (main, side), (main_next, side_next) = buffers[repeat % 2], buffers[(repeat + 1) % 2]
        final = repeat == PASSES - 1
        for start in range(0, side_rows, chunk):
            at = slice(TILE + start, TILE + start + chunk)
            middle = side[at, :]
            sums = jnp.dot(
                jnp.concatenate(halves(middle), axis=1),
                side_near_ref[...],
                preferred_element_type=jnp.float32,
            )
            edge_ref[start : start + chunk, :] = sums[:, LANES:]
            if not final:
                vertical = side[at.start - 1 : at.stop - 1, :] + side[at.start + 1 : at.stop + 1, :]
                coefficient = side_factor * side_scale[start : start + chunk, :]
                side_next[at, :] = middle + coefficient * (
                    (vertical + sums[:, :LANES]) - 4.0 * middle
                )
        if not final:
            join(side_next)
        for n in range(SIDES):
            for shell in range(shells):
                slot = (1 - shell) * SIDES + n
                for part in range(0, side_rows, chunk):
                    edge = edge_ref[part : part + chunk, :]
                    start = n * side_rows + part
                    at = slice(start, start + chunk)
                    first = TILE + start
                    middle = main[shell, first : first + chunk, :]
                    sums = jnp.dot(
                        jnp.concatenate(halves(middle), axis=1),
                        near_ref[...],
                        preferred_element_type=jnp.float32,
                    )
                    turned = pltpu.roll(edge, (2 * LANES - STRIP * slot - 12) % LANES, 1)
                    vertical = (
                        main[shell, first - 1 : first + chunk - 1, :]
                        + main[shell, first + 1 : first + chunk + 1, :]
                    )
                    if repeat == 0:
                        coefficient = factors[shell] * scale_ref[at, pl.ds(own, width)]
                        centre = 1.0 - 4.0 * coefficient
                        beside_ref[shell, at, :] = coefficient
                        centre_ref[shell, at, :] = centre
                    else:
                        coefficient = beside_ref[shell, at, :]
                        centre = centre_ref[shell, at, :]
                    sums = (vertical + sums) + jnp.where(is_edge, turned, 0.0)
                    new = centre * middle + coefficient * sums
                    if final:
                        out_ref[shell, at, :] = new
                    else:
                        main_next[shell, first : first + chunk, :] = new
            if final:
                done = pl.ds(n * side_rows, side_rows)
                copy = pltpu.make_async_copy(out_ref.at[:, done, :], out_hbm.at[:, done, :], sems.at[n])
                copy.start()
                copies.append(copy)
    for copy in copies:
        copy.wait()


def in_hbm(array):
    return pltpu.with_memory_space_constraint(array, pltpu.HBM)


def per_device(partial_kernels, block_ids, radial_smoother, shell_level, lateral_scale):
    owners = lax.axis_size("ev")
    holders = lax.axis_size("sp")
    listed = block_ids.shape[1]
    rows, columns = lateral_scale.shape
    mine = shell_level.shape[0]
    packed = pl.pallas_call(
        functools.partial(pack_kernel, owners),
        out_shape=jax.ShapeDtypeStruct((owners * MESSAGE, LANES), jnp.float32),
        in_specs=[HBM, HBM],
        out_specs=VMEM,
        scratch_shapes=[
            pltpu.SMEM((1, listed), jnp.int32),
            pltpu.VMEM((RB * listed, LANES), jnp.float32),
            pltpu.SemaphoreType.DMA((2,)),
        ],
        compiler_params=SMALL,
    )(in_hbm(block_ids), in_hbm(partial_kernels.reshape(RB * listed, BY)))
    arrived = lax.all_to_all(
        packed.reshape(owners, MESSAGE, LANES), "ev", split_axis=0, concat_axis=0, tiled=True
    )
    pieces = pl.pallas_call(
        functools.partial(smooth_kernel, owners),
        out_shape=jax.ShapeDtypeStruct((holders * PIECE, LANES), jnp.float32),
        in_specs=[VMEM, HBM],
        out_specs=VMEM,
        scratch_shapes=[
            pltpu.VMEM((3, owners, LANES), jnp.int32),
            pltpu.SMEM((3, owners, LANES), jnp.int32),
            pltpu.VMEM((NR, (BPT + 1) * LANES), jnp.float32),
            pltpu.VMEM((NR, NR), jnp.float32),
            pltpu.SemaphoreType.DMA((2,)),
        ],
        compiler_params=SMALL,
    )(arrived, in_hbm(radial_smoother))
    shells = lax.all_to_all(
        pieces.reshape(holders, 1, PIECE * LANES), "sp", split_axis=0, concat_axis=0, tiled=True
    ).reshape(holders * PIECE, LANES)
    padded = pltpu.VMEM((mine, rows + 2 * TILE, LANES), jnp.float32)
    plain = pltpu.VMEM((mine, rows, LANES), jnp.float32)
    side_rows = holders // SIDES * TILE
    side = pltpu.VMEM((side_rows + 2 * TILE, LANES), jnp.float32)
    return pl.pallas_call(
        functools.partial(diffuse_kernel, owners),
        out_shape=jax.ShapeDtypeStruct((mine, rows, columns // owners), jnp.float32),
        in_specs=[VMEM, HBM, VMEM],
        out_specs=HBM,
        scratch_shapes=[
            pltpu.SMEM((mine,), jnp.int32),
            padded,
            padded,
            side,
            side,
            pltpu.VMEM((side_rows, LANES), jnp.float32),
            plain,
            plain,
            plain,
            pltpu.VMEM((2 * LANES, LANES), jnp.bfloat16),
            pltpu.VMEM((2 * LANES, 2 * LANES), jnp.bfloat16),
            pltpu.VMEM((side_rows, LANES), jnp.float32),
            pltpu.SemaphoreType.DMA((SIDES + 1,)),
        ],
        compiler_params=SMALL,
    )(shells, in_hbm(shell_level), lateral_scale)


def solution(mesh):
    placed = (P("ev", None, "sp", None), P("ev", "sp"), P(), P("sp"), P())
    return jax.shard_map(
        per_device, mesh=mesh, in_specs=placed, out_specs=P("sp", None, "ev"), check_vma=False
    )
```

```python
import functools

import jax
import jax.numpy as jnp
from jax import lax
from jax.experimental import pallas as pl
from jax.experimental.pallas import tpu as pltpu
from jax.sharding import PartitionSpec as P

NR = 128
RB = 32
BY = 128
BPT = 8
CAP = 2
PASSES = 4
NSEG = 4
PER_OWNER = BPT * NSEG
LANES = 128
TILE = 8
MESSAGE = CAP * RB + TILE
LABELS = 64
STRIP = 16
SIDES = 4
PIECE = 2 * BPT + 1

diffusion_rate = 0.0615

SMALL = pltpu.CompilerParams(vmem_limit_bytes=12 * 1024 * 1024)
VMEM = pl.BlockSpec(memory_space=pltpu.VMEM)
HBM = pl.BlockSpec(memory_space=pltpu.HBM)


def lane_index(shape=(TILE, LANES)):
    return lax.broadcasted_iota(jnp.int32, shape, len(shape) - 1)


def stencil_matrices(near_ref, side_near_ref):
    row_of = lax.broadcasted_iota(jnp.int32, (LANES, LANES), 0)
    lane_of = lax.broadcasted_iota(jnp.int32, (LANES, LANES), 1)
    beside = jnp.abs(row_of - lane_of) == 1
    middle = jnp.where(row_of == lane_of, -4.0, 0.0)
    near = jnp.where(beside, 1.0, middle).astype(jnp.bfloat16)
    from_in, to_in = lax.bitwise_and(row_of, STRIP - 1), lax.bitwise_and(lane_of, STRIP - 1)
    same_strip = lax.shift_right_logical(row_of, 4) == lax.shift_right_logical(lane_of, 4)
    same_run = lax.shift_right_logical(row_of, 2) == lax.shift_right_logical(lane_of, 2)
    apart, later = jnp.abs(from_in - to_in), jnp.maximum(from_in, to_in)
    joined = ((apart == 7) & (later == 11)) | ((apart == 9) & (later == 12))
    side_near = jnp.where((beside & same_run) | (joined & same_strip), 1.0, middle).astype(jnp.bfloat16)
    exchanged = jnp.where(to_in == 11, lane_of + 1, jnp.where(to_in == 12, lane_of - 1, lane_of))
    exchange = jnp.where(row_of == exchanged, 1.0, 0.0).astype(jnp.bfloat16)
    for part in range(2):
        at = slice(part * LANES, (part + 1) * LANES)
        near_ref[at, :] = near
        side_near_ref[at, 0:LANES] = side_near
        side_near_ref[at, LANES:] = exchange


def pack_kernel(
    owners, ids_hbm, blocks_hbm, scale_hbm, out_ref, scale_ref, near_ref, side_near_ref,
    ids_ref, blocks_ref, sems,
):
    ids_copy = pltpu.make_async_copy(ids_hbm, ids_ref, sems.at[0])
    blocks_copy = pltpu.make_async_copy(blocks_hbm, blocks_ref, sems.at[1])
    ids_copy.start()
    blocks_copy.start()
    here = lax.axis_index("ev")
    width = scale_ref.shape[2]
    places = (jnp.maximum(here - 1, 0), here, jnp.minimum(here + 1, owners - 1))
    scale_copies = [
        pltpu.make_async_copy(
            scale_hbm.at[:, pl.ds(pl.multiple_of(place * width, width), width)],
            scale_ref.at[n],
            sems.at[2 + n],
        )
        for n, place in enumerate(places)
    ]
    for copy in scale_copies:
        copy.start()
    listed = ids_ref.shape[1]
    lane = lane_index()
    zero = jnp.zeros((TILE, LANES), jnp.float32)
    for row in range(0, owners * MESSAGE, TILE):
        out_ref[row : row + TILE, :] = zero
    stencil_matrices(near_ref, side_near_ref)
    ids_copy.wait()
    ids = [ids_ref[0, j] for j in range(listed)]
    owner_of = [lax.shift_right_logical(i, 5) for i in ids]
    ranks = []
    for j in range(listed):
        rank = jnp.int32(0)
        for i in range(j):
            rank = rank + jnp.where(owner_of[i] == owner_of[j], 1, 0)
        ranks.append(rank)
    blocks_copy.wait()

    def add(owner, cells):
        there = pl.ds(pl.multiple_of(owner * MESSAGE + CAP * RB, TILE), TILE)
        out_ref[there, :] = out_ref[there, :] + cells

    for j in range(listed):
        owner, rank = owner_of[j], ranks[j]
        within = lax.bitwise_and(ids[j], PER_OWNER - 1).astype(jnp.float32)
        first = zero
        last = zero
        for a in range(RB // TILE):
            cells = blocks_ref[pl.ds(a * TILE * listed + j, TILE, stride=listed), :]
            start = pl.multiple_of(owner * MESSAGE + rank * RB + a * TILE, TILE)
            out_ref[pl.ds(start, TILE), :] = cells
            head = jnp.where(lane < 4, cells, 0.0)
            tail = jnp.where(lane >= LANES - 4, cells, 0.0)
            first = first + (pltpu.roll(head, 16 * a, 1) if a else head)
            last = last + pltpu.roll(tail, 16 * a + 4, 1)
        add(owner, jnp.where(lane == LABELS + rank, within, 0.0))
        later = rank == 1
        to_left = jnp.where(later, pltpu.roll(first, 12, 1), pltpu.roll(first, 8, 1))
        to_left = to_left + jnp.where(lane == LABELS + 4 + rank, within, 0.0)
        to_right = jnp.where(later, pltpu.roll(last, 4, 1), last)
        to_right = to_right + jnp.where(lane == LABELS + 2 + rank, within, 0.0)
        add(jnp.maximum(owner - 1, 0), jnp.where(owner > 0, to_left, 0.0))
        add(jnp.minimum(owner + 1, owners - 1), jnp.where(owner < owners - 1, to_right, 0.0))
    for copy in scale_copies:
        copy.wait()


def halves(cells):
    high = cells.astype(jnp.bfloat16)
    low = (cells - high.astype(jnp.float32)).astype(jnp.bfloat16)
    return high, low


def scale_strips(scale_ref, owners):
    here = lax.axis_index("ev")
    part = scale_ref.shape[1] // SIDES
    lane = lane_index((part, LANES))
    inner = lax.bitwise_and(lane, STRIP - 1) < 8
    strip = lax.shift_right_logical(lane, 4)
    keep_after = (lane < 4) & (here < owners - 1)
    keep_before = (lane >= LANES - 4) & (here > 0)
    strips = jnp.zeros((part, LANES), jnp.float32)
    for n in range(SIDES):
        at = slice(n * part, (n + 1) * part)
        beyond = jnp.where(keep_before, scale_ref[0, at, :], 0.0)
        beyond = jnp.where(keep_after, scale_ref[2, at, :], beyond)
        both = jnp.where(
            inner,
            pltpu.roll(scale_ref[1, at, :], STRIP * n + 4, 1),
            pltpu.roll(beyond, STRIP * n + 12, 1),
        )
        strips = jnp.where(strip == n, both, strips)
    return strips + pltpu.roll(strips, LANES // 2, 1)


def smooth_kernel(
    groups, arrived_ref, scale_ref, smoother_hbm, out_ref, side_scale_ref,
    spots_ref, labels_ref, columns_ref, smoother_ref, sems,
):
    smoother_copy = pltpu.make_async_copy(smoother_hbm, smoother_ref, sems.at[1])
    smoother_copy.start()
    labels = arrived_ref[:, CAP * RB, :].astype(jnp.int32)
    rows = lax.shift_right_logical(labels, 2)
    label_lane = lane_index((groups, LANES)) - (LABELS + CAP)
    shift = jnp.where(label_lane >= CAP, 4, 0)
    spots_ref[0] = lax.bitwise_and(labels, NSEG - 1) * RB
    spots_ref[1] = rows * LANES
    spots_ref[2] = (BPT - 1 - rows) * 8 + shift
    labels_copy = pltpu.make_async_copy(spots_ref, labels_ref, sems.at[0])
    labels_copy.start()
    lane = lane_index()
    lane_four = lax.bitwise_and(lane, ~3)
    columns_ref[...] = jnp.zeros_like(columns_ref)
    side_scale_ref[...] = scale_strips(scale_ref, groups)
    labels_copy.wait()
    for g in range(groups):
        for rank in range(CAP):
            where = (
                pl.ds(pl.multiple_of(labels_ref[0, g, LABELS + rank], RB), RB),
                pl.ds(pl.multiple_of(labels_ref[1, g, LABELS + rank], LANES), LANES),
            )
            columns_ref[where] = columns_ref[where] + arrived_ref[g, rank * RB : (rank + 1) * RB, :]
    for g in range(groups):
        edges = arrived_ref[g, CAP * RB :, :]
        for h in range(2 * CAP):
            target = labels_ref[2, g, LABELS + CAP + h]
            keep = lane_four == target
            turned = pltpu.roll(edges, lax.bitwise_and(target + (LANES - 4 * h), LANES - 1), 1)
            parts = [turned] + [
                pltpu.roll(turned, LANES - 16 * a, 1) for a in range(1, RB // TILE)
            ]
            four = jnp.concatenate([jnp.where(keep, part, 0.0) for part in parts], axis=0)
            where = (
                pl.ds(pl.multiple_of(labels_ref[0, g, LABELS + CAP + h], RB), RB),
                pl.ds(BPT * LANES, LANES),
            )
            columns_ref[where] = columns_ref[where] + four
    edge_columns = columns_ref[:, BPT * LANES :]
    columns_ref[:, BPT * LANES :] = edge_columns + pltpu.roll(edge_columns, LANES // 2, 1)
    smoother_copy.wait()
    half = NR // 2
    smoother = jnp.concatenate(
        [smoother_ref[pl.ds(0, half, stride=2), :], smoother_ref[pl.ds(1, half, stride=2), :]], axis=0
    )
    high, low = halves(smoother)
    twice = jnp.concatenate([high, high], axis=1)

    def smoothed(start, width):
        first, second = halves(columns_ref[:, start : start + width])
        both = jnp.concatenate([first, second], axis=0)
        return jnp.dot(twice, both, preferred_element_type=jnp.float32) + jnp.dot(
            low, first, preferred_element_type=jnp.float32
        )

    for row in range(0, BPT, 2):
        done = smoothed(row * LANES, 2 * LANES)
        for i in range(2):
            cells = done[:, i * LANES : (i + 1) * LANES]
            out_ref[pl.ds(row + i, half, stride=PIECE), :] = cells[:half]
            out_ref[pl.ds(BPT + row + i, half, stride=PIECE), :] = cells[half:]
    done = smoothed(BPT * LANES, LANES)
    lower = lane_index((half, LANES)) < LANES // 2
    out_ref[pl.ds(2 * BPT, half, stride=PIECE), :] = jnp.where(lower, done[:half], done[half:])


def diffuse_kernel(
    cells_ref, level_hbm, scale_ref, side_scale_ref, near_ref, side_near_ref, out_hbm,
    level_ref, main_a, main_b, side_a, side_b, coefficient_ref, edge_ref, out_ref, sems,
):
    shells, rows, _ = out_ref.shape
    level_copy = pltpu.make_async_copy(level_hbm, level_ref, sems.at[SIDES])
    level_copy.start()
    nothing = jnp.zeros((TILE, LANES), jnp.float32)
    stripes = rows // BPT
    tiles = stripes // SIDES
    part = tiles * TILE
    for buffer in (main_a, main_b):
        for shell in range(shells):
            buffer[shell, 0:TILE, :] = nothing
            buffer[shell, TILE + rows : 2 * TILE + rows, :] = nothing
    slots = [(n, shell, (1 - shell) * SIDES + n) for n in range(SIDES) for shell in range(shells)]

    strip = lax.shift_right_logical(lane_index(), 4)
    for v in range(tiles):
        outer = nothing
        for n in range(SIDES):
            stripe = n * tiles + v
            at = stripe * PIECE
            spot = TILE + stripe * BPT
            wide = jnp.broadcast_to(cells_ref[at + 2 * BPT : at + PIECE, :], (TILE, LANES))
            turned = pltpu.roll(wide, STRIP * (n + 1), 1, stride=8, stride_axis=0)
            outer = jnp.where(lax.bitwise_and(strip, SIDES - 1) == n, turned, outer)
            for shell in range(shells):
                main_a[shell, spot : spot + BPT, :] = cells_ref[
                    at + shell * BPT : at + (shell + 1) * BPT, :
                ]
        side_a[TILE + v * TILE : 2 * TILE + v * TILE, :] = outer
    lane = lane_index((part, LANES))
    strip = lax.shift_right_logical(lane, 4)
    inner = lax.bitwise_and(lane, STRIP - 1) < 8
    side = side_a[TILE : TILE + part, :]
    for n, shell, slot in slots:
        cells = main_a[shell, TILE + n * part : TILE + (n + 1) * part, :]
        side = jnp.where(inner & (strip == slot), pltpu.roll(cells, STRIP * slot + 4, 1), side)
    side_a[TILE : TILE + part, :] = side

    lane_row = lane_index((1, LANES))
    stripe_in = lax.bitwise_and(lane_row, SIDES * STRIP - 1)
    last_row = TILE + part - 1

    def join(side):
        down = pltpu.roll(side[last_row : last_row + 1, :], STRIP, 1)
        side[TILE - 1 : TILE, :] = jnp.where(stripe_in < STRIP, 0.0, down)
        up = pltpu.roll(side[TILE : TILE + 1, :], LANES - STRIP, 1)
        side[last_row + 1 : last_row + 2, :] = jnp.where(stripe_in >= (SIDES - 1) * STRIP, 0.0, up)

    join(side_a)
    level_copy.wait()
    factors = [diffusion_rate * level_ref[shell].astype(jnp.float32) for shell in range(shells)]
    side_factor = jnp.where(lane < LANES // 2, factors[1], factors[0])
    is_edge = (lane == 0) | (lane == LANES - 1)

    def across(cells, matrix):
        return jnp.dot(
            jnp.concatenate(halves(cells), axis=1), matrix[...], preferred_element_type=jnp.float32
        )

    copies = []
    buffers = ((main_a, side_a), (main_b, side_b))
    for repeat in range(PASSES):
        (main, side), (main_next, side_next) = buffers[repeat % 2], buffers[(repeat + 1) % 2]
        final = repeat == PASSES - 1
        middle = side[TILE : TILE + part, :]
        sums = across(middle, side_near_ref)
        edge_ref[...] = sums[:, LANES:]
        if not final:
            vertical = side[TILE - 1 : TILE + part - 1, :] + side[TILE + 1 : TILE + part + 1, :]
            coefficient = side_factor * side_scale_ref[...]
            side_next[TILE : TILE + part, :] = middle + coefficient * (vertical + sums[:, :LANES])
            join(side_next)
        for n, shell, slot in slots:
            at = slice(n * part, (n + 1) * part)
            first = TILE + n * part
            middle = main[shell, first : first + part, :]
            sums = across(middle, near_ref)
            turned = pltpu.roll(edge_ref[...], (2 * LANES - STRIP * slot - 12) % LANES, 1)
            vertical = (
                main[shell, first - 1 : first + part - 1, :]
                + main[shell, first + 1 : first + part + 1, :]
            )
            if repeat == 0:
                coefficient = factors[shell] * scale_ref[1, at, :]
                coefficient_ref[shell, at, :] = coefficient
            else:
                coefficient = coefficient_ref[shell, at, :]
            new = middle + coefficient * ((vertical + sums) + jnp.where(is_edge, turned, 0.0))
            if not final:
                main_next[shell, first : first + part, :] = new
                continue
            out_ref[shell, at, :] = new
            if shell == shells - 1:
                done = pl.ds(n * part, part)
                copy = pltpu.make_async_copy(out_ref.at[:, done, :], out_hbm.at[:, done, :], sems.at[n])
                copy.start()
                copies.append(copy)
    for copy in copies:
        copy.wait()


def in_hbm(array):
    return pltpu.with_memory_space_constraint(array, pltpu.HBM)


def per_device(partial_kernels, block_ids, radial_smoother, shell_level, lateral_scale):
    owners = lax.axis_size("ev")
    holders = lax.axis_size("sp")
    listed = block_ids.shape[1]
    rows, columns = lateral_scale.shape
    mine = shell_level.shape[0]
    part = rows // SIDES
    packed, scale, near, side_near = pl.pallas_call(
        functools.partial(pack_kernel, owners),
        out_shape=[
            jax.ShapeDtypeStruct((owners * MESSAGE, LANES), jnp.float32),
            jax.ShapeDtypeStruct((3, rows, columns // owners), jnp.float32),
            jax.ShapeDtypeStruct((2 * LANES, LANES), jnp.bfloat16),
            jax.ShapeDtypeStruct((2 * LANES, 2 * LANES), jnp.bfloat16),
        ],
        in_specs=[HBM, HBM, HBM],
        out_specs=[VMEM, VMEM, VMEM, VMEM],
        scratch_shapes=[
            pltpu.SMEM((1, listed), jnp.int32),
            pltpu.VMEM((RB * listed, LANES), jnp.float32),
            pltpu.SemaphoreType.DMA((5,)),
        ],
        compiler_params=SMALL,
    )(
        in_hbm(block_ids),
        in_hbm(partial_kernels.reshape(RB * listed, BY)),
        in_hbm(lateral_scale),
    )
    arrived = lax.all_to_all(
        packed.reshape(owners, MESSAGE, LANES), "ev", split_axis=0, concat_axis=0, tiled=True
    )
    pieces, side_scale = pl.pallas_call(
        functools.partial(smooth_kernel, owners),
        out_shape=[
            jax.ShapeDtypeStruct((holders * PIECE, LANES), jnp.float32),
            jax.ShapeDtypeStruct((part, LANES), jnp.float32),
        ],
        in_specs=[VMEM, VMEM, HBM],
        out_specs=[VMEM, VMEM],
        scratch_shapes=[
            pltpu.VMEM((3, owners, LANES), jnp.int32),
            pltpu.SMEM((3, owners, LANES), jnp.int32),
            pltpu.VMEM((NR, (BPT + 1) * LANES), jnp.float32),
            pltpu.VMEM((NR, NR), jnp.float32),
            pltpu.SemaphoreType.DMA((2,)),
        ],
        compiler_params=SMALL,
    )(arrived, scale, in_hbm(radial_smoother))
    shells = lax.all_to_all(
        pieces.reshape(holders, 1, PIECE * LANES), "sp", split_axis=0, concat_axis=0, tiled=True
    ).reshape(holders * PIECE, LANES)
    padded = pltpu.VMEM((mine, rows + 2 * TILE, LANES), jnp.float32)
    plain = pltpu.VMEM((mine, rows, LANES), jnp.float32)
    side = pltpu.VMEM((part + 2 * TILE, LANES), jnp.float32)
    return pl.pallas_call(
        diffuse_kernel,
        out_shape=jax.ShapeDtypeStruct((mine, rows, columns // owners), jnp.float32),
        in_specs=[VMEM, HBM, VMEM, VMEM, VMEM, VMEM],
        out_specs=HBM,
        scratch_shapes=[
            pltpu.SMEM((mine,), jnp.int32),
            padded,
            padded,
            side,
            side,
            plain,
            pltpu.VMEM((part, LANES), jnp.float32),
            plain,
            pltpu.SemaphoreType.DMA((SIDES + 1,)),
        ],
        compiler_params=SMALL,
    )(shells, in_hbm(shell_level), scale, side_scale, near, side_near)


def solution(mesh):
    placed = (P("ev", None, "sp", None), P("ev", "sp"), P(), P("sp"), P())
    return jax.shard_map(
        per_device, mesh=mesh, in_specs=placed, out_specs=P("sp", None, "ev"), check_vma=False
    )
```

```python
import functools

import jax
import jax.numpy as jnp
from jax import lax
from jax.experimental import pallas as pl
from jax.experimental.pallas import tpu as pltpu
from jax.sharding import PartitionSpec as P

NR = 128
RB = 32
BY = 128
BPT = 8
CAP = 2
PASSES = 4
NSEG = 4
PER_OWNER = BPT * NSEG
LANES = 128
TILE = 8
MESSAGE = CAP * RB + TILE
LABELS = 64
STRIP = 16
SIDES = 4
PIECE = 2 * BPT + 1

diffusion_rate = 0.0615

SMALL = pltpu.CompilerParams(vmem_limit_bytes=12 * 1024 * 1024)
VMEM = pl.BlockSpec(memory_space=pltpu.VMEM)
HBM = pl.BlockSpec(memory_space=pltpu.HBM)


def lane_index(shape=(TILE, LANES)):
    return lax.broadcasted_iota(jnp.int32, shape, len(shape) - 1)


def stencil_matrices(near_ref, side_near_ref):
    row_of = lax.broadcasted_iota(jnp.int32, (LANES, LANES), 0)
    lane_of = lax.broadcasted_iota(jnp.int32, (LANES, LANES), 1)
    beside = jnp.abs(row_of - lane_of) == 1
    middle = jnp.where(row_of == lane_of, -4.0, 0.0)
    near = jnp.where(beside, 1.0, middle).astype(jnp.bfloat16)
    from_in, to_in = lax.bitwise_and(row_of, STRIP - 1), lax.bitwise_and(lane_of, STRIP - 1)
    same_strip = lax.shift_right_logical(row_of, 4) == lax.shift_right_logical(lane_of, 4)
    same_run = lax.shift_right_logical(row_of, 2) == lax.shift_right_logical(lane_of, 2)
    apart, later = jnp.abs(from_in - to_in), jnp.maximum(from_in, to_in)
    joined = ((apart == 7) & (later == 11)) | ((apart == 9) & (later == 12))
    side_near = jnp.where((beside & same_run) | (joined & same_strip), 1.0, middle).astype(jnp.bfloat16)
    exchanged = jnp.where(to_in == 11, lane_of + 1, jnp.where(to_in == 12, lane_of - 1, lane_of))
    exchange = jnp.where(row_of == exchanged, 1.0, 0.0).astype(jnp.bfloat16)
    for part in range(2):
        at = slice(part * LANES, (part + 1) * LANES)
        near_ref[at, :] = near
        side_near_ref[at, 0:LANES] = side_near
        side_near_ref[at, LANES:] = exchange


def pack_kernel(
    owners, ids_hbm, blocks_hbm, scale_hbm, smoother_hbm, level_hbm,
    out_ref, scale_ref, smoother_ref, factor_ref, near_ref, side_near_ref,
    ids_ref, blocks_ref, level_ref, sems,
):
    ids_copy = pltpu.make_async_copy(ids_hbm, ids_ref, sems.at[0])
    blocks_copy = pltpu.make_async_copy(blocks_hbm, blocks_ref, sems.at[1])
    ids_copy.start()
    blocks_copy.start()
    here = lax.axis_index("ev")
    width = scale_ref.shape[2]
    places = (jnp.maximum(here - 1, 0), here, jnp.minimum(here + 1, owners - 1))
    copies = [
        pltpu.make_async_copy(
            scale_hbm.at[:, pl.ds(pl.multiple_of(place * width, width), width)],
            scale_ref.at[n],
            sems.at[2 + n],
        )
        for n, place in enumerate(places)
    ]
    copies.append(pltpu.make_async_copy(smoother_hbm, smoother_ref, sems.at[5]))
    copies.append(pltpu.make_async_copy(level_hbm, level_ref, sems.at[6]))
    for copy in copies:
        copy.start()
    listed = ids_ref.shape[1]
    lane = lane_index()
    zero = jnp.zeros((TILE, LANES), jnp.float32)
    for row in range(0, owners * MESSAGE, TILE):
        out_ref[row : row + TILE, :] = zero
    stencil_matrices(near_ref, side_near_ref)
    ids_copy.wait()
    ids = [ids_ref[0, j] for j in range(listed)]
    owner_of = [lax.shift_right_logical(i, 5) for i in ids]
    ranks = []
    for j in range(listed):
        rank = jnp.int32(0)
        for i in range(j):
            rank = rank + jnp.where(owner_of[i] == owner_of[j], 1, 0)
        ranks.append(rank)
    blocks_copy.wait()

    def add(owner, cells):
        there = pl.ds(pl.multiple_of(owner * MESSAGE + CAP * RB, TILE), TILE)
        out_ref[there, :] = out_ref[there, :] + cells

    for j in range(listed):
        owner, rank = owner_of[j], ranks[j]
        within = lax.bitwise_and(ids[j], PER_OWNER - 1).astype(jnp.float32)
        first = zero
        last = zero
        for a in range(RB // TILE):
            cells = blocks_ref[pl.ds(a * TILE * listed + j, TILE, stride=listed), :]
            start = pl.multiple_of(owner * MESSAGE + rank * RB + a * TILE, TILE)
            out_ref[pl.ds(start, TILE), :] = cells
            head = jnp.where(lane < 4, cells, 0.0)
            tail = jnp.where(lane >= LANES - 4, cells, 0.0)
            first = first + (pltpu.roll(head, 16 * a, 1) if a else head)
            last = last + pltpu.roll(tail, 16 * a + 4, 1)
        add(owner, jnp.where(lane == LABELS + rank, within, 0.0))
        later = rank == 1
        to_left = jnp.where(later, pltpu.roll(first, 12, 1), pltpu.roll(first, 8, 1))
        to_left = to_left + jnp.where(lane == LABELS + 4 + rank, within, 0.0)
        to_right = jnp.where(later, pltpu.roll(last, 4, 1), last)
        to_right = to_right + jnp.where(lane == LABELS + 2 + rank, within, 0.0)
        add(jnp.maximum(owner - 1, 0), jnp.where(owner > 0, to_left, 0.0))
        add(jnp.minimum(owner + 1, owners - 1), jnp.where(owner < owners - 1, to_right, 0.0))
    for copy in copies:
        copy.wait()
    for shell in range(level_ref.shape[0]):
        factor = diffusion_rate * level_ref[shell].astype(jnp.float32)
        factor_ref[shell] = jnp.full((TILE, LANES), factor, jnp.float32)


def halves(cells):
    high = cells.astype(jnp.bfloat16)
    low = (cells - high.astype(jnp.float32)).astype(jnp.bfloat16)
    return high, low


def scale_strips(scale_ref, owners):
    here = lax.axis_index("ev")
    part = scale_ref.shape[1] // SIDES
    lane = lane_index((part, LANES))
    inner = lax.bitwise_and(lane, STRIP - 1) < 8
    strip = lax.shift_right_logical(lane, 4)
    keep_after = (lane < 4) & (here < owners - 1)
    keep_before = (lane >= LANES - 4) & (here > 0)
    strips = jnp.zeros((part, LANES), jnp.float32)
    for n in range(SIDES):
        at = slice(n * part, (n + 1) * part)
        beyond = jnp.where(keep_before, scale_ref[0, at, :], 0.0)
        beyond = jnp.where(keep_after, scale_ref[2, at, :], beyond)
        both = jnp.where(
            inner,
            pltpu.roll(scale_ref[1, at, :], STRIP * n + 4, 1),
            pltpu.roll(beyond, STRIP * n + 12, 1),
        )
        strips = jnp.where(strip == n, both, strips)
    return strips + pltpu.roll(strips, LANES // 2, 1)


def smooth_kernel(
    groups, arrived_ref, scale_ref, smoother_ref, out_ref, side_scale_ref,
    spots_ref, labels_ref, columns_ref, edge_ref, sems,
):
    labels = arrived_ref[:, CAP * RB, :].astype(jnp.int32)
    rows = lax.shift_right_logical(labels, 2)
    segments = lax.bitwise_and(labels, NSEG - 1)
    label_lane = lane_index((groups, LANES)) - (LABELS + CAP)
    spots_ref[0] = segments * jnp.where(label_lane >= 0, 2 * TILE, RB)
    spots_ref[1] = rows * LANES
    spots_ref[2] = (BPT - 1 - rows) * 8 + jnp.where(label_lane >= CAP, 4, 0)
    labels_copy = pltpu.make_async_copy(spots_ref, labels_ref, sems.at[0])
    labels_copy.start()
    lane = lane_index()
    low = lane < LANES // 2
    lane_four = lax.bitwise_and(lane, LANES // 2 - 4)
    columns_ref[:, : BPT * LANES] = jnp.zeros((NR, BPT * LANES), jnp.float32)
    edge_ref[...] = jnp.zeros_like(edge_ref)
    side_scale_ref[...] = scale_strips(scale_ref, groups)
    labels_copy.wait()
    for g in range(groups):
        for rank in range(CAP):
            where = (
                pl.ds(pl.multiple_of(labels_ref[0, g, LABELS + rank], RB), RB),
                pl.ds(pl.multiple_of(labels_ref[1, g, LABELS + rank], LANES), LANES),
            )
            columns_ref[where] = columns_ref[where] + arrived_ref[g, rank * RB : (rank + 1) * RB, :]
    for g in range(groups):
        edges = arrived_ref[g, CAP * RB :, :]
        pairs = [
            jnp.where(low, edges, pltpu.roll(edges, 48, 1)),
            jnp.where(low, pltpu.roll(edges, LANES - 32, 1), pltpu.roll(edges, 16, 1)),
        ]
        for h in range(2 * CAP):
            target = labels_ref[2, g, LABELS + CAP + h]
            keep = lane_four == target
            shift = lax.bitwise_and(target + (LANES - 4 * h), LANES - 1)
            four = jnp.concatenate(
                [jnp.where(keep, pltpu.roll(pair, shift, 1), 0.0) for pair in pairs], axis=0
            )
            where = pl.ds(pl.multiple_of(labels_ref[0, g, LABELS + CAP + h], 2 * TILE), 2 * TILE)
            edge_ref[where, :] = edge_ref[where, :] + four
    for pair in range(NR // (2 * TILE)):
        cells = edge_ref[pair * TILE : (pair + 1) * TILE, :]
        turned = pltpu.roll(cells, LANES // 2, 1)
        at = pair * 2 * TILE
        columns_ref[at : at + TILE, BPT * LANES :] = jnp.where(low, cells, turned)
        columns_ref[at + TILE : at + 2 * TILE, BPT * LANES :] = jnp.where(low, turned, cells)
    half = NR // 2
    smoother = jnp.concatenate(
        [smoother_ref[pl.ds(0, half, stride=2), :], smoother_ref[pl.ds(1, half, stride=2), :]], axis=0
    )
    high, rest = halves(smoother)
    twice = jnp.concatenate([high, high], axis=1)

    def smoothed(start, width):
        first, second = halves(columns_ref[:, start : start + width])
        both = jnp.concatenate([first, second], axis=0)
        return jnp.dot(twice, both, preferred_element_type=jnp.float32) + jnp.dot(
            rest, first, preferred_element_type=jnp.float32
        )

    for row in range(0, BPT, 2):
        done = smoothed(row * LANES, 2 * LANES)
        for i in range(2):
            cells = done[:, i * LANES : (i + 1) * LANES]
            out_ref[pl.ds(row + i, half, stride=PIECE), :] = cells[:half]
            out_ref[pl.ds(BPT + row + i, half, stride=PIECE), :] = cells[half:]
    done = smoothed(BPT * LANES, LANES)
    lower = lane_index((half, LANES)) < LANES // 2
    out_ref[pl.ds(2 * BPT, half, stride=PIECE), :] = jnp.where(lower, done[:half], done[half:])


def diffuse_kernel(
    cells_ref, factor_ref, scale_ref, side_scale_ref, near_ref, side_near_ref, out_hbm,
    main_a, main_b, side_a, side_b, coefficient_ref, edge_ref, out_ref, sems,
):
    shells, rows, _ = out_ref.shape
    nothing = jnp.zeros((TILE, LANES), jnp.float32)
    stripes = rows // BPT
    tiles = stripes // SIDES
    part = tiles * TILE
    for buffer in (main_a, main_b):
        for shell in range(shells):
            buffer[shell, 0:TILE, :] = nothing
            buffer[shell, TILE + rows : 2 * TILE + rows, :] = nothing
    slots = [(n, shell, (1 - shell) * SIDES + n) for n in range(SIDES) for shell in range(shells)]

    strip = lax.shift_right_logical(lane_index(), 4)
    for v in range(tiles):
        outer = nothing
        for n in range(SIDES):
            stripe = n * tiles + v
            at = stripe * PIECE
            spot = TILE + stripe * BPT
            wide = jnp.broadcast_to(cells_ref[at + 2 * BPT : at + PIECE, :], (TILE, LANES))
            turned = pltpu.roll(wide, STRIP * (n + 1), 1, stride=8, stride_axis=0)
            outer = jnp.where(lax.bitwise_and(strip, SIDES - 1) == n, turned, outer)
            for shell in range(shells):
                main_a[shell, spot : spot + BPT, :] = cells_ref[
                    at + shell * BPT : at + (shell + 1) * BPT, :
                ]
        side_a[TILE + v * TILE : 2 * TILE + v * TILE, :] = outer
    lane = lane_index((part, LANES))
    strip = lax.shift_right_logical(lane, 4)
    inner = lax.bitwise_and(lane, STRIP - 1) < 8

    lane_row = lane_index((1, LANES))
    stripe_in = lax.bitwise_and(lane_row, SIDES * STRIP - 1)
    last_row = TILE + part - 1

    def join(side):
        down = pltpu.roll(side[last_row : last_row + 1, :], STRIP, 1)
        side[TILE - 1 : TILE, :] = jnp.where(stripe_in < STRIP, 0.0, down)
        up = pltpu.roll(side[TILE : TILE + 1, :], LANES - STRIP, 1)
        side[last_row + 1 : last_row + 2, :] = jnp.where(stripe_in >= (SIDES - 1) * STRIP, 0.0, up)

    lane_tile = lane_index()
    factors = [jnp.tile(factor_ref[shell], (tiles, 1)) for shell in range(shells)]
    side_factor = jnp.tile(
        jnp.where(lane_tile < LANES // 2, factor_ref[1], factor_ref[0]), (tiles, 1)
    )
    is_edge = (lane == 0) | (lane == LANES - 1)

    def across(cells, matrix):
        return jnp.dot(
            jnp.concatenate(halves(cells), axis=1), matrix, preferred_element_type=jnp.float32
        )

    def side_step(side, side_next, sums):
        middle = side[TILE : TILE + part, :]
        vertical = side[TILE - 1 : TILE + part - 1, :] + side[TILE + 1 : TILE + part + 1, :]
        coefficient = side_factor * side_scale_ref[...]
        side_next[TILE : TILE + part, :] = middle + coefficient * (vertical + sums)
        join(side_next)

    copies = []
    buffers = ((main_a, side_a), (main_b, side_b))
    for repeat in range(PASSES):
        (main, side), (main_next, side_next) = buffers[repeat % 2], buffers[(repeat + 1) % 2]
        final = repeat == PASSES - 1
        if repeat == 0 or final:
            edge_ref[...] = across(side[TILE : TILE + part, :], side_near_ref[:, LANES:])
        else:
            sums = across(side[TILE : TILE + part, :], side_near_ref[...])
            edge_ref[...] = sums[:, LANES:]
            side_step(side, side_next, sums[:, :LANES])
        for n, shell, slot in slots:
            at = slice(n * part, (n + 1) * part)
            first = TILE + n * part
            middle = main[shell, first : first + part, :]
            sums = across(middle, near_ref[...])
            turned = pltpu.roll(edge_ref[...], (2 * LANES - STRIP * slot - 12) % LANES, 1)
            vertical = (
                main[shell, first - 1 : first + part - 1, :]
                + main[shell, first + 1 : first + part + 1, :]
            )
            if repeat == 0:
                coefficient = factors[shell] * scale_ref[1, at, :]
                coefficient_ref[shell, at, :] = coefficient
                side[TILE : TILE + part, :] = jnp.where(
                    inner & (strip == slot),
                    pltpu.roll(middle, STRIP * slot + 4, 1),
                    side[TILE : TILE + part, :],
                )
            else:
                coefficient = coefficient_ref[shell, at, :]
            new = middle + coefficient * ((vertical + sums) + jnp.where(is_edge, turned, 0.0))
            if not final:
                main_next[shell, first : first + part, :] = new
                continue
            out_ref[shell, at, :] = new
            if shell == shells - 1:
                done = pl.ds(n * part, part)
                copy = pltpu.make_async_copy(out_ref.at[:, done, :], out_hbm.at[:, done, :], sems.at[n])
                copy.start()
                copies.append(copy)
        if repeat == 0:
            join(side)
            side_step(
                side, side_next, across(side[TILE : TILE + part, :], side_near_ref[:, :LANES])
            )
    for copy in copies:
        copy.wait()


def in_hbm(array):
    return pltpu.with_memory_space_constraint(array, pltpu.HBM)


def per_device(partial_kernels, block_ids, radial_smoother, shell_level, lateral_scale):
    owners = lax.axis_size("ev")
    holders = lax.axis_size("sp")
    listed = block_ids.shape[1]
    rows, columns = lateral_scale.shape
    mine = shell_level.shape[0]
    part = rows // SIDES
    packed, scale, smoother, factor, near, side_near = pl.pallas_call(
        functools.partial(pack_kernel, owners),
        out_shape=[
            jax.ShapeDtypeStruct((owners * MESSAGE, LANES), jnp.float32),
            jax.ShapeDtypeStruct((3, rows, columns // owners), jnp.float32),
            jax.ShapeDtypeStruct((NR, NR), jnp.float32),
            jax.ShapeDtypeStruct((mine, TILE, LANES), jnp.float32),
            jax.ShapeDtypeStruct((2 * LANES, LANES), jnp.bfloat16),
            jax.ShapeDtypeStruct((2 * LANES, 2 * LANES), jnp.bfloat16),
        ],
        in_specs=[HBM] * 5,
        out_specs=[VMEM] * 6,
        scratch_shapes=[
            pltpu.SMEM((1, listed), jnp.int32),
            pltpu.VMEM((RB * listed, LANES), jnp.float32),
            pltpu.SMEM((mine,), jnp.int32),
            pltpu.SemaphoreType.DMA((7,)),
        ],
        compiler_params=SMALL,
    )(
        in_hbm(block_ids),
        in_hbm(partial_kernels.reshape(RB * listed, BY)),
        in_hbm(lateral_scale),
        in_hbm(radial_smoother),
        in_hbm(shell_level),
    )
    arrived = lax.all_to_all(
        packed.reshape(owners, MESSAGE, LANES), "ev", split_axis=0, concat_axis=0, tiled=True
    )
    pieces, side_scale = pl.pallas_call(
        functools.partial(smooth_kernel, owners),
        out_shape=[
            jax.ShapeDtypeStruct((holders * PIECE, LANES), jnp.float32),
            jax.ShapeDtypeStruct((part, LANES), jnp.float32),
        ],
        in_specs=[VMEM] * 3,
        out_specs=[VMEM] * 2,
        scratch_shapes=[
            pltpu.VMEM((3, owners, LANES), jnp.int32),
            pltpu.SMEM((3, owners, LANES), jnp.int32),
            pltpu.VMEM((NR, (BPT + 1) * LANES), jnp.float32),
            pltpu.VMEM((NR // 2, LANES), jnp.float32),
            pltpu.SemaphoreType.DMA((1,)),
        ],
        compiler_params=SMALL,
    )(arrived, scale, smoother)
    shells = lax.all_to_all(
        pieces.reshape(holders, 1, PIECE * LANES), "sp", split_axis=0, concat_axis=0, tiled=True
    ).reshape(holders * PIECE, LANES)
    padded = pltpu.VMEM((mine, rows + 2 * TILE, LANES), jnp.float32)
    plain = pltpu.VMEM((mine, rows, LANES), jnp.float32)
    side = pltpu.VMEM((part + 2 * TILE, LANES), jnp.float32)
    return pl.pallas_call(
        diffuse_kernel,
        out_shape=jax.ShapeDtypeStruct((mine, rows, columns // owners), jnp.float32),
        in_specs=[VMEM] * 6,
        out_specs=HBM,
        scratch_shapes=[
            padded,
            padded,
            side,
            side,
            plain,
            pltpu.VMEM((part, LANES), jnp.float32),
            plain,
            pltpu.SemaphoreType.DMA((SIDES,)),
        ],
        compiler_params=SMALL,
    )(shells, factor, scale, side_scale, near, side_near)


def solution(mesh):
    placed = (P("ev", None, "sp", None), P("ev", "sp"), P(), P("sp"), P())
    return jax.shard_map(
        per_device, mesh=mesh, in_specs=placed, out_specs=P("sp", None, "ev"), check_vma=False
    )
```

```python
import functools

import jax
import jax.numpy as jnp
from jax import lax
from jax.experimental import pallas as pl
from jax.experimental.pallas import tpu as pltpu
from jax.sharding import PartitionSpec as P

NR = 128
RB = 32
BY = 128
BPT = 8
CAP = 2
PASSES = 4
NSEG = 4
PER_OWNER = BPT * NSEG
LANES = 128
TILE = 8
MESSAGE = CAP * RB + TILE
LABELS = 64
STRIP = 16
SIDES = 4
PIECE = 2 * BPT + 1

diffusion_rate = 0.0615

SMALL = pltpu.CompilerParams(vmem_limit_bytes=12 * 1024 * 1024)
VMEM = pl.BlockSpec(memory_space=pltpu.VMEM)
HBM = pl.BlockSpec(memory_space=pltpu.HBM)


def lane_index(shape=(TILE, LANES)):
    return lax.broadcasted_iota(jnp.int32, shape, len(shape) - 1)


def stencil_matrices(near_ref, side_near_ref):
    row_of = lax.broadcasted_iota(jnp.int32, (LANES, LANES), 0)
    lane_of = lax.broadcasted_iota(jnp.int32, (LANES, LANES), 1)
    beside = jnp.abs(row_of - lane_of) == 1
    middle = jnp.where(row_of == lane_of, -4.0, 0.0)
    near = jnp.where(beside, 1.0, middle).astype(jnp.bfloat16)
    from_in, to_in = lax.bitwise_and(row_of, STRIP - 1), lax.bitwise_and(lane_of, STRIP - 1)
    same_strip = lax.shift_right_logical(row_of, 4) == lax.shift_right_logical(lane_of, 4)
    same_run = lax.shift_right_logical(row_of, 2) == lax.shift_right_logical(lane_of, 2)
    apart, later = jnp.abs(from_in - to_in), jnp.maximum(from_in, to_in)
    joined = ((apart == 7) & (later == 11)) | ((apart == 9) & (later == 12))
    side_near = jnp.where((beside & same_run) | (joined & same_strip), 1.0, middle).astype(jnp.bfloat16)
    exchanged = jnp.where(to_in == 11, lane_of + 1, jnp.where(to_in == 12, lane_of - 1, lane_of))
    exchange = jnp.where(row_of == exchanged, 1.0, 0.0).astype(jnp.bfloat16)
    for part in range(2):
        at = slice(part * LANES, (part + 1) * LANES)
        near_ref[at, :] = near
        side_near_ref[at, 0:LANES] = side_near
        side_near_ref[at, LANES:] = exchange


def pack_kernel(
    owners, ids_hbm, blocks_hbm, scale_hbm, smoother_hbm, level_hbm,
    out_ref, scale_ref, smoother_ref, factor_ref, near_ref, side_near_ref,
    ids_ref, blocks_ref, level_ref, sems,
):
    ids_copy = pltpu.make_async_copy(ids_hbm, ids_ref, sems.at[0])
    blocks_copy = pltpu.make_async_copy(blocks_hbm, blocks_ref, sems.at[1])
    ids_copy.start()
    blocks_copy.start()
    here = lax.axis_index("ev")
    width = scale_ref.shape[2]
    places = (jnp.maximum(here - 1, 0), here, jnp.minimum(here + 1, owners - 1))
    copies = [
        pltpu.make_async_copy(
            scale_hbm.at[:, pl.ds(pl.multiple_of(place * width, width), width)],
            scale_ref.at[n],
            sems.at[2 + n],
        )
        for n, place in enumerate(places)
    ]
    copies.append(pltpu.make_async_copy(smoother_hbm, smoother_ref, sems.at[5]))
    copies.append(pltpu.make_async_copy(level_hbm, level_ref, sems.at[6]))
    for copy in copies:
        copy.start()
    listed = ids_ref.shape[1]
    lane = lane_index()
    zero = jnp.zeros((TILE, LANES), jnp.float32)
    for row in range(0, owners * MESSAGE, TILE):
        out_ref[row : row + TILE, :] = zero
    stencil_matrices(near_ref, side_near_ref)
    ids_copy.wait()
    ids = [ids_ref[0, j] for j in range(listed)]
    owner_of = [lax.shift_right_logical(i, 5) for i in ids]
    ranks = []
    for j in range(listed):
        rank = jnp.int32(0)
        for i in range(j):
            rank = rank + jnp.where(owner_of[i] == owner_of[j], 1, 0)
        ranks.append(rank)
    blocks_copy.wait()

    def add(owner, cells):
        there = pl.ds(pl.multiple_of(owner * MESSAGE + CAP * RB, TILE), TILE)
        out_ref[there, :] = out_ref[there, :] + cells

    for j in range(listed):
        owner, rank = owner_of[j], ranks[j]
        within = lax.bitwise_and(ids[j], PER_OWNER - 1).astype(jnp.float32)
        first = zero
        last = zero
        for a in range(RB // TILE):
            cells = blocks_ref[pl.ds(a * TILE * listed + j, TILE, stride=listed), :]
            start = pl.multiple_of(owner * MESSAGE + rank * RB + a * TILE, TILE)
            out_ref[pl.ds(start, TILE), :] = cells
            head = jnp.where(lane < 4, cells, 0.0)
            tail = jnp.where(lane >= LANES - 4, cells, 0.0)
            first = first + (pltpu.roll(head, 16 * a, 1) if a else head)
            last = last + pltpu.roll(tail, 16 * a + 4, 1)
        add(owner, jnp.where(lane == LABELS + rank, within, 0.0))
        later = rank == 1
        to_left = jnp.where(later, pltpu.roll(first, 12, 1), pltpu.roll(first, 8, 1))
        to_left = to_left + jnp.where(lane == LABELS + 4 + rank, within, 0.0)
        to_right = jnp.where(later, pltpu.roll(last, 4, 1), last)
        to_right = to_right + jnp.where(lane == LABELS + 2 + rank, within, 0.0)
        add(jnp.maximum(owner - 1, 0), jnp.where(owner > 0, to_left, 0.0))
        add(jnp.minimum(owner + 1, owners - 1), jnp.where(owner < owners - 1, to_right, 0.0))
    for copy in copies:
        copy.wait()
    for shell in range(level_ref.shape[0]):
        factor = diffusion_rate * level_ref[shell].astype(jnp.float32)
        factor_ref[shell] = jnp.full((TILE, LANES), factor, jnp.float32)


def halves(cells):
    high = cells.astype(jnp.bfloat16)
    low = (cells - high.astype(jnp.float32)).astype(jnp.bfloat16)
    return high, low


def scale_strips(scale_ref, owners):
    here = lax.axis_index("ev")
    part = scale_ref.shape[1] // SIDES
    lane = lane_index((part, LANES))
    inner = lax.bitwise_and(lane, STRIP - 1) < 8
    strip = lax.shift_right_logical(lane, 4)
    keep_after = (lane < 4) & (here < owners - 1)
    keep_before = (lane >= LANES - 4) & (here > 0)
    strips = jnp.zeros((part, LANES), jnp.float32)
    for n in range(SIDES):
        at = slice(n * part, (n + 1) * part)
        beyond = jnp.where(keep_before, scale_ref[0, at, :], 0.0)
        beyond = jnp.where(keep_after, scale_ref[2, at, :], beyond)
        both = jnp.where(
            inner,
            pltpu.roll(scale_ref[1, at, :], STRIP * n + 4, 1),
            pltpu.roll(beyond, STRIP * n + 12, 1),
        )
        strips = jnp.where(strip == n, both, strips)
    return strips + pltpu.roll(strips, LANES // 2, 1)


def smooth_kernel(
    groups, arrived_ref, scale_ref, smoother_ref, out_ref, side_scale_ref,
    columns_ref, edge_ref,
):
    labels = arrived_ref[:, CAP * RB, :].astype(jnp.int32)
    spots = [
        [labels[g : g + 1, LABELS + i : LABELS + i + 1][0, 0] for i in range(3 * CAP)]
        for g in range(groups)
    ]
    rows = [[lax.shift_right_logical(spot, 2) for spot in group] for group in spots]
    segments = [[lax.bitwise_and(spot, NSEG - 1) for spot in group] for group in spots]
    lane = lane_index()
    low = lane < LANES // 2
    lane_four = lax.bitwise_and(lane, LANES // 2 - 4)
    columns_ref[:, : BPT * LANES] = jnp.zeros((NR, BPT * LANES), jnp.float32)
    edge_ref[...] = jnp.zeros_like(edge_ref)
    side_scale_ref[...] = scale_strips(scale_ref, groups)
    for g in range(groups):
        for rank in range(CAP):
            where = (
                pl.ds(pl.multiple_of(segments[g][rank] * RB, RB), RB),
                pl.ds(pl.multiple_of(rows[g][rank] * LANES, LANES), LANES),
            )
            columns_ref[where] = columns_ref[where] + arrived_ref[g, rank * RB : (rank + 1) * RB, :]
    for g in range(groups):
        edges = arrived_ref[g, CAP * RB :, :]
        pairs = [
            jnp.where(low, edges, pltpu.roll(edges, 48, 1)),
            jnp.where(low, pltpu.roll(edges, LANES - 32, 1), pltpu.roll(edges, 16, 1)),
        ]
        for h in range(2 * CAP):
            target = (BPT - 1 - rows[g][CAP + h]) * 8 + (4 if h >= CAP else 0)
            keep = lane_four == target
            shift = lax.bitwise_and(target + (LANES - 4 * h), LANES - 1)
            four = jnp.concatenate(
                [jnp.where(keep, pltpu.roll(pair, shift, 1), 0.0) for pair in pairs], axis=0
            )
            where = pl.ds(pl.multiple_of(segments[g][CAP + h] * (2 * TILE), 2 * TILE), 2 * TILE)
            edge_ref[where, :] = edge_ref[where, :] + four
    for pair in range(NR // (2 * TILE)):
        cells = edge_ref[pair * TILE : (pair + 1) * TILE, :]
        turned = pltpu.roll(cells, LANES // 2, 1)
        at = pair * 2 * TILE
        columns_ref[at : at + TILE, BPT * LANES :] = jnp.where(low, cells, turned)
        columns_ref[at + TILE : at + 2 * TILE, BPT * LANES :] = jnp.where(low, turned, cells)
    half = NR // 2
    smoother = jnp.concatenate(
        [smoother_ref[pl.ds(0, half, stride=2), :], smoother_ref[pl.ds(1, half, stride=2), :]], axis=0
    )
    high, rest = halves(smoother)
    twice = jnp.concatenate([high, high], axis=1)

    def smoothed(start, width):
        first, second = halves(columns_ref[:, start : start + width])
        both = jnp.concatenate([first, second], axis=0)
        return jnp.dot(twice, both, preferred_element_type=jnp.float32) + jnp.dot(
            rest, first, preferred_element_type=jnp.float32
        )

    for row in range(0, BPT, 2):
        done = smoothed(row * LANES, 2 * LANES)
        for i in range(2):
            cells = done[:, i * LANES : (i + 1) * LANES]
            out_ref[pl.ds(row + i, half, stride=PIECE), :] = cells[:half]
            out_ref[pl.ds(BPT + row + i, half, stride=PIECE), :] = cells[half:]
    done = smoothed(BPT * LANES, LANES)
    lower = lane_index((half, LANES)) < LANES // 2
    out_ref[pl.ds(2 * BPT, half, stride=PIECE), :] = jnp.where(lower, done[:half], done[half:])


def diffuse_kernel(
    cells_ref, factor_ref, scale_ref, side_scale_ref, near_ref, side_near_ref, out_hbm,
    main_a, main_b, side_a, side_b, coefficient_ref, edge_ref, out_ref, sems,
):
    shells, rows, _ = out_ref.shape
    nothing = jnp.zeros((TILE, LANES), jnp.float32)
    stripes = rows // BPT
    tiles = stripes // SIDES
    part = tiles * TILE
    for buffer in (main_a, main_b):
        for shell in range(shells):
            buffer[shell, 0:TILE, :] = nothing
            buffer[shell, TILE + rows : 2 * TILE + rows, :] = nothing
    slots = [(n, shell, (1 - shell) * SIDES + n) for n in range(SIDES) for shell in range(shells)]

    strip = lax.shift_right_logical(lane_index(), 4)
    for v in range(tiles):
        outer = nothing
        for n in range(SIDES):
            stripe = n * tiles + v
            at = stripe * PIECE
            spot = TILE + stripe * BPT
            wide = jnp.broadcast_to(cells_ref[at + 2 * BPT : at + PIECE, :], (TILE, LANES))
            turned = pltpu.roll(wide, STRIP * (n + 1), 1, stride=8, stride_axis=0)
            outer = jnp.where(lax.bitwise_and(strip, SIDES - 1) == n, turned, outer)
            for shell in range(shells):
                main_a[shell, spot : spot + BPT, :] = cells_ref[
                    at + shell * BPT : at + (shell + 1) * BPT, :
                ]
        side_a[TILE + v * TILE : 2 * TILE + v * TILE, :] = outer
    lane = lane_index((part, LANES))
    strip = lax.shift_right_logical(lane, 4)
    inner = lax.bitwise_and(lane, STRIP - 1) < 8

    lane_row = lane_index((1, LANES))
    stripe_in = lax.bitwise_and(lane_row, SIDES * STRIP - 1)
    last_row = TILE + part - 1

    def join(side):
        down = pltpu.roll(side[last_row : last_row + 1, :], STRIP, 1)
        side[TILE - 1 : TILE, :] = jnp.where(stripe_in < STRIP, 0.0, down)
        up = pltpu.roll(side[TILE : TILE + 1, :], LANES - STRIP, 1)
        side[last_row + 1 : last_row + 2, :] = jnp.where(stripe_in >= (SIDES - 1) * STRIP, 0.0, up)

    lane_tile = lane_index()
    factors = [jnp.tile(factor_ref[shell], (tiles, 1)) for shell in range(shells)]
    side_factor = jnp.tile(
        jnp.where(lane_tile < LANES // 2, factor_ref[1], factor_ref[0]), (tiles, 1)
    )
    is_edge = (lane == 0) | (lane == LANES - 1)

    def across(cells, matrix):
        return jnp.dot(
            jnp.concatenate(halves(cells), axis=1), matrix, preferred_element_type=jnp.float32
        )

    def side_step(side, side_next, sums):
        middle = side[TILE : TILE + part, :]
        vertical = side[TILE - 1 : TILE + part - 1, :] + side[TILE + 1 : TILE + part + 1, :]
        coefficient = side_factor * side_scale_ref[...]
        side_next[TILE : TILE + part, :] = middle + coefficient * (vertical + sums)
        join(side_next)

    copies = []
    buffers = ((main_a, side_a), (main_b, side_b))
    for repeat in range(PASSES):
        (main, side), (main_next, side_next) = buffers[repeat % 2], buffers[(repeat + 1) % 2]
        final = repeat == PASSES - 1
        if repeat == 0 or final:
            edge_ref[...] = across(side[TILE : TILE + part, :], side_near_ref[:, LANES:])
        else:
            sums = across(side[TILE : TILE + part, :], side_near_ref[...])
            edge_ref[...] = sums[:, LANES:]
            side_step(side, side_next, sums[:, :LANES])
        for n, shell, slot in slots:
            at = slice(n * part, (n + 1) * part)
            first = TILE + n * part
            middle = main[shell, first : first + part, :]
            sums = across(middle, near_ref[...])
            turned = pltpu.roll(edge_ref[...], (2 * LANES - STRIP * slot - 12) % LANES, 1)
            vertical = (
                main[shell, first - 1 : first + part - 1, :]
                + main[shell, first + 1 : first + part + 1, :]
            )
            if repeat == 0:
                coefficient = factors[shell] * scale_ref[1, at, :]
                coefficient_ref[shell, at, :] = coefficient
                side[TILE : TILE + part, :] = jnp.where(
                    inner & (strip == slot),
                    pltpu.roll(middle, STRIP * slot + 4, 1),
                    side[TILE : TILE + part, :],
                )
            else:
                coefficient = coefficient_ref[shell, at, :]
            new = middle + coefficient * ((vertical + sums) + jnp.where(is_edge, turned, 0.0))
            if not final:
                main_next[shell, first : first + part, :] = new
                continue
            out_ref[shell, at, :] = new
            if shell == shells - 1:
                done = pl.ds(n * part, part)
                copy = pltpu.make_async_copy(out_ref.at[:, done, :], out_hbm.at[:, done, :], sems.at[n])
                copy.start()
                copies.append(copy)
        if repeat == 0:
            join(side)
            side_step(
                side, side_next, across(side[TILE : TILE + part, :], side_near_ref[:, :LANES])
            )
    for copy in copies:
        copy.wait()


def in_hbm(array):
    return pltpu.with_memory_space_constraint(array, pltpu.HBM)


def per_device(partial_kernels, block_ids, radial_smoother, shell_level, lateral_scale):
    owners = lax.axis_size("ev")
    holders = lax.axis_size("sp")
    listed = block_ids.shape[1]
    rows, columns = lateral_scale.shape
    mine = shell_level.shape[0]
    part = rows // SIDES
    packed, scale, smoother, factor, near, side_near = pl.pallas_call(
        functools.partial(pack_kernel, owners),
        out_shape=[
            jax.ShapeDtypeStruct((owners * MESSAGE, LANES), jnp.float32),
            jax.ShapeDtypeStruct((3, rows, columns // owners), jnp.float32),
            jax.ShapeDtypeStruct((NR, NR), jnp.float32),
            jax.ShapeDtypeStruct((mine, TILE, LANES), jnp.float32),
            jax.ShapeDtypeStruct((2 * LANES, LANES), jnp.bfloat16),
            jax.ShapeDtypeStruct((2 * LANES, 2 * LANES), jnp.bfloat16),
        ],
        in_specs=[HBM] * 5,
        out_specs=[VMEM] * 6,
        scratch_shapes=[
            pltpu.SMEM((1, listed), jnp.int32),
            pltpu.VMEM((RB * listed, LANES), jnp.float32),
            pltpu.SMEM((mine,), jnp.int32),
            pltpu.SemaphoreType.DMA((7,)),
        ],
        compiler_params=SMALL,
    )(
        in_hbm(block_ids),
        in_hbm(partial_kernels.reshape(RB * listed, BY)),
        in_hbm(lateral_scale),
        in_hbm(radial_smoother),
        in_hbm(shell_level),
    )
    arrived = lax.all_to_all(
        packed.reshape(owners, MESSAGE, LANES), "ev", split_axis=0, concat_axis=0, tiled=True
    )
    pieces, side_scale = pl.pallas_call(
        functools.partial(smooth_kernel, owners),
        out_shape=[
            jax.ShapeDtypeStruct((holders * PIECE, LANES), jnp.float32),
            jax.ShapeDtypeStruct((part, LANES), jnp.float32),
        ],
        in_specs=[VMEM] * 3,
        out_specs=[VMEM] * 2,
        scratch_shapes=[
            pltpu.VMEM((NR, (BPT + 1) * LANES), jnp.float32),
            pltpu.VMEM((NR // 2, LANES), jnp.float32),
        ],
        compiler_params=SMALL,
    )(arrived, scale, smoother)
    shells = lax.all_to_all(
        pieces.reshape(holders, 1, PIECE * LANES), "sp", split_axis=0, concat_axis=0, tiled=True
    ).reshape(holders * PIECE, LANES)
    padded = pltpu.VMEM((mine, rows + 2 * TILE, LANES), jnp.float32)
    plain = pltpu.VMEM((mine, rows, LANES), jnp.float32)
    side = pltpu.VMEM((part + 2 * TILE, LANES), jnp.float32)
    return pl.pallas_call(
        diffuse_kernel,
        out_shape=jax.ShapeDtypeStruct((mine, rows, columns // owners), jnp.float32),
        in_specs=[VMEM] * 6,
        out_specs=HBM,
        scratch_shapes=[
            padded,
            padded,
            side,
            side,
            plain,
            pltpu.VMEM((part, LANES), jnp.float32),
            plain,
            pltpu.SemaphoreType.DMA((SIDES,)),
        ],
        compiler_params=SMALL,
    )(shells, factor, scale, side_scale, near, side_near)


def solution(mesh):
    placed = (P("ev", None, "sp", None), P("ev", "sp"), P(), P("sp"), P())
    return jax.shard_map(
        per_device, mesh=mesh, in_specs=placed, out_specs=P("sp", None, "ev"), check_vma=False
    )
```

```python
import functools

import jax
import jax.numpy as jnp
from jax import lax
from jax.experimental import pallas as pl
from jax.experimental.pallas import tpu as pltpu
from jax.sharding import PartitionSpec as P

NR = 128
RB = 32
BY = 128
BPT = 8
CAP = 2
PASSES = 4
NSEG = 4
PER_OWNER = BPT * NSEG
LANES = 128
TILE = 8
MESSAGE = CAP * RB + TILE
LABELS = 64
STRIP = 16
SIDES = 4
PIECE = 2 * BPT + 1

diffusion_rate = 0.0615

SMALL = pltpu.CompilerParams(vmem_limit_bytes=12 * 1024 * 1024)
PACKED = pltpu.CompilerParams(
    vmem_limit_bytes=12 * 1024 * 1024
)
VMEM = pl.BlockSpec(memory_space=pltpu.VMEM)
HBM = pl.BlockSpec(memory_space=pltpu.HBM)


def lane_index(shape=(TILE, LANES)):
    return lax.broadcasted_iota(jnp.int32, shape, len(shape) - 1)


def stencil_matrices(near_ref, side_near_ref):
    row_of = lax.broadcasted_iota(jnp.int32, (LANES, LANES), 0)
    lane_of = lax.broadcasted_iota(jnp.int32, (LANES, LANES), 1)
    beside = jnp.abs(row_of - lane_of) == 1
    middle = jnp.where(row_of == lane_of, -4.0, 0.0)
    near = jnp.where(beside, 1.0, middle).astype(jnp.bfloat16)
    from_in, to_in = lax.bitwise_and(row_of, STRIP - 1), lax.bitwise_and(lane_of, STRIP - 1)
    same_strip = lax.shift_right_logical(row_of, 4) == lax.shift_right_logical(lane_of, 4)
    same_run = lax.shift_right_logical(row_of, 2) == lax.shift_right_logical(lane_of, 2)
    apart, later = jnp.abs(from_in - to_in), jnp.maximum(from_in, to_in)
    joined = ((apart == 7) & (later == 11)) | ((apart == 9) & (later == 12))
    side_near = jnp.where((beside & same_run) | (joined & same_strip), 1.0, middle).astype(jnp.bfloat16)
    exchanged = jnp.where(to_in == 11, lane_of + 1, jnp.where(to_in == 12, lane_of - 1, lane_of))
    exchange = jnp.where(row_of == exchanged, 1.0, 0.0).astype(jnp.bfloat16)
    for part in range(2):
        at = slice(part * LANES, (part + 1) * LANES)
        near_ref[at, :] = near
        side_near_ref[at, 0:LANES] = side_near
        side_near_ref[at, LANES:] = exchange


def pack_kernel(
    owners, ids_hbm, blocks_hbm, scale_hbm, smoother_hbm, level_hbm,
    out_ref, scale_ref, smoother_ref, factor_ref, near_ref, side_near_ref,
    ids_ref, blocks_ref, level_ref, sems,
):
    ids_copy = pltpu.make_async_copy(ids_hbm, ids_ref, sems.at[0])
    blocks_copy = pltpu.make_async_copy(blocks_hbm, blocks_ref, sems.at[1])
    ids_copy.start()
    blocks_copy.start()
    here = lax.axis_index("ev")
    width = scale_ref.shape[2]
    places = (jnp.maximum(here - 1, 0), here, jnp.minimum(here + 1, owners - 1))
    copies = [
        pltpu.make_async_copy(
            scale_hbm.at[:, pl.ds(pl.multiple_of(place * width, width), width)],
            scale_ref.at[n],
            sems.at[2 + n],
        )
        for n, place in enumerate(places)
    ]
    copies.append(pltpu.make_async_copy(smoother_hbm, smoother_ref, sems.at[5]))
    copies.append(pltpu.make_async_copy(level_hbm, level_ref, sems.at[6]))
    for copy in copies:
        copy.start()
    listed = ids_ref.shape[1]
    lane = lane_index()
    zero = jnp.zeros((TILE, LANES), jnp.float32)
    for row in range(0, owners * MESSAGE, TILE):
        out_ref[row : row + TILE, :] = zero
    stencil_matrices(near_ref, side_near_ref)
    ids_copy.wait()
    ids = [ids_ref[0, j] for j in range(listed)]
    owner_of = [lax.shift_right_logical(i, 5) for i in ids]
    ranks = []
    for j in range(listed):
        rank = jnp.int32(0)
        for i in range(j):
            rank = rank + jnp.where(owner_of[i] == owner_of[j], 1, 0)
        ranks.append(rank)
    blocks_copy.wait()

    def add(owner, cells):
        there = pl.ds(pl.multiple_of(owner * MESSAGE + CAP * RB, TILE), TILE)
        out_ref[there, :] = out_ref[there, :] + cells

    for j in range(listed):
        owner, rank = owner_of[j], ranks[j]
        within = lax.bitwise_and(ids[j], PER_OWNER - 1).astype(jnp.float32)
        first = zero
        last = zero
        for a in range(RB // TILE):
            cells = blocks_ref[pl.ds(a * TILE * listed + j, TILE, stride=listed), :]
            start = pl.multiple_of(owner * MESSAGE + rank * RB + a * TILE, TILE)
            out_ref[pl.ds(start, TILE), :] = cells
            head = jnp.where(lane < 4, cells, 0.0)
            tail = jnp.where(lane >= LANES - 4, cells, 0.0)
            first = first + (pltpu.roll(head, 16 * a, 1) if a else head)
            last = last + pltpu.roll(tail, 16 * a + 4, 1)
        add(owner, jnp.where(lane == LABELS + rank, within, 0.0))
        later = rank == 1
        to_left = jnp.where(later, pltpu.roll(first, 12, 1), pltpu.roll(first, 8, 1))
        to_left = to_left + jnp.where(lane == LABELS + 4 + rank, within, 0.0)
        to_right = jnp.where(later, pltpu.roll(last, 4, 1), last)
        to_right = to_right + jnp.where(lane == LABELS + 2 + rank, within, 0.0)
        add(jnp.maximum(owner - 1, 0), jnp.where(owner > 0, to_left, 0.0))
        add(jnp.minimum(owner + 1, owners - 1), jnp.where(owner < owners - 1, to_right, 0.0))
    for copy in copies:
        copy.wait()
    for shell in range(level_ref.shape[0]):
        factor = diffusion_rate * level_ref[shell].astype(jnp.float32)
        factor_ref[shell] = jnp.full((TILE, LANES), factor, jnp.float32)


def halves(cells):
    high = cells.astype(jnp.bfloat16)
    low = (cells - high.astype(jnp.float32)).astype(jnp.bfloat16)
    return high, low


def scale_strips(scale_ref, owners):
    here = lax.axis_index("ev")
    part = scale_ref.shape[1] // SIDES
    lane = lane_index((part, LANES))
    inner = lax.bitwise_and(lane, STRIP - 1) < 8
    strip = lax.shift_right_logical(lane, 4)
    keep_after = (lane < 4) & (here < owners - 1)
    keep_before = (lane >= LANES - 4) & (here > 0)
    strips = jnp.zeros((part, LANES), jnp.float32)
    for n in range(SIDES):
        at = slice(n * part, (n + 1) * part)
        beyond = jnp.where(keep_before, scale_ref[0, at, :], 0.0)
        beyond = jnp.where(keep_after, scale_ref[2, at, :], beyond)
        both = jnp.where(
            inner,
            pltpu.roll(scale_ref[1, at, :], STRIP * n + 4, 1),
            pltpu.roll(beyond, STRIP * n + 12, 1),
        )
        strips = jnp.where(strip == n, both, strips)
    return strips + pltpu.roll(strips, LANES // 2, 1)


def smooth_kernel(
    groups, arrived_ref, scale_ref, smoother_ref, out_ref, side_scale_ref,
    columns_ref, edge_ref,
):
    labels = arrived_ref[:, CAP * RB, :].astype(jnp.int32)
    spots = [
        [labels[g : g + 1, LABELS + i : LABELS + i + 1][0, 0] for i in range(3 * CAP)]
        for g in range(groups)
    ]
    rows = [[lax.shift_right_logical(spot, 2) for spot in group] for group in spots]
    segments = [[lax.bitwise_and(spot, NSEG - 1) for spot in group] for group in spots]
    lane = lane_index()
    low = lane < LANES // 2
    lane_four = lax.bitwise_and(lane, LANES // 2 - 4)
    columns_ref[:, : BPT * LANES] = jnp.zeros((NR, BPT * LANES), jnp.float32)
    edge_ref[...] = jnp.zeros_like(edge_ref)
    side_scale_ref[...] = scale_strips(scale_ref, groups)
    for g in range(groups):
        for rank in range(CAP):
            where = (
                pl.ds(pl.multiple_of(segments[g][rank] * RB, RB), RB),
                pl.ds(pl.multiple_of(rows[g][rank] * LANES, LANES), LANES),
            )
            columns_ref[where] = columns_ref[where] + arrived_ref[g, rank * RB : (rank + 1) * RB, :]
    for g in range(groups):
        edges = arrived_ref[g, CAP * RB :, :]
        pairs = [
            jnp.where(low, edges, pltpu.roll(edges, 48, 1)),
            jnp.where(low, pltpu.roll(edges, LANES - 32, 1), pltpu.roll(edges, 16, 1)),
        ]
        for h in range(2 * CAP):
            target = (BPT - 1 - rows[g][CAP + h]) * 8 + (4 if h >= CAP else 0)
            keep = lane_four == target
            shift = lax.bitwise_and(target + (LANES - 4 * h), LANES - 1)
            four = jnp.concatenate(
                [jnp.where(keep, pltpu.roll(pair, shift, 1), 0.0) for pair in pairs], axis=0
            )
            where = pl.ds(pl.multiple_of(segments[g][CAP + h] * (2 * TILE), 2 * TILE), 2 * TILE)
            edge_ref[where, :] = edge_ref[where, :] + four
    for pair in range(NR // (2 * TILE)):
        cells = edge_ref[pair * TILE : (pair + 1) * TILE, :]
        turned = pltpu.roll(cells, LANES // 2, 1)
        at = pair * 2 * TILE
        columns_ref[at : at + TILE, BPT * LANES :] = jnp.where(low, cells, turned)
        columns_ref[at + TILE : at + 2 * TILE, BPT * LANES :] = jnp.where(low, turned, cells)
    half = NR // 2
    smoother = jnp.concatenate(
        [smoother_ref[pl.ds(0, half, stride=2), :], smoother_ref[pl.ds(1, half, stride=2), :]], axis=0
    )
    high, rest = halves(smoother)
    twice = jnp.concatenate([high, high], axis=1)

    def smoothed(start, width):
        first, second = halves(columns_ref[:, start : start + width])
        both = jnp.concatenate([first, second], axis=0)
        return jnp.dot(twice, both, preferred_element_type=jnp.float32) + jnp.dot(
            rest, first, preferred_element_type=jnp.float32
        )

    for row in range(0, BPT, 2):
        done = smoothed(row * LANES, 2 * LANES)
        for i in range(2):
            cells = done[:, i * LANES : (i + 1) * LANES]
            out_ref[pl.ds(row + i, half, stride=PIECE), :] = cells[:half]
            out_ref[pl.ds(BPT + row + i, half, stride=PIECE), :] = cells[half:]
    done = smoothed(BPT * LANES, LANES)
    lower = lane_index((half, LANES)) < LANES // 2
    out_ref[pl.ds(2 * BPT, half, stride=PIECE), :] = jnp.where(lower, done[:half], done[half:])


def diffuse_kernel(
    cells_ref, factor_ref, scale_ref, side_scale_ref, near_ref, side_near_ref, out_hbm,
    main_a, main_b, side_a, side_b, coefficient_ref, edge_ref, out_ref, sems,
):
    shells, rows, _ = out_ref.shape
    nothing = jnp.zeros((TILE, LANES), jnp.float32)
    stripes = rows // BPT
    tiles = stripes // SIDES
    part = tiles * TILE
    for buffer in (main_a, main_b):
        for shell in range(shells):
            buffer[shell, 0:TILE, :] = nothing
            buffer[shell, TILE + rows : 2 * TILE + rows, :] = nothing
    slots = [(n, shell, (1 - shell) * SIDES + n) for n in range(SIDES) for shell in range(shells)]

    strip = lax.shift_right_logical(lane_index(), 4)
    for v in range(tiles):
        outer = nothing
        for n in range(SIDES):
            stripe = n * tiles + v
            at = stripe * PIECE
            spot = TILE + stripe * BPT
            wide = jnp.broadcast_to(cells_ref[at + 2 * BPT : at + PIECE, :], (TILE, LANES))
            turned = pltpu.roll(wide, STRIP * (n + 1), 1, stride=8, stride_axis=0)
            outer = jnp.where(lax.bitwise_and(strip, SIDES - 1) == n, turned, outer)
            for shell in range(shells):
                main_a[shell, spot : spot + BPT, :] = cells_ref[
                    at + shell * BPT : at + (shell + 1) * BPT, :
                ]
        side_a[TILE + v * TILE : 2 * TILE + v * TILE, :] = outer
    lane = lane_index((part, LANES))
    strip = lax.shift_right_logical(lane, 4)
    inner = lax.bitwise_and(lane, STRIP - 1) < 8

    lane_row = lane_index((1, LANES))
    stripe_in = lax.bitwise_and(lane_row, SIDES * STRIP - 1)
    last_row = TILE + part - 1

    def join(side):
        down = pltpu.roll(side[last_row : last_row + 1, :], STRIP, 1)
        side[TILE - 1 : TILE, :] = jnp.where(stripe_in < STRIP, 0.0, down)
        up = pltpu.roll(side[TILE : TILE + 1, :], LANES - STRIP, 1)
        side[last_row + 1 : last_row + 2, :] = jnp.where(stripe_in >= (SIDES - 1) * STRIP, 0.0, up)

    lane_tile = lane_index()
    factors = [jnp.tile(factor_ref[shell], (tiles, 1)) for shell in range(shells)]
    side_factor = jnp.tile(
        jnp.where(lane_tile < LANES // 2, factor_ref[1], factor_ref[0]), (tiles, 1)
    )
    is_edge = (lane == 0) | (lane == LANES - 1)

    def across(cells, matrix):
        return jnp.dot(
            jnp.concatenate(halves(cells), axis=1), matrix, preferred_element_type=jnp.float32
        )

    def side_step(side, side_next, sums):
        middle = side[TILE : TILE + part, :]
        vertical = side[TILE - 1 : TILE + part - 1, :] + side[TILE + 1 : TILE + part + 1, :]
        coefficient = side_factor * side_scale_ref[...]
        side_next[TILE : TILE + part, :] = middle + coefficient * (vertical + sums)
        join(side_next)

    buffers = ((main_a, side_a), (main_b, side_b))
    for repeat in range(PASSES):
        (main, side), (main_next, side_next) = buffers[repeat % 2], buffers[(repeat + 1) % 2]
        final = repeat == PASSES - 1
        if repeat == 0 or final:
            edge_ref[...] = across(side[TILE : TILE + part, :], side_near_ref[:, LANES:])
        else:
            sums = across(side[TILE : TILE + part, :], side_near_ref[...])
            edge_ref[...] = sums[:, LANES:]
            side_step(side, side_next, sums[:, :LANES])
        for n, shell, slot in slots:
            at = slice(n * part, (n + 1) * part)
            first = TILE + n * part
            middle = main[shell, first : first + part, :]
            sums = across(middle, near_ref[...])
            turned = pltpu.roll(edge_ref[...], (2 * LANES - STRIP * slot - 12) % LANES, 1)
            vertical = (
                main[shell, first - 1 : first + part - 1, :]
                + main[shell, first + 1 : first + part + 1, :]
            )
            if repeat == 0:
                coefficient = factors[shell] * scale_ref[1, at, :]
                coefficient_ref[shell, at, :] = coefficient
                side[TILE : TILE + part, :] = jnp.where(
                    inner & (strip == slot),
                    pltpu.roll(middle, STRIP * slot + 4, 1),
                    side[TILE : TILE + part, :],
                )
            else:
                coefficient = coefficient_ref[shell, at, :]
            new = middle + coefficient * ((vertical + sums) + jnp.where(is_edge, turned, 0.0))
            if final:
                out_ref[shell, at, :] = new
            else:
                main_next[shell, first : first + part, :] = new
        if repeat == 0:
            join(side)
            side_step(
                side, side_next, across(side[TILE : TILE + part, :], side_near_ref[:, :LANES])
            )
    out_copy = pltpu.make_async_copy(out_ref, out_hbm, sems.at[0])
    out_copy.start()
    out_copy.wait()


def in_hbm(array):
    return pltpu.with_memory_space_constraint(array, pltpu.HBM)


def per_device(partial_kernels, block_ids, radial_smoother, shell_level, lateral_scale):
    owners = lax.axis_size("ev")
    holders = lax.axis_size("sp")
    listed = block_ids.shape[1]
    rows, columns = lateral_scale.shape
    mine = shell_level.shape[0]
    part = rows // SIDES
    packed, scale, smoother, factor, near, side_near = pl.pallas_call(
        functools.partial(pack_kernel, owners),
        out_shape=[
            jax.ShapeDtypeStruct((owners * MESSAGE, LANES), jnp.float32),
            jax.ShapeDtypeStruct((3, rows, columns // owners), jnp.float32),
            jax.ShapeDtypeStruct((NR, NR), jnp.float32),
            jax.ShapeDtypeStruct((mine, TILE, LANES), jnp.float32),
            jax.ShapeDtypeStruct((2 * LANES, LANES), jnp.bfloat16),
            jax.ShapeDtypeStruct((2 * LANES, 2 * LANES), jnp.bfloat16),
        ],
        in_specs=[HBM] * 5,
        out_specs=[VMEM] * 6,
        scratch_shapes=[
            pltpu.SMEM((1, listed), jnp.int32),
            pltpu.VMEM((RB * listed, LANES), jnp.float32),
            pltpu.SMEM((mine,), jnp.int32),
            pltpu.SemaphoreType.DMA((7,)),
        ],
        compiler_params=SMALL,
    )(
        in_hbm(block_ids),
        in_hbm(partial_kernels.reshape(RB * listed, BY)),
        in_hbm(lateral_scale),
        in_hbm(radial_smoother),
        in_hbm(shell_level),
    )
    arrived = lax.all_to_all(
        packed.reshape(owners, MESSAGE, LANES), "ev", split_axis=0, concat_axis=0, tiled=True
    )
    pieces, side_scale = pl.pallas_call(
        functools.partial(smooth_kernel, owners),
        out_shape=[
            jax.ShapeDtypeStruct((holders * PIECE, LANES), jnp.float32),
            jax.ShapeDtypeStruct((part, LANES), jnp.float32),
        ],
        in_specs=[VMEM] * 3,
        out_specs=[VMEM] * 2,
        scratch_shapes=[
            pltpu.VMEM((NR, (BPT + 1) * LANES), jnp.float32),
            pltpu.VMEM((NR // 2, LANES), jnp.float32),
        ],
        compiler_params=PACKED,
    )(arrived, scale, smoother)
    shells = lax.all_to_all(
        pieces.reshape(holders, 1, PIECE * LANES), "sp", split_axis=0, concat_axis=0, tiled=True
    ).reshape(holders * PIECE, LANES)
    padded = pltpu.VMEM((mine, rows + 2 * TILE, LANES), jnp.float32)
    plain = pltpu.VMEM((mine, rows, LANES), jnp.float32)
    side = pltpu.VMEM((part + 2 * TILE, LANES), jnp.float32)
    return pl.pallas_call(
        diffuse_kernel,
        out_shape=jax.ShapeDtypeStruct((mine, rows, columns // owners), jnp.float32),
        in_specs=[VMEM] * 6,
        out_specs=HBM,
        scratch_shapes=[
            padded,
            padded,
            side,
            side,
            plain,
            pltpu.VMEM((part, LANES), jnp.float32),
            plain,
            pltpu.SemaphoreType.DMA((1,)),
        ],
        compiler_params=SMALL,
    )(shells, factor, scale, side_scale, near, side_near)


def solution(mesh):
    placed = (P("ev", None, "sp", None), P("ev", "sp"), P(), P("sp"), P())
    return jax.shard_map(
        per_device, mesh=mesh, in_specs=placed, out_specs=P("sp", None, "ev"), check_vma=False
    )
```

```python
import functools

import jax
import jax.numpy as jnp
from jax import lax
from jax.experimental import pallas as pl
from jax.experimental.pallas import tpu as pltpu
from jax.sharding import PartitionSpec as P

NR = 128
RB = 32
BY = 128
BPT = 8
CAP = 2
PASSES = 4
NSEG = 4
PER_OWNER = BPT * NSEG
LANES = 128
TILE = 8
MESSAGE = CAP * RB + TILE
LABELS = 64
STRIP = 16
SIDES = 4
PIECE = 2 * BPT + 1

diffusion_rate = 0.0615

SMALL = pltpu.CompilerParams(vmem_limit_bytes=12 * 1024 * 1024)
PACKED = pltpu.CompilerParams(
    vmem_limit_bytes=12 * 1024 * 1024
)
VMEM = pl.BlockSpec(memory_space=pltpu.VMEM)
HBM = pl.BlockSpec(memory_space=pltpu.HBM)


def lane_index(shape=(TILE, LANES)):
    return lax.broadcasted_iota(jnp.int32, shape, len(shape) - 1)


def stencil_matrices(near_ref, side_near_ref):
    row_of = lax.broadcasted_iota(jnp.int32, (LANES, LANES), 0)
    lane_of = lax.broadcasted_iota(jnp.int32, (LANES, LANES), 1)
    beside = jnp.abs(row_of - lane_of) == 1
    middle = jnp.where(row_of == lane_of, -4.0, 0.0)
    near = jnp.where(beside, 1.0, middle).astype(jnp.bfloat16)
    from_in, to_in = lax.bitwise_and(row_of, STRIP - 1), lax.bitwise_and(lane_of, STRIP - 1)
    same_strip = lax.shift_right_logical(row_of, 4) == lax.shift_right_logical(lane_of, 4)
    same_run = lax.shift_right_logical(row_of, 2) == lax.shift_right_logical(lane_of, 2)
    apart, later = jnp.abs(from_in - to_in), jnp.maximum(from_in, to_in)
    joined = ((apart == 7) & (later == 11)) | ((apart == 9) & (later == 12))
    side_near = jnp.where((beside & same_run) | (joined & same_strip), 1.0, middle).astype(jnp.bfloat16)
    exchanged = jnp.where(to_in == 11, lane_of + 1, jnp.where(to_in == 12, lane_of - 1, lane_of))
    exchange = jnp.where(row_of == exchanged, 1.0, 0.0).astype(jnp.bfloat16)
    for part in range(2):
        at = slice(part * LANES, (part + 1) * LANES)
        near_ref[at, :] = near
        side_near_ref[at, 0:LANES] = side_near
        side_near_ref[at, LANES:] = exchange


def pack_kernel(
    owners, ids_hbm, blocks_hbm, scale_hbm, smoother_hbm, level_hbm,
    out_ref, scale_ref, smoother_ref, factor_ref, near_ref, side_near_ref,
    ids_ref, blocks_ref, level_ref, sems,
):
    ids_copy = pltpu.make_async_copy(ids_hbm, ids_ref, sems.at[0])
    blocks_copy = pltpu.make_async_copy(blocks_hbm, blocks_ref, sems.at[1])
    ids_copy.start()
    blocks_copy.start()
    here = lax.axis_index("ev")
    width = scale_ref.shape[2]
    places = (jnp.maximum(here - 1, 0), here, jnp.minimum(here + 1, owners - 1))
    copies = [
        pltpu.make_async_copy(
            scale_hbm.at[:, pl.ds(pl.multiple_of(place * width, width), width)],
            scale_ref.at[n],
            sems.at[2 + n],
        )
        for n, place in enumerate(places)
    ]
    copies.append(pltpu.make_async_copy(smoother_hbm, smoother_ref, sems.at[5]))
    copies.append(pltpu.make_async_copy(level_hbm, level_ref, sems.at[6]))
    for copy in copies:
        copy.start()
    listed = ids_ref.shape[1]
    lane = lane_index()
    zero = jnp.zeros((TILE, LANES), jnp.float32)
    for row in range(0, owners * MESSAGE, TILE):
        out_ref[row : row + TILE, :] = zero
    stencil_matrices(near_ref, side_near_ref)
    ids_copy.wait()
    ids = [ids_ref[0, j] for j in range(listed)]
    owner_of = [lax.shift_right_logical(i, 5) for i in ids]
    ranks = []
    for j in range(listed):
        rank = jnp.int32(0)
        for i in range(j):
            rank = rank + jnp.where(owner_of[i] == owner_of[j], 1, 0)
        ranks.append(rank)
    group = lax.shift_right_logical(lane, 4)
    in_four = lax.bitwise_and(lax.shift_right_logical(lane, 2), 3)
    blocks_copy.wait()

    def add(owner, cells):
        there = pl.ds(pl.multiple_of(owner * MESSAGE + CAP * RB, TILE), TILE)
        out_ref[there, :] = out_ref[there, :] + cells

    for j in range(listed):
        owner, rank = owner_of[j], ranks[j]
        within = lax.bitwise_and(ids[j], PER_OWNER - 1).astype(jnp.float32)
        both = zero
        for a in range(RB // TILE):
            cells = blocks_ref[pl.ds(a * TILE * listed + j, TILE, stride=listed), :]
            start = pl.multiple_of(owner * MESSAGE + rank * RB + a * TILE, TILE)
            out_ref[pl.ds(start, TILE), :] = cells
            both = jnp.where(group == a, pltpu.roll(cells, 16 * a + 4, 1), both)
        add(owner, jnp.where(lane == LABELS + rank, within, 0.0))
        left = jnp.where(in_four == 1, both, 0.0)
        to_left = pltpu.roll(left, 4 + 4 * rank, 1)
        to_left = to_left + jnp.where(lane == LABELS + 4 + rank, within, 0.0)
        right = jnp.where(in_four == 0, both, 0.0)
        to_right = pltpu.roll(right, 4 * rank, 1)
        to_right = to_right + jnp.where(lane == LABELS + 2 + rank, within, 0.0)
        add(jnp.maximum(owner - 1, 0), jnp.where(owner > 0, to_left, 0.0))
        add(jnp.minimum(owner + 1, owners - 1), jnp.where(owner < owners - 1, to_right, 0.0))
    for copy in copies:
        copy.wait()
    for shell in range(level_ref.shape[0]):
        factor = diffusion_rate * level_ref[shell].astype(jnp.float32)
        factor_ref[shell] = jnp.full((TILE, LANES), factor, jnp.float32)


def halves(cells):
    high = cells.astype(jnp.bfloat16)
    low = (cells - high.astype(jnp.float32)).astype(jnp.bfloat16)
    return high, low


def scale_strips(scale_ref, owners):
    here = lax.axis_index("ev")
    part = scale_ref.shape[1] // SIDES
    lane = lane_index((part, LANES))
    inner = lax.bitwise_and(lane, STRIP - 1) < 8
    strip = lax.shift_right_logical(lane, 4)
    keep_after = (lane < 4) & (here < owners - 1)
    keep_before = (lane >= LANES - 4) & (here > 0)
    strips = jnp.zeros((part, LANES), jnp.float32)
    for n in range(SIDES):
        at = slice(n * part, (n + 1) * part)
        beyond = jnp.where(keep_before, scale_ref[0, at, :], 0.0)
        beyond = jnp.where(keep_after, scale_ref[2, at, :], beyond)
        both = jnp.where(
            inner,
            pltpu.roll(scale_ref[1, at, :], STRIP * n + 4, 1),
            pltpu.roll(beyond, STRIP * n + 12, 1),
        )
        strips = jnp.where(strip == n, both, strips)
    return strips + pltpu.roll(strips, LANES // 2, 1)


def smooth_kernel(
    groups, arrived_ref, scale_ref, smoother_ref, out_ref, side_scale_ref,
    columns_ref, edge_ref,
):
    labels = arrived_ref[:, CAP * RB, :].astype(jnp.int32)
    spots = [
        [labels[g : g + 1, LABELS + i : LABELS + i + 1][0, 0] for i in range(3 * CAP)]
        for g in range(groups)
    ]
    rows = [[lax.shift_right_logical(spot, 2) for spot in group] for group in spots]
    segments = [[lax.bitwise_and(spot, NSEG - 1) for spot in group] for group in spots]
    lane = lane_index()
    low = lane < LANES // 2
    lane_four = lax.bitwise_and(lane, LANES // 2 - 4)
    columns_ref[:, : BPT * LANES] = jnp.zeros((NR, BPT * LANES), jnp.float32)
    edge_ref[...] = jnp.zeros_like(edge_ref)
    side_scale_ref[...] = scale_strips(scale_ref, groups)
    for g in range(groups):
        for rank in range(CAP):
            where = (
                pl.ds(pl.multiple_of(segments[g][rank] * RB, RB), RB),
                pl.ds(pl.multiple_of(rows[g][rank] * LANES, LANES), LANES),
            )
            columns_ref[where] = columns_ref[where] + arrived_ref[g, rank * RB : (rank + 1) * RB, :]
    for g in range(groups):
        edges = arrived_ref[g, CAP * RB :, :]
        pairs = [
            jnp.where(low, edges, pltpu.roll(edges, 48, 1)),
            jnp.where(low, pltpu.roll(edges, LANES - 32, 1), pltpu.roll(edges, 16, 1)),
        ]
        for h in range(2 * CAP):
            target = (BPT - 1 - rows[g][CAP + h]) * 8 + (4 if h >= CAP else 0)
            keep = lane_four == target
            shift = lax.bitwise_and(target + (LANES - 4 * h), LANES - 1)
            four = jnp.concatenate(
                [jnp.where(keep, pltpu.roll(pair, shift, 1), 0.0) for pair in pairs], axis=0
            )
            where = pl.ds(pl.multiple_of(segments[g][CAP + h] * (2 * TILE), 2 * TILE), 2 * TILE)
            edge_ref[where, :] = edge_ref[where, :] + four
    for pair in range(NR // (2 * TILE)):
        cells = edge_ref[pair * TILE : (pair + 1) * TILE, :]
        turned = pltpu.roll(cells, LANES // 2, 1)
        at = pair * 2 * TILE
        columns_ref[at : at + TILE, BPT * LANES :] = jnp.where(low, cells, turned)
        columns_ref[at + TILE : at + 2 * TILE, BPT * LANES :] = jnp.where(low, turned, cells)
    half = NR // 2
    smoother = jnp.concatenate(
        [smoother_ref[pl.ds(0, half, stride=2), :], smoother_ref[pl.ds(1, half, stride=2), :]], axis=0
    )
    high, rest = halves(smoother)
    twice = jnp.concatenate([high, high], axis=1)

    def smoothed(start, width):
        first, second = halves(columns_ref[:, start : start + width])
        both = jnp.concatenate([first, second], axis=0)
        return jnp.dot(twice, both, preferred_element_type=jnp.float32) + jnp.dot(
            rest, first, preferred_element_type=jnp.float32
        )

    for row in range(0, BPT, 2):
        done = smoothed(row * LANES, 2 * LANES)
        for i in range(2):
            cells = done[:, i * LANES : (i + 1) * LANES]
            out_ref[pl.ds(row + i, half, stride=PIECE), :] = cells[:half]
            out_ref[pl.ds(BPT + row + i, half, stride=PIECE), :] = cells[half:]
    done = smoothed(BPT * LANES, LANES)
    lower = lane_index((half, LANES)) < LANES // 2
    out_ref[pl.ds(2 * BPT, half, stride=PIECE), :] = jnp.where(lower, done[:half], done[half:])


def diffuse_kernel(
    cells_ref, factor_ref, scale_ref, side_scale_ref, near_ref, side_near_ref, out_hbm,
    main_a, main_b, side_a, side_b, coefficient_ref, edge_ref, out_ref, sems,
):
    shells, rows, _ = out_ref.shape
    nothing = jnp.zeros((TILE, LANES), jnp.float32)
    stripes = rows // BPT
    tiles = stripes // SIDES
    part = tiles * TILE
    for buffer in (main_a, main_b):
        for shell in range(shells):
            buffer[shell, 0:TILE, :] = nothing
            buffer[shell, TILE + rows : 2 * TILE + rows, :] = nothing
    slots = [(n, shell, (1 - shell) * SIDES + n) for n in range(SIDES) for shell in range(shells)]

    strip = lax.shift_right_logical(lane_index(), 4)
    for v in range(tiles):
        outer = nothing
        for n in range(SIDES):
            stripe = n * tiles + v
            at = stripe * PIECE
            spot = TILE + stripe * BPT
            wide = jnp.broadcast_to(cells_ref[at + 2 * BPT : at + PIECE, :], (TILE, LANES))
            turned = pltpu.roll(wide, STRIP * (n + 1), 1, stride=8, stride_axis=0)
            outer = jnp.where(lax.bitwise_and(strip, SIDES - 1) == n, turned, outer)
            for shell in range(shells):
                main_a[shell, spot : spot + BPT, :] = cells_ref[
                    at + shell * BPT : at + (shell + 1) * BPT, :
                ]
        side_a[TILE + v * TILE : 2 * TILE + v * TILE, :] = outer
    lane = lane_index((part, LANES))
    strip = lax.shift_right_logical(lane, 4)
    inner = lax.bitwise_and(lane, STRIP - 1) < 8

    lane_row = lane_index((1, LANES))
    stripe_in = lax.bitwise_and(lane_row, SIDES * STRIP - 1)
    last_row = TILE + part - 1

    def join(side):
        down = pltpu.roll(side[last_row : last_row + 1, :], STRIP, 1)
        side[TILE - 1 : TILE, :] = jnp.where(stripe_in < STRIP, 0.0, down)
        up = pltpu.roll(side[TILE : TILE + 1, :], LANES - STRIP, 1)
        side[last_row + 1 : last_row + 2, :] = jnp.where(stripe_in >= (SIDES - 1) * STRIP, 0.0, up)

    lane_tile = lane_index()
    factors = [jnp.tile(factor_ref[shell], (tiles, 1)) for shell in range(shells)]
    side_factor = jnp.tile(
        jnp.where(lane_tile < LANES // 2, factor_ref[1], factor_ref[0]), (tiles, 1)
    )
    is_edge = (lane == 0) | (lane == LANES - 1)

    def across(cells, matrix):
        return jnp.dot(
            jnp.concatenate(halves(cells), axis=1), matrix, preferred_element_type=jnp.float32
        )

    def side_step(side, side_next, sums):
        middle = side[TILE : TILE + part, :]
        vertical = side[TILE - 1 : TILE + part - 1, :] + side[TILE + 1 : TILE + part + 1, :]
        coefficient = side_factor * side_scale_ref[...]
        side_next[TILE : TILE + part, :] = middle + coefficient * (vertical + sums)
        join(side_next)

    buffers = ((main_a, side_a), (main_b, side_b))
    for repeat in range(PASSES):
        (main, side), (main_next, side_next) = buffers[repeat % 2], buffers[(repeat + 1) % 2]
        final = repeat == PASSES - 1
        if repeat == 0 or final:
            edge_ref[...] = across(side[TILE : TILE + part, :], side_near_ref[:, LANES:])
        else:
            sums = across(side[TILE : TILE + part, :], side_near_ref[...])
            edge_ref[...] = sums[:, LANES:]
            side_step(side, side_next, sums[:, :LANES])
        for n, shell, slot in slots:
            at = slice(n * part, (n + 1) * part)
            first = TILE + n * part
            middle = main[shell, first : first + part, :]
            sums = across(middle, near_ref[...])
            turned = pltpu.roll(edge_ref[...], (2 * LANES - STRIP * slot - 12) % LANES, 1)
            vertical = (
                main[shell, first - 1 : first + part - 1, :]
                + main[shell, first + 1 : first + part + 1, :]
            )
            if repeat == 0:
                coefficient = factors[shell] * scale_ref[1, at, :]
                coefficient_ref[shell, at, :] = coefficient
                side[TILE : TILE + part, :] = jnp.where(
                    inner & (strip == slot),
                    pltpu.roll(middle, STRIP * slot + 4, 1),
                    side[TILE : TILE + part, :],
                )
            else:
                coefficient = coefficient_ref[shell, at, :]
            new = middle + coefficient * ((vertical + sums) + jnp.where(is_edge, turned, 0.0))
            if final:
                out_ref[shell, at, :] = new
            else:
                main_next[shell, first : first + part, :] = new
        if repeat == 0:
            join(side)
            side_step(
                side, side_next, across(side[TILE : TILE + part, :], side_near_ref[:, :LANES])
            )
    out_copy = pltpu.make_async_copy(out_ref, out_hbm, sems.at[0])
    out_copy.start()
    out_copy.wait()


def in_hbm(array):
    return pltpu.with_memory_space_constraint(array, pltpu.HBM)


def per_device(partial_kernels, block_ids, radial_smoother, shell_level, lateral_scale):
    owners = lax.axis_size("ev")
    holders = lax.axis_size("sp")
    listed = block_ids.shape[1]
    rows, columns = lateral_scale.shape
    mine = shell_level.shape[0]
    part = rows // SIDES
    packed, scale, smoother, factor, near, side_near = pl.pallas_call(
        functools.partial(pack_kernel, owners),
        out_shape=[
            jax.ShapeDtypeStruct((owners * MESSAGE, LANES), jnp.float32),
            jax.ShapeDtypeStruct((3, rows, columns // owners), jnp.float32),
            jax.ShapeDtypeStruct((NR, NR), jnp.float32),
            jax.ShapeDtypeStruct((mine, TILE, LANES), jnp.float32),
            jax.ShapeDtypeStruct((2 * LANES, LANES), jnp.bfloat16),
            jax.ShapeDtypeStruct((2 * LANES, 2 * LANES), jnp.bfloat16),
        ],
        in_specs=[HBM] * 5,
        out_specs=[VMEM] * 6,
        scratch_shapes=[
            pltpu.SMEM((1, listed), jnp.int32),
            pltpu.VMEM((RB * listed, LANES), jnp.float32),
            pltpu.SMEM((mine,), jnp.int32),
            pltpu.SemaphoreType.DMA((7,)),
        ],
        compiler_params=SMALL,
    )(
        in_hbm(block_ids),
        in_hbm(partial_kernels.reshape(RB * listed, BY)),
        in_hbm(lateral_scale),
        in_hbm(radial_smoother),
        in_hbm(shell_level),
    )
    arrived = lax.all_to_all(
        packed.reshape(owners, MESSAGE, LANES), "ev", split_axis=0, concat_axis=0, tiled=True
    )
    pieces, side_scale = pl.pallas_call(
        functools.partial(smooth_kernel, owners),
        out_shape=[
            jax.ShapeDtypeStruct((holders * PIECE, LANES), jnp.float32),
            jax.ShapeDtypeStruct((part, LANES), jnp.float32),
        ],
        in_specs=[VMEM] * 3,
        out_specs=[VMEM] * 2,
        scratch_shapes=[
            pltpu.VMEM((NR, (BPT + 1) * LANES), jnp.float32),
            pltpu.VMEM((NR // 2, LANES), jnp.float32),
        ],
        compiler_params=PACKED,
    )(arrived, scale, smoother)
    shells = lax.all_to_all(
        pieces.reshape(holders, 1, PIECE * LANES), "sp", split_axis=0, concat_axis=0, tiled=True
    ).reshape(holders * PIECE, LANES)
    padded = pltpu.VMEM((mine, rows + 2 * TILE, LANES), jnp.float32)
    plain = pltpu.VMEM((mine, rows, LANES), jnp.float32)
    side = pltpu.VMEM((part + 2 * TILE, LANES), jnp.float32)
    return pl.pallas_call(
        diffuse_kernel,
        out_shape=jax.ShapeDtypeStruct((mine, rows, columns // owners), jnp.float32),
        in_specs=[VMEM] * 6,
        out_specs=HBM,
        scratch_shapes=[
            padded,
            padded,
            side,
            side,
            plain,
            pltpu.VMEM((part, LANES), jnp.float32),
            plain,
            pltpu.SemaphoreType.DMA((1,)),
        ],
        compiler_params=SMALL,
    )(shells, factor, scale, side_scale, near, side_near)


def solution(mesh):
    placed = (P("ev", None, "sp", None), P("ev", "sp"), P(), P("sp"), P())
    return jax.shard_map(
        per_device, mesh=mesh, in_specs=placed, out_specs=P("sp", None, "ev"), check_vma=False
    )
```

```python
import functools

import jax
import jax.numpy as jnp
from jax import lax
from jax.experimental import pallas as pl
from jax.experimental.pallas import tpu as pltpu
from jax.sharding import PartitionSpec as P

NR = 128
RB = 32
BY = 128
BPT = 8
CAP = 2
PASSES = 4
NSEG = 4
PER_OWNER = BPT * NSEG
LANES = 128
TILE = 8
MESSAGE = CAP * RB + TILE
LABELS = 64
STRIP = 16
SIDES = 4
PIECE = 2 * BPT + 1

diffusion_rate = 0.0615

SMALL = pltpu.CompilerParams(vmem_limit_bytes=12 * 1024 * 1024)
PACKED = pltpu.CompilerParams(
    vmem_limit_bytes=12 * 1024 * 1024
)
VMEM = pl.BlockSpec(memory_space=pltpu.VMEM)
HBM = pl.BlockSpec(memory_space=pltpu.HBM)


def place_of(holder, holders):
    return (holder + holders // 2) % holders


def lane_index(shape=(TILE, LANES)):
    return lax.broadcasted_iota(jnp.int32, shape, len(shape) - 1)


def stencil_matrices(near_ref, side_near_ref):
    row_of = lax.broadcasted_iota(jnp.int32, (LANES, LANES), 0)
    lane_of = lax.broadcasted_iota(jnp.int32, (LANES, LANES), 1)
    beside = jnp.abs(row_of - lane_of) == 1
    middle = jnp.where(row_of == lane_of, -4.0, 0.0)
    near = jnp.where(beside, 1.0, middle).astype(jnp.bfloat16)
    from_in, to_in = lax.bitwise_and(row_of, STRIP - 1), lax.bitwise_and(lane_of, STRIP - 1)
    same_strip = lax.shift_right_logical(row_of, 4) == lax.shift_right_logical(lane_of, 4)
    same_run = lax.shift_right_logical(row_of, 2) == lax.shift_right_logical(lane_of, 2)
    apart, later = jnp.abs(from_in - to_in), jnp.maximum(from_in, to_in)
    joined = ((apart == 7) & (later == 11)) | ((apart == 9) & (later == 12))
    side_near = jnp.where((beside & same_run) | (joined & same_strip), 1.0, middle).astype(jnp.bfloat16)
    exchanged = jnp.where(to_in == 11, lane_of + 1, jnp.where(to_in == 12, lane_of - 1, lane_of))
    exchange = jnp.where(row_of == exchanged, 1.0, 0.0).astype(jnp.bfloat16)
    for part in range(2):
        at = slice(part * LANES, (part + 1) * LANES)
        near_ref[at, :] = near
        side_near_ref[at, 0:LANES] = side_near
        side_near_ref[at, LANES:] = exchange


def pack_kernel(
    owners, ids_hbm, blocks_hbm, scale_hbm, smoother_hbm, level_hbm,
    out_ref, scale_ref, smoother_ref, factor_ref, near_ref, side_near_ref,
    ids_ref, blocks_ref, level_ref, sems,
):
    ids_copy = pltpu.make_async_copy(ids_hbm, ids_ref, sems.at[0])
    blocks_copy = pltpu.make_async_copy(blocks_hbm, blocks_ref, sems.at[1])
    ids_copy.start()
    blocks_copy.start()
    here = lax.axis_index("ev")
    width = scale_ref.shape[2]
    places = (jnp.maximum(here - 1, 0), here, jnp.minimum(here + 1, owners - 1))
    copies = [
        pltpu.make_async_copy(
            scale_hbm.at[:, pl.ds(pl.multiple_of(place * width, width), width)],
            scale_ref.at[n],
            sems.at[2 + n],
        )
        for n, place in enumerate(places)
    ]
    copies.append(pltpu.make_async_copy(smoother_hbm, smoother_ref, sems.at[5]))
    copies.append(pltpu.make_async_copy(level_hbm, level_ref, sems.at[6]))
    for copy in copies:
        copy.start()
    listed = ids_ref.shape[1]
    lane = lane_index()
    zero = jnp.zeros((TILE, LANES), jnp.float32)
    for row in range(0, owners * MESSAGE, TILE):
        out_ref[row : row + TILE, :] = zero
    stencil_matrices(near_ref, side_near_ref)
    ids_copy.wait()
    ids = [ids_ref[0, j] for j in range(listed)]
    owner_of = [lax.shift_right_logical(i, 5) for i in ids]
    ranks = []
    for j in range(listed):
        rank = jnp.int32(0)
        for i in range(j):
            rank = rank + jnp.where(owner_of[i] == owner_of[j], 1, 0)
        ranks.append(rank)
    group = lax.shift_right_logical(lane, 4)
    in_four = lax.bitwise_and(lax.shift_right_logical(lane, 2), 3)
    blocks_copy.wait()

    def add(owner, cells):
        there = pl.ds(pl.multiple_of(owner * MESSAGE + CAP * RB, TILE), TILE)
        out_ref[there, :] = out_ref[there, :] + cells

    for j in range(listed):
        owner, rank = owner_of[j], ranks[j]
        within = lax.bitwise_and(ids[j], PER_OWNER - 1).astype(jnp.float32)
        both = zero
        for a in range(RB // TILE):
            cells = blocks_ref[pl.ds(a * TILE * listed + j, TILE, stride=listed), :]
            start = pl.multiple_of(owner * MESSAGE + rank * RB + a * TILE, TILE)
            out_ref[pl.ds(start, TILE), :] = cells
            both = jnp.where(group == a, pltpu.roll(cells, 16 * a + 4, 1), both)
        add(owner, jnp.where(lane == LABELS + rank, within, 0.0))
        left = jnp.where(in_four == 1, both, 0.0)
        to_left = pltpu.roll(left, 4 + 4 * rank, 1)
        to_left = to_left + jnp.where(lane == LABELS + 4 + rank, within, 0.0)
        right = jnp.where(in_four == 0, both, 0.0)
        to_right = pltpu.roll(right, 4 * rank, 1)
        to_right = to_right + jnp.where(lane == LABELS + 2 + rank, within, 0.0)
        add(jnp.maximum(owner - 1, 0), jnp.where(owner > 0, to_left, 0.0))
        add(jnp.minimum(owner + 1, owners - 1), jnp.where(owner < owners - 1, to_right, 0.0))
    for copy in copies:
        copy.wait()
    for shell in range(level_ref.shape[0]):
        factor = diffusion_rate * level_ref[shell].astype(jnp.float32)
        factor_ref[shell] = jnp.full((TILE, LANES), factor, jnp.float32)


def halves(cells):
    high = cells.astype(jnp.bfloat16)
    low = (cells - high.astype(jnp.float32)).astype(jnp.bfloat16)
    return high, low


def scale_strips(scale_ref, owners):
    here = lax.axis_index("ev")
    part = scale_ref.shape[1] // SIDES
    lane = lane_index((part, LANES))
    inner = lax.bitwise_and(lane, STRIP - 1) < 8
    strip = lax.shift_right_logical(lane, 4)
    keep_after = (lane < 4) & (here < owners - 1)
    keep_before = (lane >= LANES - 4) & (here > 0)
    strips = jnp.zeros((part, LANES), jnp.float32)
    for n in range(SIDES):
        at = slice(n * part, (n + 1) * part)
        beyond = jnp.where(keep_before, scale_ref[0, at, :], 0.0)
        beyond = jnp.where(keep_after, scale_ref[2, at, :], beyond)
        both = jnp.where(
            inner,
            pltpu.roll(scale_ref[1, at, :], STRIP * n + 4, 1),
            pltpu.roll(beyond, STRIP * n + 12, 1),
        )
        strips = jnp.where(strip == n, both, strips)
    return strips + pltpu.roll(strips, LANES // 2, 1)


def smooth_kernel(
    groups, arrived_ref, scale_ref, smoother_ref, out_ref, side_scale_ref,
    columns_ref, edge_ref,
):
    labels = arrived_ref[:, CAP * RB, :].astype(jnp.int32)
    spots = [
        [labels[g : g + 1, LABELS + i : LABELS + i + 1][0, 0] for i in range(3 * CAP)]
        for g in range(groups)
    ]
    rows = [[lax.shift_right_logical(spot, 2) for spot in group] for group in spots]
    segments = [[lax.bitwise_and(spot, NSEG - 1) for spot in group] for group in spots]
    lane = lane_index()
    low = lane < LANES // 2
    lane_four = lax.bitwise_and(lane, LANES // 2 - 4)
    columns_ref[:, : BPT * LANES] = jnp.zeros((NR, BPT * LANES), jnp.float32)
    edge_ref[...] = jnp.zeros_like(edge_ref)
    side_scale_ref[...] = scale_strips(scale_ref, groups)
    for g in range(groups):
        for rank in range(CAP):
            where = (
                pl.ds(pl.multiple_of(segments[g][rank] * RB, RB), RB),
                pl.ds(pl.multiple_of(rows[g][rank] * LANES, LANES), LANES),
            )
            columns_ref[where] = columns_ref[where] + arrived_ref[g, rank * RB : (rank + 1) * RB, :]
    for g in range(groups):
        edges = arrived_ref[g, CAP * RB :, :]
        pairs = [
            jnp.where(low, edges, pltpu.roll(edges, 48, 1)),
            jnp.where(low, pltpu.roll(edges, LANES - 32, 1), pltpu.roll(edges, 16, 1)),
        ]
        for h in range(2 * CAP):
            target = (BPT - 1 - rows[g][CAP + h]) * 8 + (4 if h >= CAP else 0)
            keep = lane_four == target
            shift = lax.bitwise_and(target + (LANES - 4 * h), LANES - 1)
            four = jnp.concatenate(
                [jnp.where(keep, pltpu.roll(pair, shift, 1), 0.0) for pair in pairs], axis=0
            )
            where = pl.ds(pl.multiple_of(segments[g][CAP + h] * (2 * TILE), 2 * TILE), 2 * TILE)
            edge_ref[where, :] = edge_ref[where, :] + four
    for pair in range(NR // (2 * TILE)):
        cells = edge_ref[pair * TILE : (pair + 1) * TILE, :]
        turned = pltpu.roll(cells, LANES // 2, 1)
        at = pair * 2 * TILE
        columns_ref[at : at + TILE, BPT * LANES :] = jnp.where(low, cells, turned)
        columns_ref[at + TILE : at + 2 * TILE, BPT * LANES :] = jnp.where(low, turned, cells)
    half = NR // 2
    quarter = half // 2
    starts = [half + 0, 0, half + 1, 1]
    smoother = jnp.concatenate(
        [smoother_ref[pl.ds(start, quarter, stride=2), :] for start in starts], axis=0
    )
    high, rest = halves(smoother)
    twice = jnp.concatenate([high, high], axis=1)

    def smoothed(start, width):
        first, second = halves(columns_ref[:, start : start + width])
        both = jnp.concatenate([first, second], axis=0)
        return jnp.dot(twice, both, preferred_element_type=jnp.float32) + jnp.dot(
            rest, first, preferred_element_type=jnp.float32
        )

    for row in range(0, BPT, 2):
        done = smoothed(row * LANES, 2 * LANES)
        for i in range(2):
            cells = done[:, i * LANES : (i + 1) * LANES]
            out_ref[pl.ds(row + i, half, stride=PIECE), :] = cells[:half]
            out_ref[pl.ds(BPT + row + i, half, stride=PIECE), :] = cells[half:]
    done = smoothed(BPT * LANES, LANES)
    lower = lane_index((half, LANES)) < LANES // 2
    out_ref[pl.ds(2 * BPT, half, stride=PIECE), :] = jnp.where(lower, done[:half], done[half:])


def diffuse_kernel(
    cells_ref, factor_ref, scale_ref, side_scale_ref, near_ref, side_near_ref, out_hbm,
    main_a, main_b, side_a, side_b, coefficient_ref, edge_ref, out_ref, sems,
):
    shells, rows, _ = out_ref.shape
    nothing = jnp.zeros((TILE, LANES), jnp.float32)
    stripes = rows // BPT
    tiles = stripes // SIDES
    part = tiles * TILE
    for buffer in (main_a, main_b):
        for shell in range(shells):
            buffer[shell, 0:TILE, :] = nothing
            buffer[shell, TILE + rows : 2 * TILE + rows, :] = nothing
    slots = [(n, shell, (1 - shell) * SIDES + n) for n in range(SIDES) for shell in range(shells)]

    strip = lax.shift_right_logical(lane_index(), 4)
    for v in range(tiles):
        outer = nothing
        for n in range(SIDES):
            stripe = n * tiles + v
            at = place_of(stripe, stripes) * PIECE
            spot = TILE + stripe * BPT
            wide = jnp.broadcast_to(cells_ref[at + 2 * BPT : at + PIECE, :], (TILE, LANES))
            turned = pltpu.roll(wide, STRIP * (n + 1), 1, stride=8, stride_axis=0)
            outer = jnp.where(lax.bitwise_and(strip, SIDES - 1) == n, turned, outer)
            for shell in range(shells):
                main_a[shell, spot : spot + BPT, :] = cells_ref[
                    at + shell * BPT : at + (shell + 1) * BPT, :
                ]
        side_a[TILE + v * TILE : 2 * TILE + v * TILE, :] = outer
    lane = lane_index((part, LANES))
    strip = lax.shift_right_logical(lane, 4)
    inner = lax.bitwise_and(lane, STRIP - 1) < 8

    lane_row = lane_index((1, LANES))
    stripe_in = lax.bitwise_and(lane_row, SIDES * STRIP - 1)
    last_row = TILE + part - 1

    def join(side):
        down = pltpu.roll(side[last_row : last_row + 1, :], STRIP, 1)
        side[TILE - 1 : TILE, :] = jnp.where(stripe_in < STRIP, 0.0, down)
        up = pltpu.roll(side[TILE : TILE + 1, :], LANES - STRIP, 1)
        side[last_row + 1 : last_row + 2, :] = jnp.where(stripe_in >= (SIDES - 1) * STRIP, 0.0, up)

    lane_tile = lane_index()
    factors = [jnp.tile(factor_ref[shell], (tiles, 1)) for shell in range(shells)]
    side_factor = jnp.tile(
        jnp.where(lane_tile < LANES // 2, factor_ref[1], factor_ref[0]), (tiles, 1)
    )
    is_edge = (lane == 0) | (lane == LANES - 1)

    def across(cells, matrix):
        return jnp.dot(
            jnp.concatenate(halves(cells), axis=1), matrix, preferred_element_type=jnp.float32
        )

    def side_step(side, side_next, sums):
        middle = side[TILE : TILE + part, :]
        vertical = side[TILE - 1 : TILE + part - 1, :] + side[TILE + 1 : TILE + part + 1, :]
        coefficient = side_factor * side_scale_ref[...]
        side_next[TILE : TILE + part, :] = middle + coefficient * (vertical + sums)
        join(side_next)

    buffers = ((main_a, side_a), (main_b, side_b))
    for repeat in range(PASSES):
        (main, side), (main_next, side_next) = buffers[repeat % 2], buffers[(repeat + 1) % 2]
        final = repeat == PASSES - 1
        if repeat == 0 or final:
            edge_ref[...] = across(side[TILE : TILE + part, :], side_near_ref[:, LANES:])
        else:
            sums = across(side[TILE : TILE + part, :], side_near_ref[...])
            edge_ref[...] = sums[:, LANES:]
            side_step(side, side_next, sums[:, :LANES])
        for n, shell, slot in slots:
            at = slice(n * part, (n + 1) * part)
            first = TILE + n * part
            middle = main[shell, first : first + part, :]
            sums = across(middle, near_ref[...])
            turned = pltpu.roll(edge_ref[...], (2 * LANES - STRIP * slot - 12) % LANES, 1)
            vertical = (
                main[shell, first - 1 : first + part - 1, :]
                + main[shell, first + 1 : first + part + 1, :]
            )
            if repeat == 0:
                coefficient = factors[shell] * scale_ref[1, at, :]
                coefficient_ref[shell, at, :] = coefficient
                side[TILE : TILE + part, :] = jnp.where(
                    inner & (strip == slot),
                    pltpu.roll(middle, STRIP * slot + 4, 1),
                    side[TILE : TILE + part, :],
                )
            else:
                coefficient = coefficient_ref[shell, at, :]
            new = middle + coefficient * ((vertical + sums) + jnp.where(is_edge, turned, 0.0))
            if final:
                out_ref[shell, at, :] = new
            else:
                main_next[shell, first : first + part, :] = new
        if repeat == 0:
            join(side)
            side_step(
                side, side_next, across(side[TILE : TILE + part, :], side_near_ref[:, :LANES])
            )
    out_copy = pltpu.make_async_copy(out_ref, out_hbm, sems.at[0])
    out_copy.start()
    out_copy.wait()


def in_hbm(array):
    return pltpu.with_memory_space_constraint(array, pltpu.HBM)


def per_device(partial_kernels, block_ids, radial_smoother, shell_level, lateral_scale):
    owners = lax.axis_size("ev")
    holders = lax.axis_size("sp")
    listed = block_ids.shape[1]
    rows, columns = lateral_scale.shape
    mine = shell_level.shape[0]
    part = rows // SIDES
    packed, scale, smoother, factor, near, side_near = pl.pallas_call(
        functools.partial(pack_kernel, owners),
        out_shape=[
            jax.ShapeDtypeStruct((owners * MESSAGE, LANES), jnp.float32),
            jax.ShapeDtypeStruct((3, rows, columns // owners), jnp.float32),
            jax.ShapeDtypeStruct((NR, NR), jnp.float32),
            jax.ShapeDtypeStruct((mine, TILE, LANES), jnp.float32),
            jax.ShapeDtypeStruct((2 * LANES, LANES), jnp.bfloat16),
            jax.ShapeDtypeStruct((2 * LANES, 2 * LANES), jnp.bfloat16),
        ],
        in_specs=[HBM] * 5,
        out_specs=[VMEM] * 6,
        scratch_shapes=[
            pltpu.SMEM((1, listed), jnp.int32),
            pltpu.VMEM((RB * listed, LANES), jnp.float32),
            pltpu.SMEM((mine,), jnp.int32),
            pltpu.SemaphoreType.DMA((7,)),
        ],
        compiler_params=SMALL,
    )(
        in_hbm(block_ids),
        in_hbm(partial_kernels.reshape(RB * listed, BY)),
        in_hbm(lateral_scale),
        in_hbm(radial_smoother),
        in_hbm(shell_level),
    )
    arrived = lax.all_to_all(
        packed.reshape(owners, MESSAGE, LANES), "ev", split_axis=0, concat_axis=0, tiled=True
    )
    pieces, side_scale = pl.pallas_call(
        functools.partial(smooth_kernel, owners),
        out_shape=[
            jax.ShapeDtypeStruct((holders * PIECE, LANES), jnp.float32),
            jax.ShapeDtypeStruct((part, LANES), jnp.float32),
        ],
        in_specs=[VMEM] * 3,
        out_specs=[VMEM] * 2,
        scratch_shapes=[
            pltpu.VMEM((NR, (BPT + 1) * LANES), jnp.float32),
            pltpu.VMEM((NR // 2, LANES), jnp.float32),
        ],
        compiler_params=PACKED,
    )(arrived, scale, smoother)
    shells = lax.all_to_all(
        pieces.reshape(holders, 1, PIECE * LANES),
        "sp",
        split_axis=0,
        concat_axis=0,
        tiled=True,
        axis_index_groups=[[place_of(place, holders) for place in range(holders)]],
    ).reshape(holders * PIECE, LANES)
    padded = pltpu.VMEM((mine, rows + 2 * TILE, LANES), jnp.float32)
    plain = pltpu.VMEM((mine, rows, LANES), jnp.float32)
    side = pltpu.VMEM((part + 2 * TILE, LANES), jnp.float32)
    return pl.pallas_call(
        diffuse_kernel,
        out_shape=jax.ShapeDtypeStruct((mine, rows, columns // owners), jnp.float32),
        in_specs=[VMEM] * 6,
        out_specs=HBM,
        scratch_shapes=[
            padded,
            padded,
            side,
            side,
            plain,
            pltpu.VMEM((part, LANES), jnp.float32),
            plain,
            pltpu.SemaphoreType.DMA((1,)),
        ],
        compiler_params=SMALL,
    )(shells, factor, scale, side_scale, near, side_near)


def solution(mesh):
    placed = (P("ev", None, "sp", None), P("ev", "sp"), P(), P("sp"), P())
    return jax.shard_map(
        per_device, mesh=mesh, in_specs=placed, out_specs=P("sp", None, "ev"), check_vma=False
    )
```

```python
import functools

import jax
import jax.numpy as jnp
from jax import lax
from jax.experimental import pallas as pl
from jax.experimental.pallas import tpu as pltpu
from jax.sharding import PartitionSpec as P

NR = 128
RB = 32
BY = 128
BPT = 8
CAP = 2
PASSES = 4
NSEG = 4
PER_OWNER = BPT * NSEG
LANES = 128
TILE = 8
MESSAGE = CAP * RB + TILE
LABELS = 64
STRIP = 16
SIDES = 4
PIECE = 2 * BPT + 1

diffusion_rate = 0.0615

SMALL = pltpu.CompilerParams(vmem_limit_bytes=12 * 1024 * 1024)
PACKED = pltpu.CompilerParams(
    vmem_limit_bytes=12 * 1024 * 1024
)
VMEM = pl.BlockSpec(memory_space=pltpu.VMEM)
HBM = pl.BlockSpec(memory_space=pltpu.HBM)


def place_of(holder, holders):
    return (holder + holders // 2) % holders


def lane_index(shape=(TILE, LANES)):
    return lax.broadcasted_iota(jnp.int32, shape, len(shape) - 1)


def stencil_matrices(near_ref, side_near_ref):
    row_of = lax.broadcasted_iota(jnp.int32, (LANES, LANES), 0)
    lane_of = lax.broadcasted_iota(jnp.int32, (LANES, LANES), 1)
    beside = jnp.abs(row_of - lane_of) == 1
    middle = jnp.where(row_of == lane_of, -4.0, 0.0)
    near = jnp.where(beside, 1.0, middle).astype(jnp.bfloat16)
    from_in, to_in = lax.bitwise_and(row_of, STRIP - 1), lax.bitwise_and(lane_of, STRIP - 1)
    same_strip = lax.shift_right_logical(row_of, 4) == lax.shift_right_logical(lane_of, 4)
    same_run = lax.shift_right_logical(row_of, 2) == lax.shift_right_logical(lane_of, 2)
    apart, later = jnp.abs(from_in - to_in), jnp.maximum(from_in, to_in)
    joined = ((apart == 7) & (later == 11)) | ((apart == 9) & (later == 12))
    side_near = jnp.where((beside & same_run) | (joined & same_strip), 1.0, middle).astype(jnp.bfloat16)
    exchanged = jnp.where(to_in == 11, lane_of + 1, jnp.where(to_in == 12, lane_of - 1, lane_of))
    exchange = jnp.where(row_of == exchanged, 1.0, 0.0).astype(jnp.bfloat16)
    for part in range(2):
        at = slice(part * LANES, (part + 1) * LANES)
        near_ref[at, :] = near
        side_near_ref[at, 0:LANES] = side_near
        side_near_ref[at, LANES:] = exchange


def pack_kernel(
    owners, ids_hbm, blocks_hbm, scale_hbm, smoother_hbm, level_hbm,
    out_ref, scale_ref, smoother_ref, factor_ref, near_ref, side_near_ref,
    ids_ref, blocks_ref, level_ref, sems,
):
    ids_copy = pltpu.make_async_copy(ids_hbm, ids_ref, sems.at[0])
    blocks_copy = pltpu.make_async_copy(blocks_hbm, blocks_ref, sems.at[1])
    ids_copy.start()
    blocks_copy.start()
    here = lax.axis_index("ev")
    width = scale_ref.shape[2]
    places = (jnp.maximum(here - 1, 0), here, jnp.minimum(here + 1, owners - 1))
    copies = [
        pltpu.make_async_copy(
            scale_hbm.at[:, pl.ds(pl.multiple_of(place * width, width), width)],
            scale_ref.at[n],
            sems.at[2 + n],
        )
        for n, place in enumerate(places)
    ]
    copies.append(pltpu.make_async_copy(smoother_hbm, smoother_ref, sems.at[5]))
    copies.append(pltpu.make_async_copy(level_hbm, level_ref, sems.at[6]))
    for copy in copies:
        copy.start()
    listed = ids_ref.shape[1]
    lane = lane_index()
    zero = jnp.zeros((TILE, LANES), jnp.float32)
    for row in range(0, owners * MESSAGE, TILE):
        out_ref[row : row + TILE, :] = zero
    stencil_matrices(near_ref, side_near_ref)
    ids_copy.wait()
    ids = [ids_ref[0, j] for j in range(listed)]
    owner_of = [lax.shift_right_logical(i, 5) for i in ids]
    ranks = []
    for j in range(listed):
        rank = jnp.int32(0)
        for i in range(j):
            rank = rank + jnp.where(owner_of[i] == owner_of[j], 1, 0)
        ranks.append(rank)
    group = lax.shift_right_logical(lane, 4)
    in_four = lax.bitwise_and(lax.shift_right_logical(lane, 2), 3)
    blocks_copy.wait()

    def message(owner):
        return lax.rem(owner + owners // 4, owners) * MESSAGE

    def add(owner, cells):
        there = pl.ds(pl.multiple_of(message(owner) + CAP * RB, TILE), TILE)
        out_ref[there, :] = out_ref[there, :] + cells

    for j in range(listed):
        owner, rank = owner_of[j], ranks[j]
        within = lax.bitwise_and(ids[j], PER_OWNER - 1).astype(jnp.float32)
        both = zero
        for a in range(RB // TILE):
            cells = blocks_ref[pl.ds(a * TILE * listed + j, TILE, stride=listed), :]
            start = pl.multiple_of(message(owner) + rank * RB + a * TILE, TILE)
            out_ref[pl.ds(start, TILE), :] = cells
            both = jnp.where(group == a, pltpu.roll(cells, 16 * a + 4, 1), both)
        add(owner, jnp.where(lane == LABELS + rank, within, 0.0))
        left = jnp.where(in_four == 1, both, 0.0)
        to_left = pltpu.roll(left, 4 + 4 * rank, 1)
        to_left = to_left + jnp.where(lane == LABELS + 4 + rank, within, 0.0)
        right = jnp.where(in_four == 0, both, 0.0)
        to_right = pltpu.roll(right, 4 * rank, 1)
        to_right = to_right + jnp.where(lane == LABELS + 2 + rank, within, 0.0)
        add(jnp.maximum(owner - 1, 0), jnp.where(owner > 0, to_left, 0.0))
        add(jnp.minimum(owner + 1, owners - 1), jnp.where(owner < owners - 1, to_right, 0.0))
    for copy in copies:
        copy.wait()
    for shell in range(level_ref.shape[0]):
        factor = diffusion_rate * level_ref[shell].astype(jnp.float32)
        factor_ref[shell] = jnp.full((TILE, LANES), factor, jnp.float32)


def halves(cells):
    high = cells.astype(jnp.bfloat16)
    low = (cells - high.astype(jnp.float32)).astype(jnp.bfloat16)
    return high, low


def scale_strips(scale_ref, owners):
    here = lax.axis_index("ev")
    part = scale_ref.shape[1] // SIDES
    lane = lane_index((part, LANES))
    inner = lax.bitwise_and(lane, STRIP - 1) < 8
    strip = lax.shift_right_logical(lane, 4)
    keep_after = (lane < 4) & (here < owners - 1)
    keep_before = (lane >= LANES - 4) & (here > 0)
    strips = jnp.zeros((part, LANES), jnp.float32)
    for n in range(SIDES):
        at = slice(n * part, (n + 1) * part)
        beyond = jnp.where(keep_before, scale_ref[0, at, :], 0.0)
        beyond = jnp.where(keep_after, scale_ref[2, at, :], beyond)
        both = jnp.where(
            inner,
            pltpu.roll(scale_ref[1, at, :], STRIP * n + 4, 1),
            pltpu.roll(beyond, STRIP * n + 12, 1),
        )
        strips = jnp.where(strip == n, both, strips)
    return strips + pltpu.roll(strips, LANES // 2, 1)


def smooth_kernel(
    groups, arrived_ref, scale_ref, smoother_ref, out_ref, side_scale_ref,
    columns_ref, edge_ref,
):
    labels = arrived_ref[:, CAP * RB, :].astype(jnp.int32)
    spots = [
        [labels[g : g + 1, LABELS + i : LABELS + i + 1][0, 0] for i in range(3 * CAP)]
        for g in range(groups)
    ]
    rows = [[lax.shift_right_logical(spot, 2) for spot in group] for group in spots]
    segments = [[lax.bitwise_and(spot, NSEG - 1) for spot in group] for group in spots]
    lane = lane_index()
    low = lane < LANES // 2
    lane_four = lax.bitwise_and(lane, LANES // 2 - 4)
    columns_ref[:, : BPT * LANES] = jnp.zeros((NR, BPT * LANES), jnp.float32)
    edge_ref[...] = jnp.zeros_like(edge_ref)
    side_scale_ref[...] = scale_strips(scale_ref, groups)
    for g in range(groups):
        for rank in range(CAP):
            where = (
                pl.ds(pl.multiple_of(segments[g][rank] * RB, RB), RB),
                pl.ds(pl.multiple_of(rows[g][rank] * LANES, LANES), LANES),
            )
            columns_ref[where] = columns_ref[where] + arrived_ref[g, rank * RB : (rank + 1) * RB, :]
    for g in range(groups):
        edges = arrived_ref[g, CAP * RB :, :]
        pairs = [
            jnp.where(low, edges, pltpu.roll(edges, 48, 1)),
            jnp.where(low, pltpu.roll(edges, LANES - 32, 1), pltpu.roll(edges, 16, 1)),
        ]
        for h in range(2 * CAP):
            target = (BPT - 1 - rows[g][CAP + h]) * 8 + (4 if h >= CAP else 0)
            keep = lane_four == target
            shift = lax.bitwise_and(target + (LANES - 4 * h), LANES - 1)
            four = jnp.concatenate(
                [jnp.where(keep, pltpu.roll(pair, shift, 1), 0.0) for pair in pairs], axis=0
            )
            where = pl.ds(pl.multiple_of(segments[g][CAP + h] * (2 * TILE), 2 * TILE), 2 * TILE)
            edge_ref[where, :] = edge_ref[where, :] + four
    for pair in range(NR // (2 * TILE)):
        cells = edge_ref[pair * TILE : (pair + 1) * TILE, :]
        turned = pltpu.roll(cells, LANES // 2, 1)
        at = pair * 2 * TILE
        columns_ref[at : at + TILE, BPT * LANES :] = jnp.where(low, cells, turned)
        columns_ref[at + TILE : at + 2 * TILE, BPT * LANES :] = jnp.where(low, turned, cells)
    half = NR // 2
    quarter = half // 2
    starts = [half + 0, 0, half + 1, 1]
    smoother = jnp.concatenate(
        [smoother_ref[pl.ds(start, quarter, stride=2), :] for start in starts], axis=0
    )
    high, rest = halves(smoother)
    twice = jnp.concatenate([high, high], axis=1)

    def smoothed(start, width):
        first, second = halves(columns_ref[:, start : start + width])
        both = jnp.concatenate([first, second], axis=0)
        return jnp.dot(twice, both, preferred_element_type=jnp.float32) + jnp.dot(
            rest, first, preferred_element_type=jnp.float32
        )

    for row in range(0, BPT, 2):
        done = smoothed(row * LANES, 2 * LANES)
        for i in range(2):
            cells = done[:, i * LANES : (i + 1) * LANES]
            out_ref[pl.ds(row + i, half, stride=PIECE), :] = cells[:half]
            out_ref[pl.ds(BPT + row + i, half, stride=PIECE), :] = cells[half:]
    done = smoothed(BPT * LANES, LANES)
    lower = lane_index((half, LANES)) < LANES // 2
    out_ref[pl.ds(2 * BPT, half, stride=PIECE), :] = jnp.where(lower, done[:half], done[half:])


def diffuse_kernel(
    cells_ref, factor_ref, scale_ref, side_scale_ref, near_ref, side_near_ref, out_hbm,
    main_a, main_b, side_a, side_b, coefficient_ref, edge_ref, out_ref, sems,
):
    shells, rows, _ = out_ref.shape
    nothing = jnp.zeros((TILE, LANES), jnp.float32)
    stripes = rows // BPT
    tiles = stripes // SIDES
    part = tiles * TILE
    for buffer in (main_a, main_b):
        for shell in range(shells):
            buffer[shell, 0:TILE, :] = nothing
            buffer[shell, TILE + rows : 2 * TILE + rows, :] = nothing
    slots = [(n, shell, (1 - shell) * SIDES + n) for n in range(SIDES) for shell in range(shells)]

    strip = lax.shift_right_logical(lane_index(), 4)
    for v in range(tiles):
        outer = nothing
        for n in range(SIDES):
            stripe = n * tiles + v
            at = place_of(stripe, stripes) * PIECE
            spot = TILE + stripe * BPT
            wide = jnp.broadcast_to(cells_ref[at + 2 * BPT : at + PIECE, :], (TILE, LANES))
            turned = pltpu.roll(wide, STRIP * (n + 1), 1, stride=8, stride_axis=0)
            outer = jnp.where(lax.bitwise_and(strip, SIDES - 1) == n, turned, outer)
            for shell in range(shells):
                main_a[shell, spot : spot + BPT, :] = cells_ref[
                    at + shell * BPT : at + (shell + 1) * BPT, :
                ]
        side_a[TILE + v * TILE : 2 * TILE + v * TILE, :] = outer
    lane = lane_index((part, LANES))
    strip = lax.shift_right_logical(lane, 4)
    inner = lax.bitwise_and(lane, STRIP - 1) < 8

    lane_row = lane_index((1, LANES))
    stripe_in = lax.bitwise_and(lane_row, SIDES * STRIP - 1)
    last_row = TILE + part - 1

    def join(side):
        down = pltpu.roll(side[last_row : last_row + 1, :], STRIP, 1)
        side[TILE - 1 : TILE, :] = jnp.where(stripe_in < STRIP, 0.0, down)
        up = pltpu.roll(side[TILE : TILE + 1, :], LANES - STRIP, 1)
        side[last_row + 1 : last_row + 2, :] = jnp.where(stripe_in >= (SIDES - 1) * STRIP, 0.0, up)

    lane_tile = lane_index()
    factors = [jnp.tile(factor_ref[shell], (tiles, 1)) for shell in range(shells)]
    side_factor = jnp.tile(
        jnp.where(lane_tile < LANES // 2, factor_ref[1], factor_ref[0]), (tiles, 1)
    )
    is_edge = (lane == 0) | (lane == LANES - 1)

    def across(cells, matrix):
        return jnp.dot(
            jnp.concatenate(halves(cells), axis=1), matrix, preferred_element_type=jnp.float32
        )

    def side_step(side, side_next, sums):
        middle = side[TILE : TILE + part, :]
        vertical = side[TILE - 1 : TILE + part - 1, :] + side[TILE + 1 : TILE + part + 1, :]
        coefficient = side_factor * side_scale_ref[...]
        side_next[TILE : TILE + part, :] = middle + coefficient * (vertical + sums)
        join(side_next)

    buffers = ((main_a, side_a), (main_b, side_b))
    for repeat in range(PASSES):
        (main, side), (main_next, side_next) = buffers[repeat % 2], buffers[(repeat + 1) % 2]
        final = repeat == PASSES - 1
        if repeat == 0 or final:
            edge_ref[...] = across(side[TILE : TILE + part, :], side_near_ref[:, LANES:])
        else:
            sums = across(side[TILE : TILE + part, :], side_near_ref[...])
            edge_ref[...] = sums[:, LANES:]
            side_step(side, side_next, sums[:, :LANES])
        for n, shell, slot in slots:
            at = slice(n * part, (n + 1) * part)
            first = TILE + n * part
            middle = main[shell, first : first + part, :]
            sums = across(middle, near_ref[...])
            turned = pltpu.roll(edge_ref[...], (2 * LANES - STRIP * slot - 12) % LANES, 1)
            vertical = (
                main[shell, first - 1 : first + part - 1, :]
                + main[shell, first + 1 : first + part + 1, :]
            )
            if repeat == 0:
                coefficient = factors[shell] * scale_ref[1, at, :]
                coefficient_ref[shell, at, :] = coefficient
                side[TILE : TILE + part, :] = jnp.where(
                    inner & (strip == slot),
                    pltpu.roll(middle, STRIP * slot + 4, 1),
                    side[TILE : TILE + part, :],
                )
            else:
                coefficient = coefficient_ref[shell, at, :]
            new = middle + coefficient * ((vertical + sums) + jnp.where(is_edge, turned, 0.0))
            if final:
                out_ref[shell, at, :] = new
            else:
                main_next[shell, first : first + part, :] = new
        if repeat == 0:
            join(side)
            side_step(
                side, side_next, across(side[TILE : TILE + part, :], side_near_ref[:, :LANES])
            )
    out_copy = pltpu.make_async_copy(out_ref, out_hbm, sems.at[0])
    out_copy.start()
    out_copy.wait()


def in_hbm(array):
    return pltpu.with_memory_space_constraint(array, pltpu.HBM)


def per_device(partial_kernels, block_ids, radial_smoother, shell_level, lateral_scale):
    owners = lax.axis_size("ev")
    holders = lax.axis_size("sp")
    listed = block_ids.shape[1]
    rows, columns = lateral_scale.shape
    mine = shell_level.shape[0]
    part = rows // SIDES
    packed, scale, smoother, factor, near, side_near = pl.pallas_call(
        functools.partial(pack_kernel, owners),
        out_shape=[
            jax.ShapeDtypeStruct((owners * MESSAGE, LANES), jnp.float32),
            jax.ShapeDtypeStruct((3, rows, columns // owners), jnp.float32),
            jax.ShapeDtypeStruct((NR, NR), jnp.float32),
            jax.ShapeDtypeStruct((mine, TILE, LANES), jnp.float32),
            jax.ShapeDtypeStruct((2 * LANES, LANES), jnp.bfloat16),
            jax.ShapeDtypeStruct((2 * LANES, 2 * LANES), jnp.bfloat16),
        ],
        in_specs=[HBM] * 5,
        out_specs=[VMEM] * 6,
        scratch_shapes=[
            pltpu.SMEM((1, listed), jnp.int32),
            pltpu.VMEM((RB * listed, LANES), jnp.float32),
            pltpu.SMEM((mine,), jnp.int32),
            pltpu.SemaphoreType.DMA((7,)),
        ],
        compiler_params=SMALL,
    )(
        in_hbm(block_ids),
        in_hbm(partial_kernels.reshape(RB * listed, BY)),
        in_hbm(lateral_scale),
        in_hbm(radial_smoother),
        in_hbm(shell_level),
    )
    arrived = lax.all_to_all(
        packed.reshape(owners, MESSAGE, LANES),
        "ev",
        split_axis=0,
        concat_axis=0,
        tiled=True,
        axis_index_groups=[[(place - owners // 4) % owners for place in range(owners)]],
    )
    pieces, side_scale = pl.pallas_call(
        functools.partial(smooth_kernel, owners),
        out_shape=[
            jax.ShapeDtypeStruct((holders * PIECE, LANES), jnp.float32),
            jax.ShapeDtypeStruct((part, LANES), jnp.float32),
        ],
        in_specs=[VMEM] * 3,
        out_specs=[VMEM] * 2,
        scratch_shapes=[
            pltpu.VMEM((NR, (BPT + 1) * LANES), jnp.float32),
            pltpu.VMEM((NR // 2, LANES), jnp.float32),
        ],
        compiler_params=PACKED,
    )(arrived, scale, smoother)
    shells = lax.all_to_all(
        pieces.reshape(holders, 1, PIECE * LANES),
        "sp",
        split_axis=0,
        concat_axis=0,
        tiled=True,
        axis_index_groups=[[place_of(place, holders) for place in range(holders)]],
    ).reshape(holders * PIECE, LANES)
    padded = pltpu.VMEM((mine, rows + 2 * TILE, LANES), jnp.float32)
    plain = pltpu.VMEM((mine, rows, LANES), jnp.float32)
    side = pltpu.VMEM((part + 2 * TILE, LANES), jnp.float32)
    return pl.pallas_call(
        diffuse_kernel,
        out_shape=jax.ShapeDtypeStruct((mine, rows, columns // owners), jnp.float32),
        in_specs=[VMEM] * 6,
        out_specs=HBM,
        scratch_shapes=[
            padded,
            padded,
            side,
            side,
            plain,
            pltpu.VMEM((part, LANES), jnp.float32),
            plain,
            pltpu.SemaphoreType.DMA((1,)),
        ],
        compiler_params=SMALL,
    )(shells, factor, scale, side_scale, near, side_near)


def solution(mesh):
    placed = (P("ev", None, "sp", None), P("ev", "sp"), P(), P("sp"), P())
    return jax.shard_map(
        per_device, mesh=mesh, in_specs=placed, out_specs=P("sp", None, "ev"), check_vma=False
    )
```

```python
import functools

import jax
import jax.numpy as jnp
from jax import lax
from jax.experimental import pallas as pl
from jax.experimental.pallas import tpu as pltpu
from jax.sharding import PartitionSpec as P

NR = 128
RB = 32
BY = 128
BPT = 8
CAP = 2
PASSES = 4
NSEG = 4
PER_OWNER = BPT * NSEG
LANES = 128
TILE = 8
MESSAGE = CAP * RB + TILE
LABELS = 64
STRIP = 16
SIDES = 4
PIECE = 2 * BPT + 1
PLANE = 4

diffusion_rate = 0.0615

SMALL = pltpu.CompilerParams(vmem_limit_bytes=12 * 1024 * 1024)
PACKED = pltpu.CompilerParams(
    vmem_limit_bytes=12 * 1024 * 1024
)
VMEM = pl.BlockSpec(memory_space=pltpu.VMEM)
HBM = pl.BlockSpec(memory_space=pltpu.HBM)


def exchange_order(holders):
    planes = holders // PLANE
    order = sorted(range(planes), key=lambda z: -min(z, planes - z))
    return [z * PLANE + i for z in order for i in range(PLANE)]


def lane_index(shape=(TILE, LANES)):
    return lax.broadcasted_iota(jnp.int32, shape, len(shape) - 1)


def stencil_matrices(near_ref, side_near_ref):
    row_of = lax.broadcasted_iota(jnp.int32, (LANES, LANES), 0)
    lane_of = lax.broadcasted_iota(jnp.int32, (LANES, LANES), 1)
    beside = jnp.abs(row_of - lane_of) == 1
    middle = jnp.where(row_of == lane_of, -4.0, 0.0)
    near = jnp.where(beside, 1.0, middle).astype(jnp.bfloat16)
    from_in, to_in = lax.bitwise_and(row_of, STRIP - 1), lax.bitwise_and(lane_of, STRIP - 1)
    same_strip = lax.shift_right_logical(row_of, 4) == lax.shift_right_logical(lane_of, 4)
    same_run = lax.shift_right_logical(row_of, 2) == lax.shift_right_logical(lane_of, 2)
    apart, later = jnp.abs(from_in - to_in), jnp.maximum(from_in, to_in)
    joined = ((apart == 7) & (later == 11)) | ((apart == 9) & (later == 12))
    side_near = jnp.where((beside & same_run) | (joined & same_strip), 1.0, middle).astype(jnp.bfloat16)
    exchanged = jnp.where(to_in == 11, lane_of + 1, jnp.where(to_in == 12, lane_of - 1, lane_of))
    exchange = jnp.where(row_of == exchanged, 1.0, 0.0).astype(jnp.bfloat16)
    for part in range(2):
        at = slice(part * LANES, (part + 1) * LANES)
        near_ref[at, :] = near
        side_near_ref[at, 0:LANES] = side_near
        side_near_ref[at, LANES:] = exchange


def pack_kernel(
    owners, ids_hbm, blocks_hbm, scale_hbm, smoother_hbm, level_hbm,
    out_ref, scale_ref, smoother_ref, factor_ref, near_ref, side_near_ref,
    ids_ref, blocks_ref, level_ref, sems,
):
    ids_copy = pltpu.make_async_copy(ids_hbm, ids_ref, sems.at[0])
    blocks_copy = pltpu.make_async_copy(blocks_hbm, blocks_ref, sems.at[1])
    ids_copy.start()
    blocks_copy.start()
    here = lax.axis_index("ev")
    width = scale_ref.shape[2]
    places = (jnp.maximum(here - 1, 0), here, jnp.minimum(here + 1, owners - 1))
    copies = [
        pltpu.make_async_copy(
            scale_hbm.at[:, pl.ds(pl.multiple_of(place * width, width), width)],
            scale_ref.at[n],
            sems.at[2 + n],
        )
        for n, place in enumerate(places)
    ]
    copies.append(pltpu.make_async_copy(smoother_hbm, smoother_ref, sems.at[5]))
    copies.append(pltpu.make_async_copy(level_hbm, level_ref, sems.at[6]))
    for copy in copies:
        copy.start()
    listed = ids_ref.shape[1]
    lane = lane_index()
    zero = jnp.zeros((TILE, LANES), jnp.float32)
    for row in range(0, owners * MESSAGE, TILE):
        out_ref[row : row + TILE, :] = zero
    stencil_matrices(near_ref, side_near_ref)
    ids_copy.wait()
    ids = [ids_ref[0, j] for j in range(listed)]
    owner_of = [lax.shift_right_logical(i, 5) for i in ids]
    ranks = []
    for j in range(listed):
        rank = jnp.int32(0)
        for i in range(j):
            rank = rank + jnp.where(owner_of[i] == owner_of[j], 1, 0)
        ranks.append(rank)
    group = lax.shift_right_logical(lane, 4)
    in_four = lax.bitwise_and(lax.shift_right_logical(lane, 2), 3)
    blocks_copy.wait()

    def message(owner):
        return lax.rem(owner + owners // 4, owners) * MESSAGE

    def add(owner, cells):
        there = pl.ds(pl.multiple_of(message(owner) + CAP * RB, TILE), TILE)
        out_ref[there, :] = out_ref[there, :] + cells

    for j in range(listed):
        owner, rank = owner_of[j], ranks[j]
        within = lax.bitwise_and(ids[j], PER_OWNER - 1).astype(jnp.float32)
        both = zero
        for a in range(RB // TILE):
            cells = blocks_ref[pl.ds(a * TILE * listed + j, TILE, stride=listed), :]
            start = pl.multiple_of(message(owner) + rank * RB + a * TILE, TILE)
            out_ref[pl.ds(start, TILE), :] = cells
            both = jnp.where(group == a, pltpu.roll(cells, 16 * a + 4, 1), both)
        add(owner, jnp.where(lane == LABELS + rank, within, 0.0))
        left = jnp.where(in_four == 1, both, 0.0)
        to_left = pltpu.roll(left, 4 + 4 * rank, 1)
        to_left = to_left + jnp.where(lane == LABELS + 4 + rank, within, 0.0)
        right = jnp.where(in_four == 0, both, 0.0)
        to_right = pltpu.roll(right, 4 * rank, 1)
        to_right = to_right + jnp.where(lane == LABELS + 2 + rank, within, 0.0)
        add(jnp.maximum(owner - 1, 0), jnp.where(owner > 0, to_left, 0.0))
        add(jnp.minimum(owner + 1, owners - 1), jnp.where(owner < owners - 1, to_right, 0.0))
    for copy in copies:
        copy.wait()
    for shell in range(level_ref.shape[0]):
        factor = diffusion_rate * level_ref[shell].astype(jnp.float32)
        factor_ref[shell] = jnp.full((TILE, LANES), factor, jnp.float32)


def halves(cells):
    high = cells.astype(jnp.bfloat16)
    low = (cells - high.astype(jnp.float32)).astype(jnp.bfloat16)
    return high, low


def scale_strips(scale_ref, owners):
    here = lax.axis_index("ev")
    part = scale_ref.shape[1] // SIDES
    lane = lane_index((part, LANES))
    inner = lax.bitwise_and(lane, STRIP - 1) < 8
    strip = lax.shift_right_logical(lane, 4)
    keep_after = (lane < 4) & (here < owners - 1)
    keep_before = (lane >= LANES - 4) & (here > 0)
    strips = jnp.zeros((part, LANES), jnp.float32)
    for n in range(SIDES):
        at = slice(n * part, (n + 1) * part)
        beyond = jnp.where(keep_before, scale_ref[0, at, :], 0.0)
        beyond = jnp.where(keep_after, scale_ref[2, at, :], beyond)
        both = jnp.where(
            inner,
            pltpu.roll(scale_ref[1, at, :], STRIP * n + 4, 1),
            pltpu.roll(beyond, STRIP * n + 12, 1),
        )
        strips = jnp.where(strip == n, both, strips)
    return strips + pltpu.roll(strips, LANES // 2, 1)


def smooth_kernel(
    groups, arrived_ref, scale_ref, smoother_ref, out_ref, side_scale_ref,
    columns_ref, edge_ref, placed_ref,
):
    labels = arrived_ref[:, CAP * RB, :].astype(jnp.int32)
    spots = [
        [labels[g : g + 1, LABELS + i : LABELS + i + 1][0, 0] for i in range(3 * CAP)]
        for g in range(groups)
    ]
    rows = [[lax.shift_right_logical(spot, 2) for spot in group] for group in spots]
    segments = [[lax.bitwise_and(spot, NSEG - 1) for spot in group] for group in spots]
    lane = lane_index()
    low = lane < LANES // 2
    lane_four = lax.bitwise_and(lane, LANES // 2 - 4)
    columns_ref[:, : BPT * LANES] = jnp.zeros((NR, BPT * LANES), jnp.float32)
    edge_ref[...] = jnp.zeros_like(edge_ref)
    side_scale_ref[...] = scale_strips(scale_ref, groups)
    for g in range(groups):
        for rank in range(CAP):
            where = (
                pl.ds(pl.multiple_of(segments[g][rank] * RB, RB), RB),
                pl.ds(pl.multiple_of(rows[g][rank] * LANES, LANES), LANES),
            )
            columns_ref[where] = columns_ref[where] + arrived_ref[g, rank * RB : (rank + 1) * RB, :]
    for g in range(groups):
        edges = arrived_ref[g, CAP * RB :, :]
        pairs = [
            jnp.where(low, edges, pltpu.roll(edges, 48, 1)),
            jnp.where(low, pltpu.roll(edges, LANES - 32, 1), pltpu.roll(edges, 16, 1)),
        ]
        for h in range(2 * CAP):
            target = (BPT - 1 - rows[g][CAP + h]) * 8 + (4 if h >= CAP else 0)
            keep = lane_four == target
            shift = lax.bitwise_and(target + (LANES - 4 * h), LANES - 1)
            four = jnp.concatenate(
                [jnp.where(keep, pltpu.roll(pair, shift, 1), 0.0) for pair in pairs], axis=0
            )
            where = pl.ds(pl.multiple_of(segments[g][CAP + h] * (2 * TILE), 2 * TILE), 2 * TILE)
            edge_ref[where, :] = edge_ref[where, :] + four
    for pair in range(NR // (2 * TILE)):
        cells = edge_ref[pair * TILE : (pair + 1) * TILE, :]
        turned = pltpu.roll(cells, LANES // 2, 1)
        at = pair * 2 * TILE
        columns_ref[at : at + TILE, BPT * LANES :] = jnp.where(low, cells, turned)
        columns_ref[at + TILE : at + 2 * TILE, BPT * LANES :] = jnp.where(low, turned, cells)
    half = NR // 2
    for place, holder in enumerate(exchange_order(half)[::PLANE]):
        at, start = place * 2 * PLANE, holder * 2
        placed_ref[at : at + 2 * PLANE, :] = smoother_ref[start : start + 2 * PLANE, :]
    smoother = jnp.concatenate(
        [placed_ref[pl.ds(0, half, stride=2), :], placed_ref[pl.ds(1, half, stride=2), :]], axis=0
    )
    high, rest = halves(smoother)
    twice = jnp.concatenate([high, high], axis=1)

    def smoothed(start, width):
        first, second = halves(columns_ref[:, start : start + width])
        both = jnp.concatenate([first, second], axis=0)
        return jnp.dot(twice, both, preferred_element_type=jnp.float32) + jnp.dot(
            rest, first, preferred_element_type=jnp.float32
        )

    for row in range(0, BPT, 2):
        done = smoothed(row * LANES, 2 * LANES)
        for i in range(2):
            cells = done[:, i * LANES : (i + 1) * LANES]
            out_ref[pl.ds(row + i, half, stride=PIECE), :] = cells[:half]
            out_ref[pl.ds(BPT + row + i, half, stride=PIECE), :] = cells[half:]
    done = smoothed(BPT * LANES, LANES)
    lower = lane_index((half, LANES)) < LANES // 2
    out_ref[pl.ds(2 * BPT, half, stride=PIECE), :] = jnp.where(lower, done[:half], done[half:])


def diffuse_kernel(
    cells_ref, factor_ref, scale_ref, side_scale_ref, near_ref, side_near_ref, out_hbm,
    main_a, main_b, side_a, side_b, coefficient_ref, edge_ref, out_ref, sems,
):
    shells, rows, _ = out_ref.shape
    nothing = jnp.zeros((TILE, LANES), jnp.float32)
    stripes = rows // BPT
    tiles = stripes // SIDES
    part = tiles * TILE
    for buffer in (main_a, main_b):
        for shell in range(shells):
            buffer[shell, 0:TILE, :] = nothing
            buffer[shell, TILE + rows : 2 * TILE + rows, :] = nothing
    slots = [(n, shell, (1 - shell) * SIDES + n) for n in range(SIDES) for shell in range(shells)]

    strip = lax.shift_right_logical(lane_index(), 4)
    for v in range(tiles):
        outer = nothing
        for n in range(SIDES):
            stripe = n * tiles + v
            at = exchange_order(stripes).index(stripe) * PIECE
            spot = TILE + stripe * BPT
            wide = jnp.broadcast_to(cells_ref[at + 2 * BPT : at + PIECE, :], (TILE, LANES))
            turned = pltpu.roll(wide, STRIP * (n + 1), 1, stride=8, stride_axis=0)
            outer = jnp.where(lax.bitwise_and(strip, SIDES - 1) == n, turned, outer)
            for shell in range(shells):
                main_a[shell, spot : spot + BPT, :] = cells_ref[
                    at + shell * BPT : at + (shell + 1) * BPT, :
                ]
        side_a[TILE + v * TILE : 2 * TILE + v * TILE, :] = outer
    lane = lane_index((part, LANES))
    strip = lax.shift_right_logical(lane, 4)
    inner = lax.bitwise_and(lane, STRIP - 1) < 8

    lane_row = lane_index((1, LANES))
    stripe_in = lax.bitwise_and(lane_row, SIDES * STRIP - 1)
    last_row = TILE + part - 1

    def join(side):
        down = pltpu.roll(side[last_row : last_row + 1, :], STRIP, 1)
        side[TILE - 1 : TILE, :] = jnp.where(stripe_in < STRIP, 0.0, down)
        up = pltpu.roll(side[TILE : TILE + 1, :], LANES - STRIP, 1)
        side[last_row + 1 : last_row + 2, :] = jnp.where(stripe_in >= (SIDES - 1) * STRIP, 0.0, up)

    lane_tile = lane_index()
    factors = [jnp.tile(factor_ref[shell], (tiles, 1)) for shell in range(shells)]
    side_factor = jnp.tile(
        jnp.where(lane_tile < LANES // 2, factor_ref[1], factor_ref[0]), (tiles, 1)
    )
    is_edge = (lane == 0) | (lane == LANES - 1)

    def across(cells, matrix):
        return jnp.dot(
            jnp.concatenate(halves(cells), axis=1), matrix, preferred_element_type=jnp.float32
        )

    def side_step(side, side_next, sums):
        middle = side[TILE : TILE + part, :]
        vertical = side[TILE - 1 : TILE + part - 1, :] + side[TILE + 1 : TILE + part + 1, :]
        coefficient = side_factor * side_scale_ref[...]
        side_next[TILE : TILE + part, :] = middle + coefficient * (vertical + sums)
        join(side_next)

    buffers = ((main_a, side_a), (main_b, side_b))
    for repeat in range(PASSES):
        (main, side), (main_next, side_next) = buffers[repeat % 2], buffers[(repeat + 1) % 2]
        final = repeat == PASSES - 1
        if repeat == 0 or final:
            edge_ref[...] = across(side[TILE : TILE + part, :], side_near_ref[:, LANES:])
        else:
            sums = across(side[TILE : TILE + part, :], side_near_ref[...])
            edge_ref[...] = sums[:, LANES:]
            side_step(side, side_next, sums[:, :LANES])
        for n, shell, slot in slots:
            at = slice(n * part, (n + 1) * part)
            first = TILE + n * part
            middle = main[shell, first : first + part, :]
            sums = across(middle, near_ref[...])
            turned = pltpu.roll(edge_ref[...], (2 * LANES - STRIP * slot - 12) % LANES, 1)
            vertical = (
                main[shell, first - 1 : first + part - 1, :]
                + main[shell, first + 1 : first + part + 1, :]
            )
            if repeat == 0:
                coefficient = factors[shell] * scale_ref[1, at, :]
                coefficient_ref[shell, at, :] = coefficient
                side[TILE : TILE + part, :] = jnp.where(
                    inner & (strip == slot),
                    pltpu.roll(middle, STRIP * slot + 4, 1),
                    side[TILE : TILE + part, :],
                )
            else:
                coefficient = coefficient_ref[shell, at, :]
            new = middle + coefficient * ((vertical + sums) + jnp.where(is_edge, turned, 0.0))
            if final:
                out_ref[shell, at, :] = new
            else:
                main_next[shell, first : first + part, :] = new
        if repeat == 0:
            join(side)
            side_step(
                side, side_next, across(side[TILE : TILE + part, :], side_near_ref[:, :LANES])
            )
    out_copy = pltpu.make_async_copy(out_ref, out_hbm, sems.at[0])
    out_copy.start()
    out_copy.wait()


def in_hbm(array):
    return pltpu.with_memory_space_constraint(array, pltpu.HBM)


def per_device(partial_kernels, block_ids, radial_smoother, shell_level, lateral_scale):
    owners = lax.axis_size("ev")
    holders = lax.axis_size("sp")
    listed = block_ids.shape[1]
    rows, columns = lateral_scale.shape
    mine = shell_level.shape[0]
    part = rows // SIDES
    packed, scale, smoother, factor, near, side_near = pl.pallas_call(
        functools.partial(pack_kernel, owners),
        out_shape=[
            jax.ShapeDtypeStruct((owners * MESSAGE, LANES), jnp.float32),
            jax.ShapeDtypeStruct((3, rows, columns // owners), jnp.float32),
            jax.ShapeDtypeStruct((NR, NR), jnp.float32),
            jax.ShapeDtypeStruct((mine, TILE, LANES), jnp.float32),
            jax.ShapeDtypeStruct((2 * LANES, LANES), jnp.bfloat16),
            jax.ShapeDtypeStruct((2 * LANES, 2 * LANES), jnp.bfloat16),
        ],
        in_specs=[HBM] * 5,
        out_specs=[VMEM] * 6,
        scratch_shapes=[
            pltpu.SMEM((1, listed), jnp.int32),
            pltpu.VMEM((RB * listed, LANES), jnp.float32),
            pltpu.SMEM((mine,), jnp.int32),
            pltpu.SemaphoreType.DMA((7,)),
        ],
        compiler_params=SMALL,
    )(
        in_hbm(block_ids),
        in_hbm(partial_kernels.reshape(RB * listed, BY)),
        in_hbm(lateral_scale),
        in_hbm(radial_smoother),
        in_hbm(shell_level),
    )
    arrived = lax.all_to_all(
        packed.reshape(owners, MESSAGE, LANES),
        "ev",
        split_axis=0,
        concat_axis=0,
        tiled=True,
        axis_index_groups=[[(place - owners // 4) % owners for place in range(owners)]],
    )
    pieces, side_scale = pl.pallas_call(
        functools.partial(smooth_kernel, owners),
        out_shape=[
            jax.ShapeDtypeStruct((holders * PIECE, LANES), jnp.float32),
            jax.ShapeDtypeStruct((part, LANES), jnp.float32),
        ],
        in_specs=[VMEM] * 3,
        out_specs=[VMEM] * 2,
        scratch_shapes=[
            pltpu.VMEM((NR, (BPT + 1) * LANES), jnp.float32),
            pltpu.VMEM((NR // 2, LANES), jnp.float32),
            pltpu.VMEM((NR, NR), jnp.float32),
        ],
        compiler_params=PACKED,
    )(arrived, scale, smoother)
    shells = lax.all_to_all(
        pieces.reshape(holders, 1, PIECE * LANES),
        "sp",
        split_axis=0,
        concat_axis=0,
        tiled=True,
        axis_index_groups=[exchange_order(holders)],
    ).reshape(holders * PIECE, LANES)
    padded = pltpu.VMEM((mine, rows + 2 * TILE, LANES), jnp.float32)
    plain = pltpu.VMEM((mine, rows, LANES), jnp.float32)
    side = pltpu.VMEM((part + 2 * TILE, LANES), jnp.float32)
    return pl.pallas_call(
        diffuse_kernel,
        out_shape=jax.ShapeDtypeStruct((mine, rows, columns // owners), jnp.float32),
        in_specs=[VMEM] * 6,
        out_specs=HBM,
        scratch_shapes=[
            padded,
            padded,
            side,
            side,
            plain,
            pltpu.VMEM((part, LANES), jnp.float32),
            plain,
            pltpu.SemaphoreType.DMA((1,)),
        ],
        compiler_params=SMALL,
    )(shells, factor, scale, side_scale, near, side_near)


def solution(mesh):
    placed = (P("ev", None, "sp", None), P("ev", "sp"), P(), P("sp"), P())
    return jax.shard_map(
        per_device, mesh=mesh, in_specs=placed, out_specs=P("sp", None, "ev"), check_vma=False
    )
```

```python
import functools

import jax
import jax.numpy as jnp
from jax import lax
from jax.experimental import pallas as pl
from jax.experimental.pallas import tpu as pltpu
from jax.sharding import PartitionSpec as P

NR = 128
RB = 32
BY = 128
BPT = 8
CAP = 2
PASSES = 4
NSEG = 4
PER_OWNER = BPT * NSEG
LANES = 128
TILE = 8
MESSAGE = CAP * RB + TILE
LABELS = 64
STRIP = 16
SIDES = 4
PIECE = 2 * BPT + 1

diffusion_rate = 0.0615

SMALL = pltpu.CompilerParams(vmem_limit_bytes=12 * 1024 * 1024)
PACKED = pltpu.CompilerParams(
    vmem_limit_bytes=12 * 1024 * 1024
)
VMEM = pl.BlockSpec(memory_space=pltpu.VMEM)
HBM = pl.BlockSpec(memory_space=pltpu.HBM)


def place_of(holder, holders):
    return (holder + holders // 2) % holders


def lane_index(shape=(TILE, LANES)):
    return lax.broadcasted_iota(jnp.int32, shape, len(shape) - 1)


def stencil_matrices(near_ref, side_near_ref):
    row_of = lax.broadcasted_iota(jnp.int32, (LANES, LANES), 0)
    lane_of = lax.broadcasted_iota(jnp.int32, (LANES, LANES), 1)
    beside = jnp.abs(row_of - lane_of) == 1
    middle = jnp.where(row_of == lane_of, -4.0, 0.0)
    near = jnp.where(beside, 1.0, middle).astype(jnp.bfloat16)
    from_in, to_in = lax.bitwise_and(row_of, STRIP - 1), lax.bitwise_and(lane_of, STRIP - 1)
    same_strip = lax.shift_right_logical(row_of, 4) == lax.shift_right_logical(lane_of, 4)
    same_run = lax.shift_right_logical(row_of, 2) == lax.shift_right_logical(lane_of, 2)
    apart, later = jnp.abs(from_in - to_in), jnp.maximum(from_in, to_in)
    joined = ((apart == 7) & (later == 11)) | ((apart == 9) & (later == 12))
    side_near = jnp.where((beside & same_run) | (joined & same_strip), 1.0, middle).astype(jnp.bfloat16)
    exchanged = jnp.where(to_in == 11, lane_of + 1, jnp.where(to_in == 12, lane_of - 1, lane_of))
    exchange = jnp.where(row_of == exchanged, 1.0, 0.0).astype(jnp.bfloat16)
    for part in range(2):
        at = slice(part * LANES, (part + 1) * LANES)
        near_ref[at, :] = near
        side_near_ref[at, 0:LANES] = side_near
        side_near_ref[at, LANES:] = exchange


def pack_kernel(
    owners, ids_hbm, blocks_hbm, scale_hbm, smoother_hbm, level_hbm,
    out_ref, scale_ref, smoother_ref, factor_ref, near_ref, side_near_ref,
    ids_ref, blocks_ref, level_ref, sems,
):
    ids_copy = pltpu.make_async_copy(ids_hbm, ids_ref, sems.at[0])
    blocks_copy = pltpu.make_async_copy(blocks_hbm, blocks_ref, sems.at[1])
    ids_copy.start()
    blocks_copy.start()
    here = lax.axis_index("ev")
    width = scale_ref.shape[2]
    places = (jnp.maximum(here - 1, 0), here, jnp.minimum(here + 1, owners - 1))
    copies = [
        pltpu.make_async_copy(
            scale_hbm.at[:, pl.ds(pl.multiple_of(place * width, width), width)],
            scale_ref.at[n],
            sems.at[2 + n],
        )
        for n, place in enumerate(places)
    ]
    copies.append(pltpu.make_async_copy(smoother_hbm, smoother_ref, sems.at[5]))
    copies.append(pltpu.make_async_copy(level_hbm, level_ref, sems.at[6]))
    for copy in copies:
        copy.start()
    listed = ids_ref.shape[1]
    lane = lane_index()
    zero = jnp.zeros((TILE, LANES), jnp.float32)
    for row in range(0, owners * MESSAGE, TILE):
        out_ref[row : row + TILE, :] = zero
    stencil_matrices(near_ref, side_near_ref)
    ids_copy.wait()
    ids = [ids_ref[0, j] for j in range(listed)]
    owner_of = [lax.shift_right_logical(i, 5) for i in ids]
    ranks = []
    for j in range(listed):
        rank = jnp.int32(0)
        for i in range(j):
            rank = rank + jnp.where(owner_of[i] == owner_of[j], 1, 0)
        ranks.append(rank)
    group = lax.shift_right_logical(lane, 4)
    in_four = lax.bitwise_and(lax.shift_right_logical(lane, 2), 3)
    blocks_copy.wait()

    def message(owner):
        return lax.rem(2 * owners - owners // 4 - owner, owners) * MESSAGE

    def add(owner, cells):
        there = pl.ds(pl.multiple_of(message(owner) + CAP * RB, TILE), TILE)
        out_ref[there, :] = out_ref[there, :] + cells

    for j in range(listed):
        owner, rank = owner_of[j], ranks[j]
        within = lax.bitwise_and(ids[j], PER_OWNER - 1).astype(jnp.float32)
        both = zero
        for a in range(RB // TILE):
            cells = blocks_ref[pl.ds(a * TILE * listed + j, TILE, stride=listed), :]
            start = pl.multiple_of(message(owner) + rank * RB + a * TILE, TILE)
            out_ref[pl.ds(start, TILE), :] = cells
            both = jnp.where(group == a, pltpu.roll(cells, 16 * a + 4, 1), both)
        add(owner, jnp.where(lane == LABELS + rank, within, 0.0))
        left = jnp.where(in_four == 1, both, 0.0)
        to_left = pltpu.roll(left, 4 + 4 * rank, 1)
        to_left = to_left + jnp.where(lane == LABELS + 4 + rank, within, 0.0)
        right = jnp.where(in_four == 0, both, 0.0)
        to_right = pltpu.roll(right, 4 * rank, 1)
        to_right = to_right + jnp.where(lane == LABELS + 2 + rank, within, 0.0)
        add(jnp.maximum(owner - 1, 0), jnp.where(owner > 0, to_left, 0.0))
        add(jnp.minimum(owner + 1, owners - 1), jnp.where(owner < owners - 1, to_right, 0.0))
    for copy in copies:
        copy.wait()
    for shell in range(level_ref.shape[0]):
        factor = diffusion_rate * level_ref[shell].astype(jnp.float32)
        factor_ref[shell] = jnp.full((TILE, LANES), factor, jnp.float32)


def halves(cells):
    high = cells.astype(jnp.bfloat16)
    low = (cells - high.astype(jnp.float32)).astype(jnp.bfloat16)
    return high, low


def scale_strips(scale_ref, owners):
    here = lax.axis_index("ev")
    part = scale_ref.shape[1] // SIDES
    lane = lane_index((part, LANES))
    inner = lax.bitwise_and(lane, STRIP - 1) < 8
    strip = lax.shift_right_logical(lane, 4)
    keep_after = (lane < 4) & (here < owners - 1)
    keep_before = (lane >= LANES - 4) & (here > 0)
    strips = jnp.zeros((part, LANES), jnp.float32)
    for n in range(SIDES):
        at = slice(n * part, (n + 1) * part)
        beyond = jnp.where(keep_before, scale_ref[0, at, :], 0.0)
        beyond = jnp.where(keep_after, scale_ref[2, at, :], beyond)
        both = jnp.where(
            inner,
            pltpu.roll(scale_ref[1, at, :], STRIP * n + 4, 1),
            pltpu.roll(beyond, STRIP * n + 12, 1),
        )
        strips = jnp.where(strip == n, both, strips)
    return strips + pltpu.roll(strips, LANES // 2, 1)


def smooth_kernel(
    groups, arrived_ref, scale_ref, smoother_ref, out_ref, side_scale_ref,
    columns_ref, edge_ref,
):
    labels = arrived_ref[:, CAP * RB, :].astype(jnp.int32)
    spots = [
        [labels[g : g + 1, LABELS + i : LABELS + i + 1][0, 0] for i in range(3 * CAP)]
        for g in range(groups)
    ]
    rows = [[lax.shift_right_logical(spot, 2) for spot in group] for group in spots]
    segments = [[lax.bitwise_and(spot, NSEG - 1) for spot in group] for group in spots]
    lane = lane_index()
    low = lane < LANES // 2
    lane_four = lax.bitwise_and(lane, LANES // 2 - 4)
    columns_ref[:, : BPT * LANES] = jnp.zeros((NR, BPT * LANES), jnp.float32)
    edge_ref[...] = jnp.zeros_like(edge_ref)
    side_scale_ref[...] = scale_strips(scale_ref, groups)
    for g in range(groups):
        for rank in range(CAP):
            where = (
                pl.ds(pl.multiple_of(segments[g][rank] * RB, RB), RB),
                pl.ds(pl.multiple_of(rows[g][rank] * LANES, LANES), LANES),
            )
            columns_ref[where] = columns_ref[where] + arrived_ref[g, rank * RB : (rank + 1) * RB, :]
    for g in range(groups):
        edges = arrived_ref[g, CAP * RB :, :]
        pairs = [
            jnp.where(low, edges, pltpu.roll(edges, 48, 1)),
            jnp.where(low, pltpu.roll(edges, LANES - 32, 1), pltpu.roll(edges, 16, 1)),
        ]
        for h in range(2 * CAP):
            target = (BPT - 1 - rows[g][CAP + h]) * 8 + (4 if h >= CAP else 0)
            keep = lane_four == target
            shift = lax.bitwise_and(target + (LANES - 4 * h), LANES - 1)
            four = jnp.concatenate(
                [jnp.where(keep, pltpu.roll(pair, shift, 1), 0.0) for pair in pairs], axis=0
            )
            where = pl.ds(pl.multiple_of(segments[g][CAP + h] * (2 * TILE), 2 * TILE), 2 * TILE)
            edge_ref[where, :] = edge_ref[where, :] + four
    for pair in range(NR // (2 * TILE)):
        cells = edge_ref[pair * TILE : (pair + 1) * TILE, :]
        turned = pltpu.roll(cells, LANES // 2, 1)
        at = pair * 2 * TILE
        columns_ref[at : at + TILE, BPT * LANES :] = jnp.where(low, cells, turned)
        columns_ref[at + TILE : at + 2 * TILE, BPT * LANES :] = jnp.where(low, turned, cells)
    half = NR // 2
    quarter = half // 2
    starts = [half + 0, 0, half + 1, 1]
    smoother = jnp.concatenate(
        [smoother_ref[pl.ds(start, quarter, stride=2), :] for start in starts], axis=0
    )
    high, rest = halves(smoother)
    twice = jnp.concatenate([high, high], axis=1)

    def smoothed(start, width):
        first, second = halves(columns_ref[:, start : start + width])
        both = jnp.concatenate([first, second], axis=0)
        return jnp.dot(twice, both, preferred_element_type=jnp.float32) + jnp.dot(
            rest, first, preferred_element_type=jnp.float32
        )

    for row in range(0, BPT, 2):
        done = smoothed(row * LANES, 2 * LANES)
        for i in range(2):
            cells = done[:, i * LANES : (i + 1) * LANES]
            out_ref[pl.ds(row + i, half, stride=PIECE), :] = cells[:half]
            out_ref[pl.ds(BPT + row + i, half, stride=PIECE), :] = cells[half:]
    done = smoothed(BPT * LANES, LANES)
    lower = lane_index((half, LANES)) < LANES // 2
    out_ref[pl.ds(2 * BPT, half, stride=PIECE), :] = jnp.where(lower, done[:half], done[half:])


def diffuse_kernel(
    cells_ref, factor_ref, scale_ref, side_scale_ref, near_ref, side_near_ref, out_hbm,
    main_a, main_b, side_a, side_b, coefficient_ref, edge_ref, out_ref, sems,
):
    shells, rows, _ = out_ref.shape
    nothing = jnp.zeros((TILE, LANES), jnp.float32)
    stripes = rows // BPT
    tiles = stripes // SIDES
    part = tiles * TILE
    for buffer in (main_a, main_b):
        for shell in range(shells):
            buffer[shell, 0:TILE, :] = nothing
            buffer[shell, TILE + rows : 2 * TILE + rows, :] = nothing
    slots = [(n, shell, (1 - shell) * SIDES + n) for n in range(SIDES) for shell in range(shells)]

    strip = lax.shift_right_logical(lane_index(), 4)
    for v in range(tiles):
        outer = nothing
        for n in range(SIDES):
            stripe = n * tiles + v
            at = place_of(stripe, stripes) * PIECE
            spot = TILE + stripe * BPT
            wide = jnp.broadcast_to(cells_ref[at + 2 * BPT : at + PIECE, :], (TILE, LANES))
            turned = pltpu.roll(wide, STRIP * (n + 1), 1, stride=8, stride_axis=0)
            outer = jnp.where(lax.bitwise_and(strip, SIDES - 1) == n, turned, outer)
            for shell in range(shells):
                main_a[shell, spot : spot + BPT, :] = cells_ref[
                    at + shell * BPT : at + (shell + 1) * BPT, :
                ]
        side_a[TILE + v * TILE : 2 * TILE + v * TILE, :] = outer
    lane = lane_index((part, LANES))
    strip = lax.shift_right_logical(lane, 4)
    inner = lax.bitwise_and(lane, STRIP - 1) < 8

    lane_row = lane_index((1, LANES))
    stripe_in = lax.bitwise_and(lane_row, SIDES * STRIP - 1)
    last_row = TILE + part - 1

    def join(side):
        down = pltpu.roll(side[last_row : last_row + 1, :], STRIP, 1)
        side[TILE - 1 : TILE, :] = jnp.where(stripe_in < STRIP, 0.0, down)
        up = pltpu.roll(side[TILE : TILE + 1, :], LANES - STRIP, 1)
        side[last_row + 1 : last_row + 2, :] = jnp.where(stripe_in >= (SIDES - 1) * STRIP, 0.0, up)

    lane_tile = lane_index()
    factors = [jnp.tile(factor_ref[shell], (tiles, 1)) for shell in range(shells)]
    side_factor = jnp.tile(
        jnp.where(lane_tile < LANES // 2, factor_ref[1], factor_ref[0]), (tiles, 1)
    )
    is_edge = (lane == 0) | (lane == LANES - 1)

    def across(cells, matrix):
        return jnp.dot(
            jnp.concatenate(halves(cells), axis=1), matrix, preferred_element_type=jnp.float32
        )

    def side_step(side, side_next, sums):
        middle = side[TILE : TILE + part, :]
        vertical = side[TILE - 1 : TILE + part - 1, :] + side[TILE + 1 : TILE + part + 1, :]
        coefficient = side_factor * side_scale_ref[...]
        side_next[TILE : TILE + part, :] = middle + coefficient * (vertical + sums)
        join(side_next)

    buffers = ((main_a, side_a), (main_b, side_b))
    for repeat in range(PASSES):
        (main, side), (main_next, side_next) = buffers[repeat % 2], buffers[(repeat + 1) % 2]
        final = repeat == PASSES - 1
        if repeat == 0 or final:
            edge_ref[...] = across(side[TILE : TILE + part, :], side_near_ref[:, LANES:])
        else:
            sums = across(side[TILE : TILE + part, :], side_near_ref[...])
            edge_ref[...] = sums[:, LANES:]
            side_step(side, side_next, sums[:, :LANES])
        for n, shell, slot in slots:
            at = slice(n * part, (n + 1) * part)
            first = TILE + n * part
            middle = main[shell, first : first + part, :]
            sums = across(middle, near_ref[...])
            turned = pltpu.roll(edge_ref[...], (2 * LANES - STRIP * slot - 12) % LANES, 1)
            vertical = (
                main[shell, first - 1 : first + part - 1, :]
                + main[shell, first + 1 : first + part + 1, :]
            )
            if repeat == 0:
                coefficient = factors[shell] * scale_ref[1, at, :]
                coefficient_ref[shell, at, :] = coefficient
                side[TILE : TILE + part, :] = jnp.where(
                    inner & (strip == slot),
                    pltpu.roll(middle, STRIP * slot + 4, 1),
                    side[TILE : TILE + part, :],
                )
            else:
                coefficient = coefficient_ref[shell, at, :]
            new = middle + coefficient * ((vertical + sums) + jnp.where(is_edge, turned, 0.0))
            if final:
                out_ref[shell, at, :] = new
            else:
                main_next[shell, first : first + part, :] = new
        if repeat == 0:
            join(side)
            side_step(
                side, side_next, across(side[TILE : TILE + part, :], side_near_ref[:, :LANES])
            )
    out_copy = pltpu.make_async_copy(out_ref, out_hbm, sems.at[0])
    out_copy.start()
    out_copy.wait()


def in_hbm(array):
    return pltpu.with_memory_space_constraint(array, pltpu.HBM)


def per_device(partial_kernels, block_ids, radial_smoother, shell_level, lateral_scale):
    owners = lax.axis_size("ev")
    holders = lax.axis_size("sp")
    listed = block_ids.shape[1]
    rows, columns = lateral_scale.shape
    mine = shell_level.shape[0]
    part = rows // SIDES
    packed, scale, smoother, factor, near, side_near = pl.pallas_call(
        functools.partial(pack_kernel, owners),
        out_shape=[
            jax.ShapeDtypeStruct((owners * MESSAGE, LANES), jnp.float32),
            jax.ShapeDtypeStruct((3, rows, columns // owners), jnp.float32),
            jax.ShapeDtypeStruct((NR, NR), jnp.float32),
            jax.ShapeDtypeStruct((mine, TILE, LANES), jnp.float32),
            jax.ShapeDtypeStruct((2 * LANES, LANES), jnp.bfloat16),
            jax.ShapeDtypeStruct((2 * LANES, 2 * LANES), jnp.bfloat16),
        ],
        in_specs=[HBM] * 5,
        out_specs=[VMEM] * 6,
        scratch_shapes=[
            pltpu.SMEM((1, listed), jnp.int32),
            pltpu.VMEM((RB * listed, LANES), jnp.float32),
            pltpu.SMEM((mine,), jnp.int32),
            pltpu.SemaphoreType.DMA((7,)),
        ],
        compiler_params=SMALL,
    )(
        in_hbm(block_ids),
        in_hbm(partial_kernels.reshape(RB * listed, BY)),
        in_hbm(lateral_scale),
        in_hbm(radial_smoother),
        in_hbm(shell_level),
    )
    arrived = lax.all_to_all(
        packed.reshape(owners, MESSAGE, LANES),
        "ev",
        split_axis=0,
        concat_axis=0,
        tiled=True,
        axis_index_groups=[[(-owners // 4 - place) % owners for place in range(owners)]],
    )
    pieces, side_scale = pl.pallas_call(
        functools.partial(smooth_kernel, owners),
        out_shape=[
            jax.ShapeDtypeStruct((holders * PIECE, LANES), jnp.float32),
            jax.ShapeDtypeStruct((part, LANES), jnp.float32),
        ],
        in_specs=[VMEM] * 3,
        out_specs=[VMEM] * 2,
        scratch_shapes=[
            pltpu.VMEM((NR, (BPT + 1) * LANES), jnp.float32),
            pltpu.VMEM((NR // 2, LANES), jnp.float32),
        ],
        compiler_params=PACKED,
    )(arrived, scale, smoother)
    shells = lax.all_to_all(
        pieces.reshape(holders, 1, PIECE * LANES),
        "sp",
        split_axis=0,
        concat_axis=0,
        tiled=True,
        axis_index_groups=[[place_of(place, holders) for place in range(holders)]],
    ).reshape(holders * PIECE, LANES)
    padded = pltpu.VMEM((mine, rows + 2 * TILE, LANES), jnp.float32)
    plain = pltpu.VMEM((mine, rows, LANES), jnp.float32)
    side = pltpu.VMEM((part + 2 * TILE, LANES), jnp.float32)
    return pl.pallas_call(
        diffuse_kernel,
        out_shape=jax.ShapeDtypeStruct((mine, rows, columns // owners), jnp.float32),
        in_specs=[VMEM] * 6,
        out_specs=HBM,
        scratch_shapes=[
            padded,
            padded,
            side,
            side,
            plain,
            pltpu.VMEM((part, LANES), jnp.float32),
            plain,
            pltpu.SemaphoreType.DMA((1,)),
        ],
        compiler_params=SMALL,
    )(shells, factor, scale, side_scale, near, side_near)


def solution(mesh):
    placed = (P("ev", None, "sp", None), P("ev", "sp"), P(), P("sp"), P())
    return jax.shard_map(
        per_device, mesh=mesh, in_specs=placed, out_specs=P("sp", None, "ev"), check_vma=False
    )
```
